128 devices in a mesh: col: 32 (over x, z, core), leg: 4 (over y).
Axes of the slice: x: 4, y: 4, z: 4, core: 2. Of those that a mesh axis runs over, the one named last changes fastest.
Arguments:
- coeffs: float32 [2048, 4, 128, 128], P(('col', 'leg')), may hold values from -0.5 to 0.5
- block_ids: int32 [2048, 4], P(('col', 'leg')), may hold values from 0 to 127
- col_counts: int32 [2048], P(('col', 'leg')), may hold values from 1 to 128
- primal: float32 [2048, 128], P(('col', 'leg')), may hold values from 0.3 to 3
- slack: float32 [2048, 128], P(('col', 'leg')), may hold values from 0.3 to 3
- cost: float32 [2048, 128], P(('col', 'leg')), may hold values from -6 to 6
- duals: float32 [128, 128], P('leg'), may hold values from -6 to 6
- demand: float32 [128, 128], P('leg'), may hold values from -6 to 6
Outputs:
- step_dual: float32 [128, 128], P('leg')
- step_primal: float32 [2048, 128], P(('col', 'leg'))
The draws below stay inside these ranges and needn't reach their ends.
Inputs may be any that keep to these rules, and one draw needn't show every extreme that they name: `block_ids`: leg block of each tile; many tiles may share a block, the tiles of one column group too. `col_counts`: columns at or after this count in a column group are padding.
All inputs are finite; a program needn't handle non-finite values.
Results may differ from the reference program's by a relative error of at most 0.0003.
Values sent between devices are 32-bit elements; how exact they have to be, the bound alone decides.
No kernel may reach another device: no remote copies, remote signals or barrier semaphores. Data moves between devices by JAX's collectives and lax.ppermute only.
A program may use at most 128 MiB of HBM per device.

```python
import math
import jax
import jax.numpy as jnp
import numpy as np
from jax import lax

BS = 128
CW = 128
SPAN = 4
NG_DEV = 16
ITERS = 3
LB = 128
NG = 2048


def place_ends(drawn, rng, least, high):
    dims = drawn.shape
    place = [jax.random.randint(jax.random.fold_in(rng, axis), (), 0, dims[axis]) for axis in range(len(dims))]
    drawn = drawn.at[tuple(place)].set(least)
    longest = dims.index(max(dims))
    place[longest] = (place[longest] + 1) % dims[longest]
    return drawn.at[tuple(place)].set(high)


def level_of(rng, extent, cuts, least, high):
    gain, own = 1.0, jax.random.fold_in(rng, 6)
    for axis_at, blocks in cuts:
        draws = jnp.exp(jax.random.uniform(jax.random.fold_in(own, axis_at), (blocks,), jnp.float32, least / len(cuts), high / len(cuts)))
        gain = gain * jnp.repeat(draws, extent[axis_at] // blocks).reshape([-1 if axis == axis_at else 1 for axis in range(len(extent))])
    return gain


def rank_bounds(amount, skew):
    portions = [(1 << 20) // math.isqrt(rank ** skew) + 1 for rank in range(1, amount + 1)]
    spread = 1 + sum(portions) // (1 << 30)
    return np.cumsum(np.array([max(1, weight // spread) for weight in portions]))


def ranked_ids(own_key, shape, number_of, lean):
    grid = rank_bounds(number_of, lean)
    ticket = jax.random.randint(jax.random.fold_in(own_key, 1), shape, 0, int(grid[number_of - 1]))
    rank = jnp.searchsorted(jnp.asarray(grid, jnp.int32), ticket, side="right")
    return jax.random.permutation(jax.random.fold_in(own_key, 2), number_of)[rank].astype(jnp.int32)


def gaussian(stream_key, extent, spread, reach, cuts=(), kind=jnp.bfloat16):
    result = jax.random.normal(stream_key, extent, jnp.float32) * spread
    if len(cuts) > 0:
        result = level_of(stream_key, extent, cuts, -0.22, 0.18) * result
    return jnp.clip(result, min=-reach, max=reach).astype(kind)


def setup_inputs(seed: int = 0) -> dict:
    keys = jax.random.split(jax.random.key(seed), 9)
    return {
        "coeffs": gaussian(keys[0], (NG, SPAN, BS, CW), CW ** -0.5, 0.5, ((0, 128),), jnp.float32),
        "block_ids": place_ends(ranked_ids(keys[1], (NG, SPAN), LB, 2), jax.random.fold_in(keys[1], 3), 0, LB - 1).astype(jnp.int32),
        "col_counts": place_ends(jax.random.randint(keys[2], (NG,), 1, CW + 1), jax.random.fold_in(keys[2], 1), 1, CW).astype(jnp.int32),
        "primal": jnp.clip(jnp.exp(math.log(3.0) - 2.3025851 * jax.random.uniform(keys[3], (NG, CW), jnp.float32) ** level_of(keys[3], (NG, CW), ((0, 128),), -0.2, 0.2)), 0.3, 3.0),
        "slack": jnp.clip(jnp.exp(math.log(3.0) - 2.3025851 * jax.random.uniform(keys[4], (NG, CW), jnp.float32) ** level_of(keys[4], (NG, CW), ((0, 128),), -0.2, 0.2)), 0.3, 3.0),
        "cost": gaussian(keys[5], (NG, CW), 1.0, 6.0, ((0, 128),), jnp.float32),
        "duals": gaussian(keys[6], (LB, BS), 1.0, 6.0, ((0, 4),), jnp.float32),
        "demand": gaussian(keys[7], (LB, BS), 1.0, 6.0, ((0, 4),), jnp.float32),
    }


SIGMA = 0.3
REGULAR = 1.0
PRECISE = lax.Precision.HIGHEST

def invert_blocks(blocks):
    identity = jnp.eye(blocks.shape[1], dtype=jnp.float32)

    def invert_one(matrix):
        factor = jnp.linalg.cholesky(matrix)
        return jax.scipy.linalg.cho_solve((factor, True), identity)
    return jax.vmap(invert_one)(blocks + REGULAR * identity)

def reference(coeffs, block_ids, col_counts, primal, slack, cost, duals, demand):
    total_blocks = duals.shape[0]
    groups_all = coeffs.shape[0]
    span = coeffs.shape[1]
    rows_tile = coeffs.shape[2]
    columns = coeffs.shape[3]
    valid = (jnp.arange(columns, dtype=jnp.int32)[None, :] < col_counts[:, None]).astype(jnp.float32)
    tile_vals = coeffs * valid[:, None, None, :]
    mean_comp = jnp.sum(valid * primal * slack) / jnp.sum(valid)
    scaling = primal / slack
    flat_ids = block_ids.reshape(groups_all * span)
    onehot = (flat_ids[:, None] == jnp.arange(total_blocks, dtype=jnp.int32)[None, :]).astype(jnp.float32)

    def transpose_apply(vector):
        per_tile = jnp.dot(onehot, vector, precision=PRECISE).reshape(groups_all, span, rows_tile)
        return jnp.einsum('gsij,gsi->gj', tile_vals, per_tile, precision=PRECISE)

    def forward_apply(colvec):
        per_tile = jnp.einsum('gsij,gj->gsi', tile_vals, colvec, precision=PRECISE)
        return jnp.dot(onehot.T, per_tile.reshape(groups_all * span, rows_tile), precision=PRECISE)
    dual_res = cost - transpose_apply(duals) - slack
    comp_res = SIGMA * mean_comp - primal * slack
    shifted = primal - scaling * dual_res + comp_res / slack
    rhs = demand - forward_apply(shifted)
    groups = groups_all // NG_DEV

    def add_group(totals, pieces):
        group_vals, group_scale, group_hot = pieces
        weighted = group_vals * group_scale[:, None, None, :]
        gram = jnp.einsum('gsij,gskj->gsik', weighted, group_vals, precision=PRECISE)
        gram = gram.reshape(group_hot.shape[0], rows_tile, rows_tile)
        return (totals + jnp.einsum('tb,tik->bik', group_hot, gram, precision=PRECISE), None)
    start = jnp.zeros((total_blocks, rows_tile, rows_tile), jnp.float32)
    blocks, _ = lax.scan(add_group, start, (tile_vals.reshape(groups, NG_DEV, span, rows_tile, columns), scaling.reshape(groups, NG_DEV, columns), onehot.reshape(groups, NG_DEV * span, total_blocks)))
    inverse = invert_blocks(blocks)

    def precondition(vector):
        return jnp.einsum('bij,bj->bi', inverse, vector, precision=PRECISE)

    def operate(vector):
        return forward_apply(scaling * transpose_apply(vector)) + REGULAR * vector
    step_dual = jnp.zeros_like(rhs)
    residual = rhs
    smoothed = precondition(residual)
    direction = smoothed
    norm_now = jnp.sum(residual * smoothed)
    for turn in range(ITERS):
        image = operate(direction)
        step_len = norm_now / jnp.sum(direction * image)
        step_dual = step_dual + step_len * direction
        residual = residual - step_len * image
        if turn + 1 < ITERS:
            smoothed = precondition(residual)
            norm_next = jnp.sum(residual * smoothed)
            direction = smoothed + norm_next / norm_now * direction
            norm_now = norm_next
    step_primal = valid * (scaling * transpose_apply(step_dual) + comp_res / slack - scaling * dual_res)
    return (step_dual, step_primal)
```

```python
import jax
import jax.numpy as jnp
from jax import lax
from jax.experimental import pallas as pl
from jax.experimental.pallas import tpu as pltpu
from jax.sharding import Mesh, PartitionSpec as P

ITERS = 3
SIGMA = 0.3
REGULAR = 1.0
PRECISE = lax.Precision.HIGHEST

N = 128
HALF = 64
SPAN = 4
GROUPS = 16
TILES = GROUPS * SPAN
EXTRA = 8
ROWS = HALF + EXTRA

VMEM = pltpu.MemorySpace.VMEM
SMEM = pltpu.MemorySpace.SMEM
NT = (((1,), (1,)), ((), ()))


def iota(shape, axis):
    return lax.broadcasted_iota(jnp.int32, shape, axis)


def vspec():
    return pl.BlockSpec(memory_space=VMEM)


def sspec():
    return pl.BlockSpec(memory_space=SMEM)


def f32(*shape):
    return jax.ShapeDtypeStruct(shape, jnp.float32)


def params():
    return pltpu.CompilerParams(vmem_limit_bytes=48 << 20)


def gram_kernel(
    ids, counts, me, coeffs, primal, slack, own, other, small, scale_out, acc, diag, sem
):
    g = pl.program_id(0)

    @pl.when(g == 0)
    def _():
        acc[...] = jnp.zeros_like(acc)
        diag[...] = jnp.zeros_like(diag)

    valid = iota((1, N), 1) < counts[g]
    scale = jnp.where(valid, primal[pl.ds(g, 1), :] / slack[pl.ds(g, 1), :], 0.0)
    scale_out[pl.ds(g, 1), :] = scale
    row = iota((HALF, N), 0)
    lane = iota((HALF, N), 1)
    lower = jnp.logical_or(row >= lane, lane >= HALF)
    for s in range(SPAN):
        tile = coeffs[0, s]
        gram = lax.dot_general(
            tile * scale, tile, NT, precision=PRECISE, preferred_element_type=jnp.float32
        )
        top = gram[:HALF]
        rolled = pltpu.roll(gram[HALF:], HALF, 1)
        packed = jnp.where(lower, top, rolled)
        line = jnp.sum(jnp.where(row == lane, rolled, 0.0), axis=0, keepdims=True)
        block = ids[g * SPAN + s]
        place = ((block & 1) ^ me[0]) * HALF + (block >> 1)
        acc[place] += packed
        diag[place, 0:1, :] += line

    @pl.when(g == GROUPS - 1)
    def _():
        copies = [
            pltpu.make_async_copy(acc.at[pl.ds(0, HALF)], own, sem.at[0]),
            pltpu.make_async_copy(acc.at[pl.ds(HALF, HALF)], other, sem.at[1]),
            pltpu.make_async_copy(diag, small, sem.at[2]),
        ]
        for copy in copies:
            copy.start()
        for copy in copies:
            copy.wait()


def run_gram(ids, counts, me, coeffs, primal, slack):
    return pl.pallas_call(
        gram_kernel,
        out_shape=(f32(HALF, HALF, N), f32(HALF, HALF, N), f32(N, EXTRA, N), f32(GROUPS, N)),
        grid_spec=pltpu.PrefetchScalarGridSpec(
            num_scalar_prefetch=3,
            grid=(GROUPS,),
            in_specs=[
                pl.BlockSpec((1, SPAN, N, N), lambda g, *_: (g, 0, 0, 0)),
                pl.BlockSpec((GROUPS, N), lambda g, *_: (0, 0)),
                pl.BlockSpec((GROUPS, N), lambda g, *_: (0, 0)),
            ],
            out_specs=(
                pl.BlockSpec(memory_space=pl.ANY),
                pl.BlockSpec(memory_space=pl.ANY),
                pl.BlockSpec(memory_space=pl.ANY),
                pl.BlockSpec((GROUPS, N), lambda g, *_: (0, 0)),
            ),
            scratch_shapes=[
                pltpu.VMEM((N, HALF, N), jnp.float32),
                pltpu.VMEM((N, EXTRA, N), jnp.float32),
                pltpu.SemaphoreType.DMA((3,)),
            ],
        ),
        compiler_params=params(),
        cost_estimate=pl.CostEstimate(
            flops=TILES * 2 * N**3 * 6, bytes_accessed=12 << 20, transcendentals=0
        ),
        name="gram",
    )(ids, counts, me, coeffs, primal, slack)


def transpose_apply(ids, coeffs, vector, spread):
    for t in range(TILES):
        spread[pl.ds(t, 1), :] = vector[pl.ds(ids[t], 1), :]
    columns = jnp.transpose(spread[...])
    lines = []
    for g in range(GROUPS):
        total = None
        for s in range(SPAN):
            t = g * SPAN + s
            prod = coeffs[g, s] * jnp.broadcast_to(columns[:, t : t + 1], (N, N))
            part = jnp.sum(prod.reshape(N // 8, 8, N), axis=0)
            total = part if total is None else total + part
        lines.append(jnp.sum(total, axis=0, keepdims=True))
    return jnp.concatenate(lines, axis=0)


def forward_apply(coeffs, colvec):
    lane = iota((N, N), 1)
    columns = jnp.zeros((N, N), jnp.float32)
    for g in range(GROUPS):
        w = colvec[g : g + 1, :]
        for s in range(SPAN):
            t = g * SPAN + s
            total = jnp.sum(coeffs[g, s] * w, axis=1, keepdims=True)
            columns = jnp.where(lane == t, total, columns)
    return jnp.transpose(columns)[:TILES]


def place_rows(ids_line, rows, count, stride, offset):
    hot = (iota((count, TILES), 0) == stride * ids_line + offset).astype(jnp.float32)
    return jnp.dot(hot, rows, precision=PRECISE, preferred_element_type=jnp.float32)


def rhs_kernel(
    ids, counts, ids_line, coeffs, dual0, dual1, dual2, dual3, primal, slack, cost, scale, small,
    small_out, dual_res_out, spread, duals, valid_s,
):
    for k, part in enumerate((dual0, dual1, dual2, dual3)):
        duals[pl.ds(k * 32, 32), :] = part[...]
    for g in range(GROUPS):
        valid_s[pl.ds(g, 1), :] = (iota((1, N), 1) < counts[g]).astype(jnp.float32)
    valid = valid_s[...]
    dual_res = cost[...] - valid * transpose_apply(ids[0], coeffs, duals, spread) - slack[...]
    dual_res_out[...] = dual_res
    first = forward_apply(coeffs, scale[...] * dual_res)
    second = forward_apply(coeffs, valid / slack[...])
    small_out[:, 0:1, :] = small[:, 0:1, :]
    rows1 = place_rows(ids_line[...], first, N, 1, 0)
    rows2 = place_rows(ids_line[...], second, N, 1, 0)
    comp = jnp.sum(valid * primal[...] * slack[...], axis=0, keepdims=True)
    used = jnp.sum(valid, axis=0, keepdims=True)
    small_out[:, 1:2, :] = rows1.reshape(N, 1, N)
    small_out[:, 2:3, :] = rows2.reshape(N, 1, N)
    small_out[:, 3:4, :] = jnp.broadcast_to(comp.reshape(1, 1, N), (N, 1, N))
    small_out[:, 4:5, :] = jnp.broadcast_to(used.reshape(1, 1, N), (N, 1, N))
    small_out[:, 5:8, :] = jnp.zeros((N, 3, N), jnp.float32)


class Row:
    def __init__(self, ref, row):
        self.ref, self.row = ref, row

    def __getitem__(self, t):
        return self.ref[self.row, t]


def run_rhs(ids_dual, counts, ids_line, coeffs, duals, primal, slack, cost, scale, small):
    def kernel(ids_ref, *refs):
        rhs_kernel((Row(ids_ref, 0),), *refs)

    return pl.pallas_call(
        kernel,
        out_shape=(f32(N, EXTRA, N), f32(GROUPS, N)),
        in_specs=[sspec(), sspec()] + [vspec()] * 11,
        out_specs=(vspec(), vspec()),
        scratch_shapes=[
            pltpu.VMEM((TILES, N), jnp.float32),
            pltpu.VMEM((N, N), jnp.float32),
            pltpu.VMEM((GROUPS, N), jnp.float32),
        ],
        compiler_params=params(),
        cost_estimate=pl.CostEstimate(flops=1 << 27, bytes_accessed=6 << 20, transcendentals=0),
        name="rhs",
    )(ids_dual, counts, ids_line, coeffs, *duals, primal, slack, cost, scale, small)


def join_kernel(own, got, small_own, small_got, out):
    out[:, 0:HALF, :] = own[...] + got[...]
    out[:, HALF:ROWS, :] = small_own[...] + small_got[...]


def run_join(own, got, small_own, small_got):
    step = 8
    big = pl.BlockSpec((step, HALF, N), lambda i: (i, 0, 0))
    little = pl.BlockSpec((step, EXTRA, N), lambda i: (i, 0, 0))
    return pl.pallas_call(
        join_kernel,
        out_shape=f32(HALF, ROWS, N),
        grid=(HALF // step,),
        in_specs=[big, big, little, little],
        out_specs=pl.BlockSpec((step, ROWS, N), lambda i: (i, 0, 0)),
        compiler_params=params(),
        name="join",
    )(own, got, small_own, small_got)


def small_inverse(cols):
    cols = list(cols)
    sub = iota((8, N), 0)
    for m in range(8):
        rows = [jnp.broadcast_to(c[m : m + 1, :], (8, N)) for c in cols]
        inv = 1.0 / rows[m]
        factor = cols[m]
        here = sub == m
        for j in range(8):
            if j == m:
                cols[j] = jnp.where(here, inv, -factor * inv)
            else:
                scaled = rows[j] * inv
                cols[j] = jnp.where(here, scaled, cols[j] - factor * scaled)
    return cols


def invert(panels):
    panels = list(panels)
    lane = iota((8, N), 1)
    count = len(panels)
    for k in range(count):
        mine = jnp.logical_and(lane >= 8 * k, lane < 8 * k + 8)
        pivot = panels[k]
        cols = [jnp.broadcast_to(pivot[:, 8 * k + m : 8 * k + m + 1], (8, N)) for m in range(8)]
        cols = small_inverse(cols)
        total = None
        for m in range(8):
            term = cols[m] * jnp.broadcast_to(pivot[m : m + 1, :], (8, N))
            total = term if total is None else total + term
        for m in range(8):
            total = jnp.where(lane == 8 * k + m, cols[m], total)
        rows = [jnp.broadcast_to(total[m : m + 1, :], (8, N)) for m in range(8)]
        for step in range(1, count):
            i = (k + step) % count
            old = panels[i]
            new = jnp.where(mine, 0.0, old)
            for m in range(8):
                col = jnp.broadcast_to(old[:, 8 * k + m : 8 * k + m + 1], (8, N))
                new = new - col * rows[m]
            panels[i] = new
        panels[k] = total
    return panels


def pair_rows(first, second):
    return jnp.where((iota((8, N), 0) & 1) == 0, first, second)


def set_message(msg, line, scalar):
    pair = pair_rows(jnp.broadcast_to(line, (8, N)), jnp.broadcast_to(scalar, (8, N)))
    msg[...] = jnp.broadcast_to(pair[None], (N // 4, 8, N)).reshape(2 * N, N)


def first_kernel(me, got, demand, inverse_out, residual_out, mu_out, msg):
    def add(i, carry):
        return carry + got[i]

    total = lax.fori_loop(1, HALF, add, got[0], unroll=7)
    packed = total[:HALF]
    line = total[HALF : HALF + 1]
    tail = total[HALF:]
    comp = jnp.sum(tail[3:4], axis=1, keepdims=True)
    used = jnp.sum(tail[4:5], axis=1, keepdims=True)
    mu = SIGMA * (comp / used)
    mu_out[...] = jnp.broadcast_to(mu, (8, N))
    residual = demand[pl.ds(me[0], 1), :] + tail[1:2] - mu * tail[2:3]
    residual_out[...] = jnp.broadcast_to(residual, (8, N))

    row = iota((HALF, N), 0)
    lane = iota((HALF, N), 1)
    flipped = jnp.transpose(jnp.concatenate([packed, jnp.zeros((HALF, N), jnp.float32)], axis=0))
    flip_top, flip_bottom = flipped[:HALF], flipped[HALF:]
    top = jnp.where(jnp.logical_or(row >= lane, lane >= HALF), packed, flip_top)
    corner = jnp.where(row < lane, packed, flip_top)
    corner = jnp.where(row == lane, jnp.broadcast_to(line, (HALF, N)), corner)
    bottom = jnp.where(lane < HALF, flip_bottom, pltpu.roll(corner, HALF, 1))
    top = top + jnp.where(row == lane, REGULAR, 0.0)
    bottom = bottom + jnp.where(row + HALF == lane, REGULAR, 0.0)
    panels = [top[8 * i : 8 * i + 8] for i in range(8)]
    panels += [bottom[8 * i : 8 * i + 8] for i in range(8)]
    inverse = jnp.concatenate(invert(panels), axis=0)
    inverse_out[...] = inverse
    smoothed = jnp.dot(
        jnp.broadcast_to(residual, (8, N)),
        inverse,
        precision=PRECISE,
        preferred_element_type=jnp.float32,
    )[0:1]
    norm = jnp.sum(residual * smoothed, axis=1, keepdims=True)
    set_message(msg, smoothed, norm)


def run_first(me, got, demand):
    return pl.pallas_call(
        first_kernel,
        out_shape=(f32(N, N), f32(8, N), f32(8, N), f32(2 * N, N)),
        in_specs=[sspec(), vspec(), vspec()],
        out_specs=(vspec(),) * 4,
        compiler_params=params(),
        name="first",
    )(me, got, demand)


def sum_pairs(got):
    total = jnp.sum(got[...].reshape(N // 4, 8, N), axis=0)
    even = (total[0:1] + total[2:3]) + (total[4:5] + total[6:7])
    odd = (total[1:2] + total[3:4]) + (total[5:6] + total[7:8])
    return even, odd


def owner_kernel(me, got, direction, norms, residual, inverse, residual_out, msg):
    image, curve = sum_pairs(got)
    image = image + REGULAR * direction[pl.ds(me[0], 1), :]
    curve = jnp.sum(curve, axis=1, keepdims=True)
    step_len = norms[0:1, :] / (curve + norms[1:2, :])
    new = residual[0:1, :] - step_len * image
    residual_out[...] = pair_rows(jnp.broadcast_to(new, (8, N)), jnp.broadcast_to(curve, (8, N)))
    smoothed = jnp.dot(
        jnp.broadcast_to(new, (8, N)),
        inverse[...],
        precision=PRECISE,
        preferred_element_type=jnp.float32,
    )[0:1]
    set_message(msg, smoothed, jnp.sum(new * smoothed, axis=1, keepdims=True))


def run_owner(me, got, direction, norms, residual, inverse):
    return pl.pallas_call(
        owner_kernel,
        out_shape=(f32(8, N), f32(2 * N, N)),
        in_specs=[sspec()] + [vspec()] * 5,
        out_specs=(vspec(),) * 2,
        compiler_params=params(),
        name="owner",
    )(me, got, direction, norms, residual, inverse)


def tile_kernel(last, begin, ids, ids_line, coeffs, scale, got, *refs):
    if begin:
        direction_out, applied_out, norms_out, msg, spread = refs
    else:
        direction_in, norms_in, direction_out, applied_out, norms_out, msg, spread = refs
    pairs = got[...].reshape(N, 2, N)
    smoothed = pairs[:, 0, :]
    norm = jnp.sum(pairs[:, 1, :], axis=0, keepdims=True)
    if begin:
        direction = smoothed
    else:
        direction = smoothed + (norm / norms_in[0:1, :]) * direction_in[...]
    direction_out[...] = direction
    square = jnp.sum(jnp.sum(direction * direction, axis=0, keepdims=True), axis=1, keepdims=True)
    square = jnp.broadcast_to(REGULAR * square, (1, N))
    norms_out[0:1, :] = norm
    norms_out[1:2, :] = square
    applied = transpose_apply(ids, coeffs, direction_out, spread)
    applied_out[...] = applied
    weighted = scale[...] * applied
    curve = jnp.sum(weighted * applied, axis=0, keepdims=True)
    if last:
        msg[...] = jnp.broadcast_to(curve, (N, N))
    else:
        image = place_rows(ids_line[...], forward_apply(coeffs, weighted), 2 * N, 2, 0)
        odd = (iota((2 * N, N), 0) & 1) == 1
        msg[...] = jnp.where(odd, jnp.broadcast_to(curve, (2 * N, N)), image)


def run_tile(last, ids, ids_line, coeffs, scale, got, direction=None, norms=None):
    begin = direction is None
    extra = () if begin else (direction, norms)

    def kernel(*refs):
        tile_kernel(last, begin, *refs)

    return pl.pallas_call(
        kernel,
        out_shape=(f32(N, N), f32(GROUPS, N), f32(8, N), f32(N if last else 2 * N, N)),
        in_specs=[sspec()] + [vspec()] * (4 + len(extra)),
        out_specs=(vspec(),) * 4,
        scratch_shapes=[pltpu.VMEM((TILES, N), jnp.float32)],
        compiler_params=params(),
        name="tile_last" if last else "tile",
    )(ids, ids_line, coeffs, scale, got, *extra)


def final_kernel(
    leg, counts, got, curve0, curve1, d0, d1, d2, u0, u1, u2, n0, n1, n2, mu, primal, slack,
    scale, dual_res, step_dual, step_primal,
):
    curve2 = jnp.sum(jnp.sum(got[...], axis=0, keepdims=True), axis=1, keepdims=True)
    lens = []
    for curve, norms in ((curve0[1:2, :], n0), (curve1[1:2, :], n1), (curve2, n2)):
        lens.append(norms[0:1, :] / (curve + norms[1:2, :]))
    at = pl.ds(pl.multiple_of(leg[0] * 32, 32), 32)
    step_dual[...] = lens[0] * d0[at, :] + lens[1] * d1[at, :] + lens[2] * d2[at, :]
    applied = lens[0] * u0[...] + lens[1] * u1[...] + lens[2] * u2[...]
    inner = scale[...] * (applied - dual_res[...]) + (mu[0:1, :] / slack[...] - primal[...])
    for g in range(GROUPS):
        valid = iota((1, N), 1) < counts[g]
        step_primal[g : g + 1, :] = jnp.where(valid, inner[g : g + 1, :], 0.0)


def run_final(leg, counts, *args):
    return pl.pallas_call(
        final_kernel,
        out_shape=(f32(32, N), f32(GROUPS, N)),
        in_specs=[sspec(), sspec()] + [vspec()] * len(args),
        out_specs=(vspec(), vspec()),
        compiler_params=params(),
        name="final",
    )(leg, counts, *args)


ALL = ("leg", "x", "z", "core")
CHIPS = ("leg", "x", "z")


def exchange(rows, axes):
    return lax.all_to_all(rows, axes, split_axis=0, concat_axis=0, tiled=True)


def per_device(coeffs, block_ids, col_counts, primal, slack, cost, duals, demand):
    leg = lax.axis_index("leg")
    core = lax.axis_index("core")
    col = (lax.axis_index("x") * 4 + lax.axis_index("z")) * 2 + core
    ids = block_ids.reshape(TILES)
    me = (leg * 32 + col).astype(jnp.int32).reshape(1)
    core1 = core.astype(jnp.int32).reshape(1)

    parts = [duals]
    for k in (1, 2, 3):
        parts.append(lax.ppermute(duals, "leg", [(i, (i + k) % 4) for i in range(4)]))
    ids_dual = ((((leg - (ids >> 5)) & 3) << 5) | (ids & 31)).reshape(1, TILES)
    place = ((ids & 1) ^ core) * HALF + (ids >> 1)

    own, other, small, scale = run_gram(ids, col_counts, core1, coeffs, primal, slack)
    swap = [(0, 1), (1, 0)]
    got_big = lax.ppermute(other, "core", swap)
    small, dual_res = run_rhs(
        ids_dual, col_counts, place.reshape(1, TILES), coeffs, parts, primal, slack, cost, scale,
        small,
    )
    got_small = lax.ppermute(small[HALF:], "core", swap)
    joined = run_join(own, got_big, small[:HALF], got_small)
    blocks = exchange(joined, CHIPS)
    inverse, residual, mu, msg = run_first(col.astype(jnp.int32).reshape(1), blocks, demand)

    ids_line = ids.reshape(1, TILES)
    direction = norms = None
    kept = []
    curves = []
    for turn in range(ITERS):
        got = exchange(msg, ALL)
        last = turn + 1 == ITERS
        direction, applied, norms, msg = run_tile(
            last, ids, ids_line, coeffs, scale, got, direction, norms
        )
        kept.append((direction, applied, norms))
        got = exchange(msg, ALL)
        if not last:
            residual, msg = run_owner(me, got, direction, norms, residual, inverse)
            curves.append(residual)
    (d0, u0, n0), (d1, u1, n1), (d2, u2, n2) = kept
    return run_final(
        leg.astype(jnp.int32).reshape(1), col_counts, got, curves[0], curves[1], d0, d1, d2,
        u0, u1, u2, n0, n1, n2, mu, primal, slack, scale, dual_res,
    )


def solution(mesh):
    fine = Mesh(mesh.devices.reshape(4, 4, 2, 4), ("x", "z", "core", "leg"))
    every = ("x", "z", "core", "leg")
    return jax.shard_map(
        per_device,
        mesh=fine,
        in_specs=(
            P(every, None, None, None),
            P(every, None),
            P(every),
            P(every, None),
            P(every, None),
            P(every, None),
            P("leg", None),
            P("leg", None),
        ),
        out_specs=(P("leg", None), P(every, None)),
        check_vma=False,
    )
```

```python
import jax
import jax.numpy as jnp
from jax import lax
from jax.experimental import pallas as pl
from jax.experimental.pallas import tpu as pltpu
from jax.sharding import Mesh, PartitionSpec as P

ITERS = 3
SIGMA = 0.3
REGULAR = 1.0
PRECISE = lax.Precision.HIGHEST

N = 128
HALF = 64
SPAN = 4
GROUPS = 16
TILES = GROUPS * SPAN
EXTRA = 8
ROWS = HALF + EXTRA

VMEM = pltpu.MemorySpace.VMEM
SMEM = pltpu.MemorySpace.SMEM
HBM = pltpu.MemorySpace.HBM
NT = (((1,), (1,)), ((), ()))


def iota(shape, axis):
    return lax.broadcasted_iota(jnp.int32, shape, axis)


def vspec():
    return pl.BlockSpec(memory_space=VMEM)


def sspec():
    return pl.BlockSpec(memory_space=SMEM)


def f32(*shape):
    return jax.ShapeDtypeStruct(shape, jnp.float32)


def device_col():
    return (lax.axis_index("x") * 4 + lax.axis_index("z")) * 2 + lax.axis_index("core")


def params():
    return pltpu.CompilerParams(vmem_limit_bytes=24 << 20)


def split(x):
    high = x.astype(jnp.bfloat16)
    return high, (x - high.astype(jnp.float32)).astype(jnp.bfloat16)


def gram_product(tile, root):
    high, low = split(tile * root)
    both = lax.dot_general(high, high, NT, preferred_element_type=jnp.float32)
    cross = lax.dot_general(
        jnp.concatenate([high, low], axis=1),
        jnp.concatenate([low, high], axis=1),
        NT,
        preferred_element_type=jnp.float32,
    )
    return both + cross


UNROLL = 4


def gram_kernel(
    coeffs_in, ids_in, counts_in, primal_in, slack_in, coeffs, acc, other, small, scale_out,
    hot_ids, hot_place, ids, counts, primal, slack, hot, hot2, sem, tile_sem,
):
    little = [
        pltpu.make_async_copy(ids_in, ids, sem.at[0]),
        pltpu.make_async_copy(counts_in, counts, sem.at[1]),
        pltpu.make_async_copy(primal_in, primal, sem.at[2]),
        pltpu.make_async_copy(slack_in, slack, sem.at[3]),
    ]
    for copy in little:
        copy.start()
    for g in range(GROUPS):
        pltpu.make_async_copy(coeffs_in.at[g], coeffs.at[g], tile_sem.at[g]).start()
    acc[...] = jnp.zeros_like(acc)
    small[...] = jnp.zeros_like(small)
    hot[...] = jnp.zeros_like(hot)
    hot2[...] = jnp.zeros_like(hot2)
    core = lax.axis_index("core")
    for copy in little:
        copy.wait()
    row = iota((HALF, N), 0)
    lane = iota((HALF, N), 1)
    line_lane = iota((1, N), 1)
    lower = jnp.logical_or(row >= lane, lane >= HALF)

    def group(g):
        pltpu.make_async_copy(coeffs_in.at[g], coeffs.at[g], tile_sem.at[g]).wait()
        valid = line_lane < counts[g]
        scale = jnp.where(valid, primal[pl.ds(g, 1), :] / slack[pl.ds(g, 1), :], 0.0)
        scale_out[pl.ds(g, 1), :] = scale
        root = jnp.sqrt(scale)
        for s in range(SPAN):
            gram = gram_product(coeffs[g, s], root)
            rolled = pltpu.roll(gram[HALF:], HALF, 1)
            packed = jnp.where(lower, gram[:HALF], rolled)
            line = jnp.sum(jnp.where(row == lane, rolled, 0.0), axis=0, keepdims=True)
            block = ids[s, g]
            place = ((block & 1) ^ core) * HALF + (block >> 1)
            acc[place] += packed
            small[place, 0:1, :] += line
            t = g * SPAN + s
            hot[pl.ds(t, 1), :] = (line_lane == block).astype(jnp.float32)
            hot2[pl.ds(t, 1), :] = (line_lane == place).astype(jnp.float32)

    @pl.loop(0, GROUPS // UNROLL)
    def _(i):
        for k in range(UNROLL):
            group(i * UNROLL + k)

    other[...] = acc[pl.ds(HALF, HALF)]
    hot_ids[...] = jnp.transpose(hot[...]).astype(jnp.bfloat16)
    hot_place[...] = jnp.transpose(hot2[...]).astype(jnp.bfloat16)


def run_gram(coeffs, ids, counts, primal, slack):
    return pl.pallas_call(
        gram_kernel,
        out_shape=(
            f32(GROUPS, SPAN, N, N),
            f32(N, HALF, N),
            f32(HALF, HALF, N),
            f32(N, EXTRA, N),
            f32(GROUPS, N),
            jax.ShapeDtypeStruct((N, N), jnp.bfloat16),
            jax.ShapeDtypeStruct((N, N), jnp.bfloat16),
        ),
        in_specs=[pl.BlockSpec(memory_space=HBM)] * 5,
        out_specs=(vspec(),) * 7,
        scratch_shapes=[
            pltpu.SMEM((SPAN, GROUPS), jnp.int32),
            pltpu.SMEM((GROUPS,), jnp.int32),
            pltpu.VMEM((GROUPS, N), jnp.float32),
            pltpu.VMEM((GROUPS, N), jnp.float32),
            pltpu.VMEM((N, N), jnp.float32),
            pltpu.VMEM((N, N), jnp.float32),
            pltpu.SemaphoreType.DMA((4,)),
            pltpu.SemaphoreType.DMA((GROUPS,)),
        ],
        compiler_params=params(),
        cost_estimate=pl.CostEstimate(
            flops=TILES * 2 * N**3 * 3, bytes_accessed=12 << 20, transcendentals=0
        ),
        name="gram",
    )(*(pltpu.with_memory_space_constraint(x, HBM) for x in (coeffs, ids, counts, primal, slack)))


def transpose_apply(ids, coeffs, vector, spread):
    for t in range(TILES):
        spread[pl.ds(t, 1), :] = vector[pl.ds(ids[t % SPAN, t // SPAN], 1), :]
    columns = jnp.transpose(spread[...])
    lines = []
    for g in range(GROUPS):
        total = None
        for s in range(SPAN):
            t = g * SPAN + s
            prod = coeffs[g, s] * jnp.broadcast_to(columns[:, t : t + 1], (N, N))
            part = jnp.sum(prod.reshape(N // 8, 8, N), axis=0)
            total = part if total is None else total + part
        lines.append(jnp.sum(total, axis=0, keepdims=True))
    return jnp.concatenate(lines, axis=0)


def forward_apply(coeffs, colvec):
    lane = iota((N, N), 1)
    columns = jnp.zeros((N, N), jnp.float32)
    for g in range(GROUPS):
        w = colvec[g : g + 1, :]
        for s in range(SPAN):
            t = g * SPAN + s
            total = jnp.sum(coeffs[g, s] * w, axis=1, keepdims=True)
            columns = jnp.where(lane == t, total, columns)
    return jnp.transpose(columns)[:TILES]


def place_rows(hot, rows):
    rows = jnp.concatenate([rows, jnp.zeros((N - TILES, N), jnp.float32)], axis=0)
    high, rest = rows.astype(jnp.bfloat16), None
    rest = rows - high.astype(jnp.float32)
    middle, low = split(rest)
    total = jnp.dot(hot, high, preferred_element_type=jnp.float32)
    total = total + jnp.dot(hot, middle, preferred_element_type=jnp.float32)
    return total + jnp.dot(hot, low, preferred_element_type=jnp.float32)


def rhs_kernel(
    ids, counts, hot_place, coeffs, dual0, dual1, dual2, dual3, primal, slack, cost, scale, small,
    own_out, other_out, dual_res_out, spread, duals, valid_s,
):
    leg = lax.axis_index("leg")
    for k, part in enumerate((dual0, dual1, dual2, dual3)):
        at = pl.multiple_of(((leg - k) & 3) * 32, 32)
        duals[pl.ds(at, 32), :] = part[...]
    for g in range(GROUPS):
        valid_s[pl.ds(g, 1), :] = (iota((1, N), 1) < counts[g]).astype(jnp.float32)
    valid = valid_s[...]
    dual_res = cost[...] - valid * transpose_apply(ids, coeffs, duals, spread) - slack[...]
    dual_res_out[...] = dual_res
    first = place_rows(hot_place[...], forward_apply(coeffs, scale[...] * dual_res))
    second = place_rows(hot_place[...], forward_apply(coeffs, valid / slack[...]))
    comp = jnp.sum(valid * primal[...] * slack[...], axis=0, keepdims=True)
    used = jnp.sum(valid, axis=0, keepdims=True)
    for k, out in enumerate((own_out, other_out)):
        half = slice(k * HALF, k * HALF + HALF)
        out[:, 0:1, :] = small[half, 0:1, :]
        out[:, 1:2, :] = first[half].reshape(HALF, 1, N)
        out[:, 2:3, :] = second[half].reshape(HALF, 1, N)
        out[:, 3:4, :] = jnp.broadcast_to(comp.reshape(1, 1, N), (HALF, 1, N))
        out[:, 4:5, :] = jnp.broadcast_to(used.reshape(1, 1, N), (HALF, 1, N))
        out[:, 5:8, :] = jnp.zeros((HALF, 3, N), jnp.float32)


def run_rhs(ids, counts, hot_place, coeffs, duals, primal, slack, cost, scale, small):
    return pl.pallas_call(
        rhs_kernel,
        out_shape=(f32(HALF, EXTRA, N), f32(HALF, EXTRA, N), f32(GROUPS, N)),
        in_specs=[sspec(), sspec()] + [vspec()] * 11,
        out_specs=(vspec(),) * 3,
        scratch_shapes=[
            pltpu.VMEM((TILES, N), jnp.float32),
            pltpu.VMEM((N, N), jnp.float32),
            pltpu.VMEM((GROUPS, N), jnp.float32),
        ],
        compiler_params=params(),
        cost_estimate=pl.CostEstimate(flops=1 << 27, bytes_accessed=6 << 20, transcendentals=0),
        name="rhs",
    )(ids, counts, hot_place, coeffs, *duals, primal, slack, cost, scale, small)


def join_kernel(acc, got, small, small_got, out):
    out[:, 0:HALF, :] = acc[pl.ds(0, HALF)] + got[...]
    out[:, HALF:ROWS, :] = small[...] + small_got[...]


def run_join(acc, got, small, small_got):
    return pl.pallas_call(
        join_kernel,
        out_shape=f32(HALF, ROWS, N),
        in_specs=[vspec()] * 4,
        out_specs=vspec(),
        compiler_params=params(),
        name="join",
    )(acc, got, small, small_got)


def small_inverse(cols):
    cols = list(cols)
    sub = iota((8, N), 0)
    for m in range(8):
        rows = [jnp.broadcast_to(c[m : m + 1, :], (8, N)) for c in cols]
        inv = 1.0 / rows[m]
        factor = cols[m]
        here = sub == m
        for j in range(8):
            if j == m:
                cols[j] = jnp.where(here, inv, -factor * inv)
            else:
                scaled = rows[j] * inv
                cols[j] = jnp.where(here, scaled, cols[j] - factor * scaled)
    return cols


def invert(panels):
    panels = list(panels)
    lane = iota((8, N), 1)
    count = len(panels)
    for k in range(count):
        mine = jnp.logical_and(lane >= 8 * k, lane < 8 * k + 8)
        pivot = panels[k]
        cols = [jnp.broadcast_to(pivot[:, 8 * k + m : 8 * k + m + 1], (8, N)) for m in range(8)]
        cols = small_inverse(cols)
        total = None
        for m in range(8):
            term = cols[m] * jnp.broadcast_to(pivot[m : m + 1, :], (8, N))
            total = term if total is None else total + term
        for m in range(8):
            total = jnp.where(lane == 8 * k + m, cols[m], total)
        rows = [jnp.broadcast_to(total[m : m + 1, :], (8, N)) for m in range(8)]
        for step in range(1, count):
            i = (k + step) % count
            old = panels[i]
            new = jnp.where(mine, 0.0, old)
            for m in range(8):
                col = jnp.broadcast_to(old[:, 8 * k + m : 8 * k + m + 1], (8, N))
                new = new - col * rows[m]
            panels[i] = new
        panels[k] = total
    return panels


def pair_rows(first, second):
    return jnp.where((iota((8, N), 0) & 1) == 0, first, second)


def set_message(msg, line, scalar):
    pair = pair_rows(jnp.broadcast_to(line, (8, N)), jnp.broadcast_to(scalar, (8, N)))
    msg[...] = jnp.broadcast_to(pair[None], (N // 4, 8, N)).reshape(2 * N, N)


def first_kernel(got, demand, inverse_out, residual_out, mu_out, msg):
    def add(i, carry):
        return carry + got[i]

    total = lax.fori_loop(1, HALF, add, got[0], unroll=7)
    packed = total[:HALF]
    line = total[HALF : HALF + 1]
    tail = total[HALF:]
    comp = jnp.sum(tail[3:4], axis=1, keepdims=True)
    used = jnp.sum(tail[4:5], axis=1, keepdims=True)
    mu = SIGMA * (comp / used)
    mu_out[...] = jnp.broadcast_to(mu, (8, N))
    residual = demand[pl.ds(device_col(), 1), :] + tail[1:2] - mu * tail[2:3]
    residual_out[...] = jnp.broadcast_to(residual, (8, N))

    row = iota((HALF, N), 0)
    lane = iota((HALF, N), 1)
    flipped = jnp.transpose(jnp.concatenate([packed, jnp.zeros((HALF, N), jnp.float32)], axis=0))
    flip_top, flip_bottom = flipped[:HALF], flipped[HALF:]
    top = jnp.where(jnp.logical_or(row >= lane, lane >= HALF), packed, flip_top)
    corner = jnp.where(row < lane, packed, flip_top)
    corner = jnp.where(row == lane, jnp.broadcast_to(line, (HALF, N)), corner)
    bottom = jnp.where(lane < HALF, flip_bottom, pltpu.roll(corner, HALF, 1))
    top = top + jnp.where(row == lane, REGULAR, 0.0)
    bottom = bottom + jnp.where(row + HALF == lane, REGULAR, 0.0)
    panels = [top[8 * i : 8 * i + 8] for i in range(8)]
    panels += [bottom[8 * i : 8 * i + 8] for i in range(8)]
    inverse = jnp.concatenate(invert(panels), axis=0)
    inverse_out[...] = inverse
    smoothed = jnp.dot(
        jnp.broadcast_to(residual, (8, N)),
        inverse,
        precision=PRECISE,
        preferred_element_type=jnp.float32,
    )[0:1]
    norm = jnp.sum(residual * smoothed, axis=1, keepdims=True)
    set_message(msg, smoothed, norm)


def run_first(got, demand):
    return pl.pallas_call(
        first_kernel,
        out_shape=(f32(N, N), f32(8, N), f32(8, N), f32(2 * N, N)),
        in_specs=[vspec(), vspec()],
        out_specs=(vspec(),) * 4,
        compiler_params=params(),
        name="first",
    )(got, demand)


def sum_pairs(got):
    total = jnp.sum(got[...].reshape(N // 4, 8, N), axis=0)
    even = (total[0:1] + total[2:3]) + (total[4:5] + total[6:7])
    odd = (total[1:2] + total[3:4]) + (total[5:6] + total[7:8])
    return even, odd


def owner_kernel(got, direction, norms, residual, inverse, residual_out, msg):
    image, curve = sum_pairs(got)
    image = image + REGULAR * direction[pl.ds(lax.axis_index("leg") * 32 + device_col(), 1), :]
    curve = jnp.sum(curve, axis=1, keepdims=True)
    step_len = norms[0:1, :] / (curve + norms[1:2, :])
    new = residual[0:1, :] - step_len * image
    residual_out[...] = pair_rows(jnp.broadcast_to(new, (8, N)), jnp.broadcast_to(curve, (8, N)))
    smoothed = jnp.dot(
        jnp.broadcast_to(new, (8, N)),
        inverse[...],
        precision=PRECISE,
        preferred_element_type=jnp.float32,
    )[0:1]
    set_message(msg, smoothed, jnp.sum(new * smoothed, axis=1, keepdims=True))


def run_owner(got, direction, norms, residual, inverse):
    return pl.pallas_call(
        owner_kernel,
        out_shape=(f32(8, N), f32(2 * N, N)),
        in_specs=[vspec()] * 5,
        out_specs=(vspec(),) * 2,
        compiler_params=params(),
        name="owner",
    )(got, direction, norms, residual, inverse)


def tile_kernel(last, begin, ids, hot, coeffs, scale, got, *refs):
    if begin:
        direction_out, applied_out, norms_out, msg, spread = refs
    else:
        direction_in, norms_in, direction_out, applied_out, norms_out, msg, spread = refs
    smoothed = got[pl.ds(0, N, stride=2), :]
    norm = jnp.sum(got[pl.ds(1, N, stride=2), :], axis=0, keepdims=True)
    if begin:
        direction = smoothed
    else:
        direction = smoothed + (norm / norms_in[0:1, :]) * direction_in[...]
    direction_out[...] = direction
    square = jnp.sum(jnp.sum(direction * direction, axis=0, keepdims=True), axis=1, keepdims=True)
    square = jnp.broadcast_to(REGULAR * square, (1, N))
    norms_out[0:1, :] = norm
    norms_out[1:2, :] = square
    applied = transpose_apply(ids, coeffs, direction_out, spread)
    applied_out[...] = applied
    weighted = scale[...] * applied
    curve = jnp.sum(weighted * applied, axis=0, keepdims=True)
    if last:
        msg[...] = jnp.broadcast_to(curve, (N, N))
    else:
        image = place_rows(hot[...], forward_apply(coeffs, weighted))
        msg[pl.ds(0, N, stride=2), :] = image
        msg[pl.ds(1, N, stride=2), :] = jnp.broadcast_to(curve, (N, N))


def run_tile(last, ids, hot, coeffs, scale, got, direction=None, norms=None):
    begin = direction is None
    extra = () if begin else (direction, norms)

    def kernel(*refs):
        tile_kernel(last, begin, *refs)

    return pl.pallas_call(
        kernel,
        out_shape=(f32(N, N), f32(GROUPS, N), f32(8, N), f32(N if last else 2 * N, N)),
        in_specs=[sspec()] + [vspec()] * (4 + len(extra)),
        out_specs=(vspec(),) * 4,
        scratch_shapes=[pltpu.VMEM((TILES, N), jnp.float32)],
        compiler_params=params(),
        name="tile_last" if last else "tile",
    )(ids, hot, coeffs, scale, got, *extra)


def final_kernel(
    counts, got, curve0, curve1, d0, d1, d2, u0, u1, u2, n0, n1, n2, mu, primal, slack,
    scale, dual_res, step_dual, step_primal,
):
    curve2 = jnp.sum(jnp.sum(got[...], axis=0, keepdims=True), axis=1, keepdims=True)
    lens = []
    for curve, norms in ((curve0[1:2, :], n0), (curve1[1:2, :], n1), (curve2, n2)):
        lens.append(norms[0:1, :] / (curve + norms[1:2, :]))
    at = pl.ds(pl.multiple_of(lax.axis_index("leg") * 32, 32), 32)
    step_dual[...] = lens[0] * d0[at, :] + lens[1] * d1[at, :] + lens[2] * d2[at, :]
    applied = lens[0] * u0[...] + lens[1] * u1[...] + lens[2] * u2[...]
    inner = scale[...] * (applied - dual_res[...]) + (mu[0:1, :] / slack[...] - primal[...])
    for g in range(GROUPS):
        valid = iota((1, N), 1) < counts[g]
        step_primal[g : g + 1, :] = jnp.where(valid, inner[g : g + 1, :], 0.0)


def run_final(counts, *args):
    return pl.pallas_call(
        final_kernel,
        out_shape=(f32(32, N), f32(GROUPS, N)),
        in_specs=[sspec()] + [vspec()] * len(args),
        out_specs=(vspec(), vspec()),
        compiler_params=params(),
        name="final",
    )(counts, *args)


ALL = ("leg", "x", "z", "core")
CHIPS = ("leg", "x", "z")


def exchange(rows, axes):
    return lax.all_to_all(rows, axes, split_axis=0, concat_axis=0, tiled=True)


def per_device(coeffs, block_ids, col_counts, primal, slack, cost, duals, demand):
    ids = block_ids.T
    parts = [duals]
    for k in (1, 2, 3):
        parts.append(lax.ppermute(duals, "leg", [(i, (i + k) % 4) for i in range(4)]))

    tiles, acc, other, small, scale, hot, hot_place = run_gram(
        coeffs, ids, col_counts, primal, slack
    )
    swap = [(0, 1), (1, 0)]
    got_big = lax.ppermute(other, "core", swap)
    small, small_other, dual_res = run_rhs(
        ids, col_counts, hot_place, tiles, parts, primal, slack, cost, scale, small
    )
    got_small = lax.ppermute(small_other, "core", swap)
    joined = run_join(acc, got_big, small, got_small)
    blocks = exchange(joined, CHIPS)
    inverse, residual, mu, msg = run_first(blocks, demand)

    direction = norms = None
    kept = []
    curves = []
    for turn in range(ITERS):
        got = exchange(msg, ALL)
        last = turn + 1 == ITERS
        direction, applied, norms, msg = run_tile(
            last, ids, hot, tiles, scale, got, direction, norms
        )
        kept.append((direction, applied, norms))
        got = exchange(msg, ALL)
        if not last:
            residual, msg = run_owner(got, direction, norms, residual, inverse)
            curves.append(residual)
    (d0, u0, n0), (d1, u1, n1), (d2, u2, n2) = kept
    return run_final(
        col_counts, got, curves[0], curves[1], d0, d1, d2, u0, u1, u2, n0, n1, n2, mu, primal,
        slack, scale, dual_res,
    )


def solution(mesh):
    fine = Mesh(mesh.devices.reshape(4, 4, 2, 4), ("x", "z", "core", "leg"))
    every = ("x", "z", "core", "leg")
    return jax.shard_map(
        per_device,
        mesh=fine,
        in_specs=(
            P(every, None, None, None),
            P(every, None),
            P(every),
            P(every, None),
            P(every, None),
            P(every, None),
            P("leg", None),
            P("leg", None),
        ),
        out_specs=(P("leg", None), P(every, None)),
        check_vma=False,
    )
```

```python
import jax
import jax.numpy as jnp
from jax import lax
from jax.experimental import pallas as pl
from jax.experimental.pallas import tpu as pltpu
from jax.sharding import Mesh, PartitionSpec as P

ITERS = 3
SIGMA = 0.3
REGULAR = 1.0
PRECISE = lax.Precision.HIGHEST

N = 128
HALF = 64
SPAN = 4
GROUPS = 16
TILES = GROUPS * SPAN
EXTRA = 4
ROWS = HALF + EXTRA

VMEM = pltpu.MemorySpace.VMEM
SMEM = pltpu.MemorySpace.SMEM
HBM = pltpu.MemorySpace.HBM
NT = (((1,), (1,)), ((), ()))


def iota(shape, axis):
    return lax.broadcasted_iota(jnp.int32, shape, axis)


def vspec():
    return pl.BlockSpec(memory_space=VMEM)


def sspec():
    return pl.BlockSpec(memory_space=SMEM)


def f32(*shape):
    return jax.ShapeDtypeStruct(shape, jnp.float32)


def device_col():
    return (lax.axis_index("x") * 2 + lax.axis_index("core")) * 4 + lax.axis_index("z")


def params():
    return pltpu.CompilerParams(vmem_limit_bytes=24 << 20)


def split(x):
    high = x.astype(jnp.bfloat16)
    return high, (x - high.astype(jnp.float32)).astype(jnp.bfloat16)


def gram_product(high, low):
    both = jnp.concatenate([high, low], axis=0)
    full = lax.dot_general(both, both, NT, preferred_element_type=jnp.float32)
    return (full[:N, :N] + full[N:, N:]) + (full[:N, N:] + full[N:, :N])


def gram_kernel(
    coeffs_in, ids_in, counts_in, primal_in, slack_in, tiles, acc, other, small, root_out,
    hot_ids, hot_place, coeffs, ids, counts, primal, slack, hot, hot2, sem, tile_sem,
):
    little = [
        pltpu.make_async_copy(ids_in, ids, sem.at[0]),
        pltpu.make_async_copy(counts_in, counts, sem.at[1]),
        pltpu.make_async_copy(primal_in, primal, sem.at[2]),
        pltpu.make_async_copy(slack_in, slack, sem.at[3]),
    ]
    big = [pltpu.make_async_copy(coeffs_in.at[g], coeffs.at[g], tile_sem.at[g]) for g in range(GROUPS)]
    for copy in little + big:
        copy.start()
    acc[...] = jnp.zeros_like(acc)
    small[...] = jnp.zeros_like(small)
    hot[...] = jnp.zeros_like(hot)
    hot2[...] = jnp.zeros_like(hot2)
    core = lax.axis_index("core")
    for copy in little:
        copy.wait()
    row = iota((HALF, N), 0)
    lane = iota((HALF, N), 1)
    line_lane = iota((1, N), 1)
    lower = jnp.logical_or(row >= lane, lane >= HALF)
    for g in range(GROUPS):
        scale = jnp.where(line_lane < counts[g], primal[g : g + 1, :] / slack[g : g + 1, :], 0.0)
        root_out[g : g + 1, :] = jnp.sqrt(scale)
    for g in range(GROUPS):
        big[g].wait()
        root = root_out[g : g + 1, :]
        for s in range(SPAN):
            high, low = split(coeffs[g, s] * root)
            tiles[g, s * N : (s + 1) * N, :] = jnp.concatenate([high, low], axis=1)
            gram = gram_product(high, low)
            rolled = pltpu.roll(gram[HALF:], HALF, 1)
            packed = jnp.where(lower, gram[:HALF], rolled)
            line = jnp.sum(jnp.where(row == lane, rolled, 0.0), axis=0, keepdims=True)
            block = ids[s, g]
            chip = ((block >> 3) << 2) | (block & 3)
            place = (((block >> 2) & 1) ^ core) * HALF + chip
            acc[place] += packed
            small[pl.ds(place * EXTRA, 1), :] += line
            t = g * SPAN + s
            hot[t : t + 1, :] = (line_lane == block).astype(jnp.float32)
            hot2[t : t + 1, :] = (line_lane == place).astype(jnp.float32)
    other[...] = acc[pl.ds(HALF, HALF)]
    hot_ids[...] = jnp.transpose(hot[...]).astype(jnp.bfloat16)
    hot_place[...] = jnp.transpose(hot2[...]).astype(jnp.bfloat16)


def run_gram(coeffs, ids, counts, primal, slack):
    return pl.pallas_call(
        gram_kernel,
        out_shape=(
            jax.ShapeDtypeStruct((GROUPS, SPAN * N, 2 * N), jnp.bfloat16),
            f32(N, HALF, N),
            f32(HALF, HALF, N),
            f32(N * EXTRA, N),
            f32(GROUPS, N),
            jax.ShapeDtypeStruct((N, N), jnp.bfloat16),
            jax.ShapeDtypeStruct((N, N), jnp.bfloat16),
        ),
        in_specs=[pl.BlockSpec(memory_space=HBM)] * 5,
        out_specs=(vspec(),) * 7,
        scratch_shapes=[
            pltpu.VMEM((GROUPS, SPAN, N, N), jnp.float32),
            pltpu.SMEM((SPAN, GROUPS), jnp.int32),
            pltpu.SMEM((GROUPS,), jnp.int32),
            pltpu.VMEM((GROUPS, N), jnp.float32),
            pltpu.VMEM((GROUPS, N), jnp.float32),
            pltpu.VMEM((N, N), jnp.float32),
            pltpu.VMEM((N, N), jnp.float32),
            pltpu.SemaphoreType.DMA((4,)),
            pltpu.SemaphoreType.DMA((GROUPS,)),
        ],
        compiler_params=params(),
        cost_estimate=pl.CostEstimate(
            flops=TILES * 2 * N**3 * 4, bytes_accessed=12 << 20, transcendentals=0
        ),
        name="gram",
    )(*(pltpu.with_memory_space_constraint(x, HBM) for x in (coeffs, ids, counts, primal, slack)))


def transpose_apply(ids, tiles, vector, spread, out):
    for t in range(TILES):
        spread[t : t + 1, :] = vector[pl.ds(ids[t % SPAN, t // SPAN], 1), :]
    high, low = split(spread[...])
    for g in range(GROUPS):
        parts = []
        for rows in (high, low):
            own = [rows[g * SPAN + s : g * SPAN + s + 1] for s in range(SPAN)]
            parts.append(jnp.concatenate(own, axis=1))
        both = jnp.concatenate(parts, axis=0)
        full = jnp.dot(both, tiles[g], preferred_element_type=jnp.float32)
        out[g : g + 1, :] = (full[0:1, :N] + full[1:2, N:]) + (full[0:1, N:] + full[1:2, :N])


def forward_apply(tiles, colvecs, outs):
    lines = []
    for w in colvecs:
        high, low = split(w)
        lines.append(jnp.concatenate([high, high], axis=1))
        lines.append(jnp.concatenate([low, jnp.zeros_like(low)], axis=1))
    for g in range(GROUPS):
        both = jnp.concatenate([line[g : g + 1] for line in lines], axis=0)
        full = lax.dot_general(both, tiles[g], NT, preferred_element_type=jnp.float32)
        for k, out in enumerate(outs):
            total = full[2 * k : 2 * k + 1] + full[2 * k + 1 : 2 * k + 2]
            for s in range(SPAN):
                t = g * SPAN + s
                out[t : t + 1, :] = total[:, s * N : (s + 1) * N]


def place_rows(hot, rows):
    rows = jnp.concatenate([rows, jnp.zeros((N - TILES, N), jnp.float32)], axis=0)
    high = rows.astype(jnp.bfloat16)
    middle, low = split(rows - high.astype(jnp.float32))
    total = jnp.dot(hot, high, preferred_element_type=jnp.float32)
    total = total + jnp.dot(hot, middle, preferred_element_type=jnp.float32)
    return total + jnp.dot(hot, low, preferred_element_type=jnp.float32)


def rhs_kernel(
    ids, counts, hot_place, tiles, dual0, dual1, dual2, dual3, primal, slack, cost, root, small,
    own_out, other_out, base_out, scale_out, spread, spread2, duals, valid_s, applied,
):
    leg = lax.axis_index("leg")
    for k, part in enumerate((dual0, dual1, dual2, dual3)):
        at = pl.multiple_of(((leg - k) & 3) * 32, 32)
        duals[pl.ds(at, 32), :] = part[...]
    for g in range(GROUPS):
        valid_s[g : g + 1, :] = (iota((1, N), 1) < counts[g]).astype(jnp.float32)
    valid = valid_s[...]
    used = valid > 0.0
    transpose_apply(ids, tiles, duals, spread, applied)
    dual_res = cost[...] - applied[...] / jnp.where(used, root[...], 1.0) - slack[...]
    weighted = root[...] * dual_res
    ratio = valid / slack[...]
    base_out[...] = -(root[...] * weighted) - valid * primal[...]
    scale_out[...] = ratio
    product = primal[...] * slack[...]
    forward_apply(tiles, (weighted, valid / jnp.sqrt(product)), (spread, spread2))
    first = place_rows(hot_place[...], spread[...])
    second = place_rows(hot_place[...], spread2[...])
    comp = jnp.sum(valid * product, axis=0, keepdims=True)
    count = jnp.sum(jnp.sum(valid, axis=0, keepdims=True), axis=1, keepdims=True)
    for k, out in enumerate((own_out, other_out)):
        half = slice(k * HALF, k * HALF + HALF)
        diag = small[pl.ds(k * HALF * EXTRA, HALF, stride=EXTRA), :]
        diag = jnp.where(iota((HALF, N), 1) < HALF, diag, jnp.broadcast_to(count, (HALF, N)))
        out[pl.ds(0, HALF, stride=EXTRA), :] = diag
        out[pl.ds(1, HALF, stride=EXTRA), :] = first[half]
        out[pl.ds(2, HALF, stride=EXTRA), :] = second[half]
        out[pl.ds(3, HALF, stride=EXTRA), :] = jnp.broadcast_to(comp, (HALF, N))


def run_rhs(ids, counts, hot_place, tiles, duals, primal, slack, cost, root, small):
    return pl.pallas_call(
        rhs_kernel,
        out_shape=(f32(HALF * EXTRA, N), f32(HALF * EXTRA, N), f32(GROUPS, N), f32(GROUPS, N)),
        in_specs=[sspec(), sspec()] + [vspec()] * 11,
        out_specs=(vspec(),) * 4,
        scratch_shapes=[
            pltpu.VMEM((TILES, N), jnp.float32),
            pltpu.VMEM((TILES, N), jnp.float32),
            pltpu.VMEM((N, N), jnp.float32),
            pltpu.VMEM((GROUPS, N), jnp.float32),
            pltpu.VMEM((GROUPS, N), jnp.float32),
        ],
        compiler_params=params(),
        cost_estimate=pl.CostEstimate(flops=1 << 27, bytes_accessed=6 << 20, transcendentals=0),
        name="rhs",
    )(ids, counts, hot_place, tiles, *duals, primal, slack, cost, root, small)


def join_kernel(acc, got, small, small_got, out):
    for p in range(HALF // 2):
        at = 2 * ROWS * p
        out[at : at + HALF, :] = acc[2 * p] + got[2 * p]
        extra = slice(2 * EXTRA * p, 2 * EXTRA * (p + 1))
        out[at + HALF : at + HALF + 2 * EXTRA, :] = small[extra, :] + small_got[extra, :]
        out[at + HALF + 2 * EXTRA : at + 2 * ROWS, :] = acc[2 * p + 1] + got[2 * p + 1]


def run_join(acc, got, small, small_got):
    return pl.pallas_call(
        join_kernel,
        out_shape=f32(HALF * ROWS, N),
        in_specs=[vspec()] * 4,
        out_specs=vspec(),
        compiler_params=params(),
        name="join",
    )(acc, got, small, small_got)


def small_inverse(cols):
    cols = list(cols)
    sub = iota((8, N), 0)
    for m in range(8):
        rows = [jnp.broadcast_to(c[m : m + 1, :], (8, N)) for c in cols]
        inv = 1.0 / rows[m]
        factor = cols[m]
        here = sub == m
        for j in range(8):
            if j == m:
                cols[j] = jnp.where(here, inv, -factor * inv)
            else:
                scaled = rows[j] * inv
                cols[j] = jnp.where(here, scaled, cols[j] - factor * scaled)
    return cols


def invert(panels):
    panels = list(panels)
    lane = iota((8, N), 1)
    count = len(panels)
    for k in range(count):
        mine = jnp.logical_and(lane >= 8 * k, lane < 8 * k + 8)
        pivot = panels[k]
        cols = [jnp.broadcast_to(pivot[:, 8 * k + m : 8 * k + m + 1], (8, N)) for m in range(8)]
        cols = small_inverse(cols)
        total = None
        for m in range(8):
            term = cols[m] * jnp.broadcast_to(pivot[m : m + 1, :], (8, N))
            total = term if total is None else total + term
        for m in range(8):
            total = jnp.where(lane == 8 * k + m, cols[m], total)
        rows = [jnp.broadcast_to(total[m : m + 1, :], (8, N)) for m in range(8)]
        for step in range(1, count):
            i = (k + step) % count
            old = panels[i]
            new = jnp.where(mine, 0.0, old)
            for m in range(8):
                col = jnp.broadcast_to(old[:, 8 * k + m : 8 * k + m + 1], (8, N))
                new = new - col * rows[m]
            panels[i] = new
        panels[k] = total
    return panels


def pair_rows(first, second):
    return jnp.where((iota((8, N), 0) & 1) == 0, first, second)


def set_message(msg, line, scalar):
    pair = pair_rows(jnp.broadcast_to(line, (8, N)), jnp.broadcast_to(scalar, (8, N)))
    msg[...] = jnp.broadcast_to(pair[None], (N // 4, 8, N)).reshape(2 * N, N)


def first_kernel(got, demand, inverse_out, residual_out, mu_out, msg):
    def add(i, carry):
        return carry + got[pl.ds(pl.multiple_of(i * 2 * ROWS, 8), 2 * ROWS), :]

    total = lax.fori_loop(1, HALF // 2, add, got[0 : 2 * ROWS, :], unroll=True)
    total = total[:ROWS] + total[ROWS:]
    odd = (lax.axis_index("z") & 1) == 1
    packed = jnp.where(odd, total[EXTRA:], total[:HALF])
    tail = jnp.where(odd, total[:EXTRA], total[HALF:])
    line = tail[0:1]
    comp = jnp.sum(tail[3:4], axis=1, keepdims=True)
    used = line[:, HALF : HALF + 1]
    mu = SIGMA * (comp / used)
    mu_out[...] = jnp.broadcast_to(mu, (8, N))
    residual = demand[pl.ds(device_col(), 1), :] + tail[1:2] - mu * tail[2:3]
    residual_out[...] = jnp.broadcast_to(residual, (8, N))

    row = iota((HALF, N), 0)
    lane = iota((HALF, N), 1)
    flipped = jnp.transpose(jnp.concatenate([packed, jnp.zeros((HALF, N), jnp.float32)], axis=0))
    flip_top, flip_bottom = flipped[:HALF], flipped[HALF:]
    top = jnp.where(jnp.logical_or(row >= lane, lane >= HALF), packed, flip_top)
    corner = jnp.where(row < lane, packed, flip_top)
    corner = jnp.where(row == lane, jnp.broadcast_to(line, (HALF, N)), corner)
    bottom = jnp.where(lane < HALF, flip_bottom, pltpu.roll(corner, HALF, 1))
    top = top + jnp.where(row == lane, REGULAR, 0.0)
    bottom = bottom + jnp.where(row + HALF == lane, REGULAR, 0.0)
    panels = [top[8 * i : 8 * i + 8] for i in range(8)]
    panels += [bottom[8 * i : 8 * i + 8] for i in range(8)]
    inverse = jnp.concatenate(invert(panels), axis=0)
    inverse_out[...] = inverse
    smoothed = jnp.dot(
        jnp.broadcast_to(residual, (8, N)),
        inverse,
        precision=PRECISE,
        preferred_element_type=jnp.float32,
    )[0:1]
    norm = jnp.sum(residual * smoothed, axis=1, keepdims=True)
    set_message(msg, smoothed, norm)


def run_first(got, demand):
    return pl.pallas_call(
        first_kernel,
        out_shape=(f32(N, N), f32(8, N), f32(8, N), f32(2 * N, N)),
        in_specs=[vspec(), vspec()],
        out_specs=(vspec(),) * 4,
        compiler_params=params(),
        name="first",
    )(got, demand)


def sum_pairs(got):
    total = jnp.sum(got[...].reshape(N // 4, 8, N), axis=0)
    even = (total[0:1] + total[2:3]) + (total[4:5] + total[6:7])
    odd = (total[1:2] + total[3:4]) + (total[5:6] + total[7:8])
    return even, odd


def owner_kernel(got, direction, norms, residual, inverse, residual_out, msg):
    image, curve = sum_pairs(got)
    image = image + REGULAR * direction[pl.ds(lax.axis_index("leg") * 32 + device_col(), 1), :]
    curve = jnp.sum(curve, axis=1, keepdims=True)
    step_len = norms[0:1, :] / (curve + norms[1:2, :])
    new = residual[0:1, :] - step_len * image
    residual_out[...] = pair_rows(jnp.broadcast_to(new, (8, N)), jnp.broadcast_to(curve, (8, N)))
    smoothed = jnp.dot(
        jnp.broadcast_to(new, (8, N)),
        inverse[...],
        precision=PRECISE,
        preferred_element_type=jnp.float32,
    )[0:1]
    set_message(msg, smoothed, jnp.sum(new * smoothed, axis=1, keepdims=True))


def run_owner(got, direction, norms, residual, inverse):
    return pl.pallas_call(
        owner_kernel,
        out_shape=(f32(8, N), f32(2 * N, N)),
        in_specs=[vspec()] * 5,
        out_specs=(vspec(),) * 2,
        compiler_params=params(),
        name="owner",
    )(got, direction, norms, residual, inverse)


def tile_kernel(last, begin, ids, hot, tiles, got, *refs):
    if begin:
        direction_out, applied_out, norms_out, msg, spread = refs
    else:
        direction_in, norms_in, direction_out, applied_out, norms_out, msg, spread = refs
    smoothed = got[pl.ds(0, N, stride=2), :]
    norm = jnp.sum(got[pl.ds(1, N, stride=2), :], axis=0, keepdims=True)
    if begin:
        direction = smoothed
    else:
        direction = smoothed + (norm / norms_in[0:1, :]) * direction_in[...]
    direction_out[...] = direction
    transpose_apply(ids, tiles, direction_out, spread, applied_out)
    square = jnp.sum(jnp.sum(direction * direction, axis=0, keepdims=True), axis=1, keepdims=True)
    norms_out[0:1, :] = norm
    norms_out[1:2, :] = jnp.broadcast_to(REGULAR * square, (1, N))
    applied = applied_out[...]
    curve = jnp.sum(applied * applied, axis=0, keepdims=True)
    if last:
        msg[...] = jnp.broadcast_to(curve, (N, N))
    else:
        forward_apply(tiles, (applied,), (spread,))
        msg[pl.ds(0, N, stride=2), :] = place_rows(hot[...], spread[...])
        msg[pl.ds(1, N, stride=2), :] = jnp.broadcast_to(curve, (N, N))


def run_tile(last, ids, hot, tiles, got, direction=None, norms=None):
    begin = direction is None
    extra = () if begin else (direction, norms)

    def kernel(*refs):
        tile_kernel(last, begin, *refs)

    return pl.pallas_call(
        kernel,
        out_shape=(f32(N, N), f32(GROUPS, N), f32(8, N), f32(N if last else 2 * N, N)),
        in_specs=[sspec()] + [vspec()] * (3 + len(extra)),
        out_specs=(vspec(),) * 4,
        scratch_shapes=[pltpu.VMEM((TILES, N), jnp.float32)],
        compiler_params=params(),
        name="tile_last" if last else "tile",
    )(ids, hot, tiles, got, *extra)


def final_kernel(
    got, curve0, curve1, d0, d1, d2, u0, u1, u2, n0, n1, n2, mu, root, base, ratio, step_dual,
    step_primal,
):
    curve2 = jnp.sum(jnp.sum(got[...], axis=0, keepdims=True), axis=1, keepdims=True)
    lens = []
    for curve, norms in ((curve0[1:2, :], n0), (curve1[1:2, :], n1), (curve2, n2)):
        lens.append(norms[0:1, :] / (curve + norms[1:2, :]))
    at = pl.ds(pl.multiple_of(lax.axis_index("leg") * 32, 32), 32)
    step_dual[...] = lens[0] * d0[at, :] + lens[1] * d1[at, :] + lens[2] * d2[at, :]
    applied = lens[0] * u0[...] + lens[1] * u1[...] + lens[2] * u2[...]
    step_primal[...] = root[...] * applied + (mu[0:1, :] * ratio[...] + base[...])


def run_final(*args):
    return pl.pallas_call(
        final_kernel,
        out_shape=(f32(32, N), f32(GROUPS, N)),
        in_specs=[vspec()] * len(args),
        out_specs=(vspec(), vspec()),
        compiler_params=params(),
        name="final",
    )(*args)


ALL = ("leg", "x", "core", "z")
CHIPS = ("leg", "x", "z")


def exchange(rows, axes):
    return lax.all_to_all(rows, axes, split_axis=0, concat_axis=0, tiled=True)


def per_device(coeffs, block_ids, col_counts, primal, slack, cost, duals, demand):
    ids = block_ids.T
    parts = [duals]
    for k in (1, 2, 3):
        parts.append(lax.ppermute(duals, "leg", [(i, (i + k) % 4) for i in range(4)]))

    tiles, acc, other, small, root, hot, hot_place = run_gram(
        coeffs, ids, col_counts, primal, slack
    )
    swap = [(0, 1), (1, 0)]
    other, *parts = lax.optimization_barrier((other, *parts))
    got_big = lax.ppermute(other, "core", swap)
    small, small_other, base, ratio = run_rhs(
        ids, col_counts, hot_place, tiles, parts, primal, slack, cost, root, small
    )
    got_small = lax.ppermute(small_other, "core", swap)
    joined = run_join(acc, got_big, small, got_small)
    blocks = exchange(joined.reshape(HALF * ROWS // 4, 4, N), CHIPS).reshape(HALF * ROWS, N)
    inverse, residual, mu, msg = run_first(blocks, demand)

    direction = norms = None
    kept = []
    curves = []
    for turn in range(ITERS):
        got = exchange(msg, ALL)
        last = turn + 1 == ITERS
        direction, applied, norms, msg = run_tile(last, ids, hot, tiles, got, direction, norms)
        kept.append((direction, applied, norms))
        got = exchange(msg, ALL)
        if not last:
            residual, msg = run_owner(got, direction, norms, residual, inverse)
            curves.append(residual)
    (d0, u0, n0), (d1, u1, n1), (d2, u2, n2) = kept
    return run_final(
        got, curves[0], curves[1], d0, d1, d2, u0, u1, u2, n0, n1, n2, mu, root, base, ratio
    )


def solution(mesh):
    fine = Mesh(mesh.devices.reshape(4, 4, 2, 4), ("x", "z", "core", "leg"))
    every = ("x", "z", "core", "leg")
    return jax.shard_map(
        per_device,
        mesh=fine,
        in_specs=(
            P(every, None, None, None),
            P(every, None),
            P(every),
            P(every, None),
            P(every, None),
            P(every, None),
            P("leg", None),
            P("leg", None),
        ),
        out_specs=(P("leg", None), P(every, None)),
        check_vma=False,
    )
```

```python
import jax
import jax.numpy as jnp
from jax import lax
from jax.experimental import pallas as pl
from jax.experimental.pallas import tpu as pltpu
from jax.sharding import Mesh, PartitionSpec as P

ITERS = 3
SIGMA = 0.3
REGULAR = 1.0
PRECISE = lax.Precision.HIGHEST

N = 128
HALF = 64
SPAN = 4
GROUPS = 16
TILES = GROUPS * SPAN
EXTRA = 4
ROWS = HALF + EXTRA

VMEM = pltpu.MemorySpace.VMEM
SMEM = pltpu.MemorySpace.SMEM
HBM = pltpu.MemorySpace.HBM
NT = (((1,), (1,)), ((), ()))


def iota(shape, axis):
    return lax.broadcasted_iota(jnp.int32, shape, axis)


def vspec():
    return pl.BlockSpec(memory_space=VMEM)


def sspec():
    return pl.BlockSpec(memory_space=SMEM)


def f32(*shape):
    return jax.ShapeDtypeStruct(shape, jnp.float32)


def device_col():
    return (lax.axis_index("x") * 2 + lax.axis_index("core")) * 4 + lax.axis_index("z")


def params():
    return pltpu.CompilerParams(vmem_limit_bytes=24 << 20)


def split(x):
    high = x.astype(jnp.bfloat16)
    return high, (x - high.astype(jnp.float32)).astype(jnp.bfloat16)


def gram_product(high, low):
    both = jnp.concatenate([high, low], axis=0)
    full = lax.dot_general(both, both, NT, preferred_element_type=jnp.float32)
    return (full[:N, :N] + full[N:, N:]) + (full[:N, N:] + full[N:, :N])


CHUNKS = (0, 2, 6)


def gram_kernel(
    coeffs_in, ids_in, counts_in, primal_in, slack_in, tiles, acc, other, small, root_out,
    hot_ids, hot_place, coeffs, ids, counts, primal, slack, hot, hot2, sem, tile_sem,
):
    little = [
        pltpu.make_async_copy(ids_in, ids, sem.at[0]),
        pltpu.make_async_copy(counts_in, counts, sem.at[1]),
        pltpu.make_async_copy(primal_in, primal, sem.at[2]),
        pltpu.make_async_copy(slack_in, slack, sem.at[3]),
    ]
    big = {}
    for k, g in enumerate(CHUNKS):
        part = pl.ds(g, (CHUNKS + (GROUPS,))[k + 1] - g)
        big[g] = pltpu.make_async_copy(coeffs_in.at[part], coeffs.at[part], tile_sem.at[k])
    for copy in little + list(big.values()):
        copy.start()
    acc[...] = jnp.zeros_like(acc)
    small[...] = jnp.zeros_like(small)
    hot[...] = jnp.zeros_like(hot)
    hot2[...] = jnp.zeros_like(hot2)
    core = lax.axis_index("core")
    for copy in little:
        copy.wait()
    row = iota((HALF, N), 0)
    lane = iota((HALF, N), 1)
    line_lane = iota((1, N), 1)
    lower = jnp.logical_or(row >= lane, lane >= HALF)
    for g in range(GROUPS):
        scale = jnp.where(line_lane < counts[g], primal[g : g + 1, :] / slack[g : g + 1, :], 0.0)
        root_out[g : g + 1, :] = jnp.sqrt(scale)
    for g in range(GROUPS):
        if g in big:
            big[g].wait()
        root = root_out[g : g + 1, :]
        for s in range(SPAN):
            high, low = split(coeffs[g, s] * root)
            tiles[g, s * N : (s + 1) * N, :] = jnp.concatenate([high, low], axis=1)
            gram = gram_product(high, low)
            rolled = pltpu.roll(gram[HALF:], HALF, 1)
            packed = jnp.where(lower, gram[:HALF], rolled)
            line = jnp.sum(jnp.where(row == lane, rolled, 0.0), axis=0, keepdims=True)
            block = ids[s, g]
            chip = (((block >> 3) & 3) << 4) | ((block & 3) << 2) | (block >> 5)
            place = (((block >> 2) & 1) ^ core) * HALF + chip
            acc[place] += packed
            small[pl.ds(place * EXTRA, 1), :] += line
            t = g * SPAN + s
            hot[t : t + 1, :] = (line_lane == block).astype(jnp.float32)
            hot2[t : t + 1, :] = (line_lane == place).astype(jnp.float32)
    other[...] = acc[pl.ds(HALF, HALF)]
    hot_ids[...] = jnp.transpose(hot[...]).astype(jnp.bfloat16)
    hot_place[...] = jnp.transpose(hot2[...]).astype(jnp.bfloat16)


def run_gram(coeffs, ids, counts, primal, slack):
    return pl.pallas_call(
        gram_kernel,
        out_shape=(
            jax.ShapeDtypeStruct((GROUPS, SPAN * N, 2 * N), jnp.bfloat16),
            f32(N, HALF, N),
            f32(HALF, HALF, N),
            f32(N * EXTRA, N),
            f32(GROUPS, N),
            jax.ShapeDtypeStruct((N, N), jnp.bfloat16),
            jax.ShapeDtypeStruct((N, N), jnp.bfloat16),
        ),
        in_specs=[pl.BlockSpec(memory_space=HBM)] * 5,
        out_specs=(vspec(),) * 7,
        scratch_shapes=[
            pltpu.VMEM((GROUPS, SPAN, N, N), jnp.float32),
            pltpu.SMEM((SPAN, GROUPS), jnp.int32),
            pltpu.SMEM((GROUPS,), jnp.int32),
            pltpu.VMEM((GROUPS, N), jnp.float32),
            pltpu.VMEM((GROUPS, N), jnp.float32),
            pltpu.VMEM((N, N), jnp.float32),
            pltpu.VMEM((N, N), jnp.float32),
            pltpu.SemaphoreType.DMA((4,)),
            pltpu.SemaphoreType.DMA((GROUPS,)),
        ],
        compiler_params=params(),
        cost_estimate=pl.CostEstimate(
            flops=TILES * 2 * N**3 * 4, bytes_accessed=12 << 20, transcendentals=0
        ),
        name="gram",
    )(*(pltpu.with_memory_space_constraint(x, HBM) for x in (coeffs, ids, counts, primal, slack)))


def transpose_apply(ids, tiles, vector, spread, out):
    for t in range(TILES):
        spread[t : t + 1, :] = vector[pl.ds(ids[t % SPAN, t // SPAN], 1), :]
    high, low = split(spread[...])
    for g in range(GROUPS):
        parts = []
        for rows in (high, low):
            own = [rows[g * SPAN + s : g * SPAN + s + 1] for s in range(SPAN)]
            parts.append(jnp.concatenate(own, axis=1))
        both = jnp.concatenate(parts, axis=0)
        full = jnp.dot(both, tiles[g], preferred_element_type=jnp.float32)
        out[g : g + 1, :] = (full[0:1, :N] + full[1:2, N:]) + (full[0:1, N:] + full[1:2, :N])


def forward_apply(tiles, colvecs, outs):
    lines = []
    for w in colvecs:
        high, low = split(w)
        lines.append(jnp.concatenate([high, high], axis=1))
        lines.append(jnp.concatenate([low, jnp.zeros_like(low)], axis=1))
    for g in range(GROUPS):
        both = jnp.concatenate([line[g : g + 1] for line in lines], axis=0)
        full = lax.dot_general(both, tiles[g], NT, preferred_element_type=jnp.float32)
        for k, out in enumerate(outs):
            total = full[2 * k : 2 * k + 1] + full[2 * k + 1 : 2 * k + 2]
            for s in range(SPAN):
                t = g * SPAN + s
                out[t : t + 1, :] = total[:, s * N : (s + 1) * N]


def place_rows(hot, rows):
    rows = jnp.concatenate([rows, jnp.zeros((N - TILES, N), jnp.float32)], axis=0)
    high = rows.astype(jnp.bfloat16)
    middle, low = split(rows - high.astype(jnp.float32))
    total = jnp.dot(hot, high, preferred_element_type=jnp.float32)
    total = total + jnp.dot(hot, middle, preferred_element_type=jnp.float32)
    return total + jnp.dot(hot, low, preferred_element_type=jnp.float32)


def rhs_kernel(
    ids, counts, hot_place, tiles, dual0, dual1, dual2, dual3, primal, slack, cost, root, small,
    own_out, other_out, base_out, scale_out, spread, spread2, duals, valid_s, applied,
):
    leg = lax.axis_index("leg")
    for k, part in enumerate((dual0, dual1, dual2, dual3)):
        at = pl.multiple_of(((leg - k) & 3) * 32, 32)
        duals[pl.ds(at, 32), :] = part[...]
    for g in range(GROUPS):
        valid_s[g : g + 1, :] = (iota((1, N), 1) < counts[g]).astype(jnp.float32)
    valid = valid_s[...]
    used = valid > 0.0
    transpose_apply(ids, tiles, duals, spread, applied)
    dual_res = cost[...] - applied[...] / jnp.where(used, root[...], 1.0) - slack[...]
    weighted = root[...] * dual_res
    ratio = valid / slack[...]
    base_out[...] = -(root[...] * weighted) - valid * primal[...]
    scale_out[...] = ratio
    product = primal[...] * slack[...]
    forward_apply(tiles, (weighted, valid / jnp.sqrt(product)), (spread, spread2))
    first = place_rows(hot_place[...], spread[...])
    second = place_rows(hot_place[...], spread2[...])
    comp = jnp.sum(valid * product, axis=0, keepdims=True)
    count = jnp.sum(jnp.sum(valid, axis=0, keepdims=True), axis=1, keepdims=True)
    for k, out in enumerate((own_out, other_out)):
        half = slice(k * HALF, k * HALF + HALF)
        diag = small[pl.ds(k * HALF * EXTRA, HALF, stride=EXTRA), :]
        diag = jnp.where(iota((HALF, N), 1) < HALF, diag, jnp.broadcast_to(count, (HALF, N)))
        out[pl.ds(0, HALF, stride=EXTRA), :] = diag
        out[pl.ds(1, HALF, stride=EXTRA), :] = first[half]
        out[pl.ds(2, HALF, stride=EXTRA), :] = second[half]
        out[pl.ds(3, HALF, stride=EXTRA), :] = jnp.broadcast_to(comp, (HALF, N))


def run_rhs(ids, counts, hot_place, tiles, duals, primal, slack, cost, root, small):
    return pl.pallas_call(
        rhs_kernel,
        out_shape=(f32(HALF * EXTRA, N), f32(HALF * EXTRA, N), f32(GROUPS, N), f32(GROUPS, N)),
        in_specs=[sspec(), sspec()] + [vspec()] * 11,
        out_specs=(vspec(),) * 4,
        scratch_shapes=[
            pltpu.VMEM((TILES, N), jnp.float32),
            pltpu.VMEM((TILES, N), jnp.float32),
            pltpu.VMEM((N, N), jnp.float32),
            pltpu.VMEM((GROUPS, N), jnp.float32),
            pltpu.VMEM((GROUPS, N), jnp.float32),
        ],
        compiler_params=params(),
        cost_estimate=pl.CostEstimate(flops=1 << 27, bytes_accessed=6 << 20, transcendentals=0),
        name="rhs",
    )(ids, counts, hot_place, tiles, *duals, primal, slack, cost, root, small)


def join_kernel(acc, got, small, small_got, out):
    for p in range(HALF // 2):
        at = 2 * ROWS * p
        out[at : at + HALF, :] = acc[2 * p] + got[2 * p]
        extra = slice(2 * EXTRA * p, 2 * EXTRA * (p + 1))
        out[at + HALF : at + HALF + 2 * EXTRA, :] = small[extra, :] + small_got[extra, :]
        out[at + HALF + 2 * EXTRA : at + 2 * ROWS, :] = acc[2 * p + 1] + got[2 * p + 1]


def run_join(acc, got, small, small_got):
    return pl.pallas_call(
        join_kernel,
        out_shape=f32(HALF * ROWS, N),
        in_specs=[vspec()] * 4,
        out_specs=vspec(),
        compiler_params=params(),
        name="join",
    )(acc, got, small, small_got)


def small_inverse(cols):
    cols = list(cols)
    sub = iota((8, N), 0)
    for m in range(8):
        rows = [jnp.broadcast_to(c[m : m + 1, :], (8, N)) for c in cols]
        inv = 1.0 / rows[m]
        factor = cols[m]
        here = sub == m
        for j in range(8):
            if j == m:
                cols[j] = jnp.where(here, inv, -factor * inv)
            else:
                scaled = rows[j] * inv
                cols[j] = jnp.where(here, scaled, cols[j] - factor * scaled)
    return cols


def invert(panels):
    panels = list(panels)
    lane = iota((8, N), 1)
    count = len(panels)
    for k in range(count):
        mine = jnp.logical_and(lane >= 8 * k, lane < 8 * k + 8)
        pivot = panels[k]
        cols = [jnp.broadcast_to(pivot[:, 8 * k + m : 8 * k + m + 1], (8, N)) for m in range(8)]
        cols = small_inverse(cols)
        total = None
        for m in range(8):
            term = cols[m] * jnp.broadcast_to(pivot[m : m + 1, :], (8, N))
            total = term if total is None else total + term
        for m in range(8):
            total = jnp.where(lane == 8 * k + m, cols[m], total)
        rows = [jnp.broadcast_to(total[m : m + 1, :], (8, N)) for m in range(8)]
        for step in range(1, count):
            i = (k + step) % count
            old = panels[i]
            new = jnp.where(mine, 0.0, old)
            for m in range(8):
                col = jnp.broadcast_to(old[:, 8 * k + m : 8 * k + m + 1], (8, N))
                new = new - col * rows[m]
            panels[i] = new
        panels[k] = total
    return panels


def pair_rows(first, second):
    return jnp.where((iota((8, N), 0) & 1) == 0, first, second)


def set_message(msg, line, scalar):
    pair = pair_rows(jnp.broadcast_to(line, (8, N)), jnp.broadcast_to(scalar, (8, N)))
    msg[...] = jnp.broadcast_to(pair[None], (N // 4, 8, N)).reshape(2 * N, N)


def first_kernel(got, demand, inverse_out, residual_out, mu_out, msg):
    def add(i, carry):
        return carry + got[pl.ds(pl.multiple_of(i * 2 * ROWS, 8), 2 * ROWS), :]

    total = lax.fori_loop(1, HALF // 2, add, got[0 : 2 * ROWS, :], unroll=True)
    total = total[:ROWS] + total[ROWS:]
    odd = (lax.axis_index("leg") & 1) == 1
    packed = jnp.where(odd, total[EXTRA:], total[:HALF])
    tail = jnp.where(odd, total[:EXTRA], total[HALF:])
    line = tail[0:1]
    comp = jnp.sum(tail[3:4], axis=1, keepdims=True)
    used = line[:, HALF : HALF + 1]
    mu = SIGMA * (comp / used)
    mu_out[...] = jnp.broadcast_to(mu, (8, N))
    residual = demand[pl.ds(device_col(), 1), :] + tail[1:2] - mu * tail[2:3]
    residual_out[...] = jnp.broadcast_to(residual, (8, N))

    row = iota((HALF, N), 0)
    lane = iota((HALF, N), 1)
    flipped = jnp.transpose(jnp.concatenate([packed, jnp.zeros((HALF, N), jnp.float32)], axis=0))
    flip_top, flip_bottom = flipped[:HALF], flipped[HALF:]
    top = jnp.where(jnp.logical_or(row >= lane, lane >= HALF), packed, flip_top)
    corner = jnp.where(row < lane, packed, flip_top)
    corner = jnp.where(row == lane, jnp.broadcast_to(line, (HALF, N)), corner)
    bottom = jnp.where(lane < HALF, flip_bottom, pltpu.roll(corner, HALF, 1))
    top = top + jnp.where(row == lane, REGULAR, 0.0)
    bottom = bottom + jnp.where(row + HALF == lane, REGULAR, 0.0)
    panels = [top[8 * i : 8 * i + 8] for i in range(8)]
    panels += [bottom[8 * i : 8 * i + 8] for i in range(8)]
    inverse = jnp.concatenate(invert(panels), axis=0)
    inverse_out[...] = inverse
    smoothed = jnp.dot(
        jnp.broadcast_to(residual, (8, N)),
        inverse,
        precision=PRECISE,
        preferred_element_type=jnp.float32,
    )[0:1]
    norm = jnp.sum(residual * smoothed, axis=1, keepdims=True)
    set_message(msg, smoothed, norm)


def run_first(got, demand):
    return pl.pallas_call(
        first_kernel,
        out_shape=(f32(N, N), f32(8, N), f32(8, N), f32(2 * N, N)),
        in_specs=[vspec(), vspec()],
        out_specs=(vspec(),) * 4,
        compiler_params=params(),
        name="first",
    )(got, demand)


def sum_pairs(got):
    total = jnp.sum(got[...].reshape(N // 4, 8, N), axis=0)
    even = (total[0:1] + total[2:3]) + (total[4:5] + total[6:7])
    odd = (total[1:2] + total[3:4]) + (total[5:6] + total[7:8])
    return even, odd


def owner_kernel(got, direction, norms, residual, inverse, residual_out, msg):
    image, curve = sum_pairs(got)
    image = image + REGULAR * direction[pl.ds(lax.axis_index("leg") * 32 + device_col(), 1), :]
    curve = jnp.sum(curve, axis=1, keepdims=True)
    step_len = norms[0:1, :] / (curve + norms[1:2, :])
    new = residual[0:1, :] - step_len * image
    residual_out[...] = pair_rows(jnp.broadcast_to(new, (8, N)), jnp.broadcast_to(curve, (8, N)))
    smoothed = jnp.dot(
        jnp.broadcast_to(new, (8, N)),
        inverse[...],
        precision=PRECISE,
        preferred_element_type=jnp.float32,
    )[0:1]
    set_message(msg, smoothed, jnp.sum(new * smoothed, axis=1, keepdims=True))


def run_owner(got, direction, norms, residual, inverse):
    return pl.pallas_call(
        owner_kernel,
        out_shape=(f32(8, N), f32(2 * N, N)),
        in_specs=[vspec()] * 5,
        out_specs=(vspec(),) * 2,
        compiler_params=params(),
        name="owner",
    )(got, direction, norms, residual, inverse)


def tile_kernel(last, begin, ids, hot, tiles, got, *refs):
    if begin:
        direction_out, applied_out, norms_out, msg, spread = refs
    else:
        direction_in, norms_in, direction_out, applied_out, norms_out, msg, spread = refs
    smoothed = got[pl.ds(0, N, stride=2), :]
    norm = jnp.sum(got[pl.ds(1, N, stride=2), :], axis=0, keepdims=True)
    if begin:
        direction = smoothed
    else:
        direction = smoothed + (norm / norms_in[0:1, :]) * direction_in[...]
    direction_out[...] = direction
    transpose_apply(ids, tiles, direction_out, spread, applied_out)
    square = jnp.sum(jnp.sum(direction * direction, axis=0, keepdims=True), axis=1, keepdims=True)
    norms_out[0:1, :] = norm
    norms_out[1:2, :] = jnp.broadcast_to(REGULAR * square, (1, N))
    applied = applied_out[...]
    curve = jnp.sum(applied * applied, axis=0, keepdims=True)
    if last:
        msg[...] = jnp.broadcast_to(curve, (N, N))
    else:
        forward_apply(tiles, (applied,), (spread,))
        msg[pl.ds(0, N, stride=2), :] = place_rows(hot[...], spread[...])
        msg[pl.ds(1, N, stride=2), :] = jnp.broadcast_to(curve, (N, N))


def run_tile(last, ids, hot, tiles, got, direction=None, norms=None):
    begin = direction is None
    extra = () if begin else (direction, norms)

    def kernel(*refs):
        tile_kernel(last, begin, *refs)

    return pl.pallas_call(
        kernel,
        out_shape=(f32(N, N), f32(GROUPS, N), f32(8, N), f32(N if last else 2 * N, N)),
        in_specs=[sspec()] + [vspec()] * (3 + len(extra)),
        out_specs=(vspec(),) * 4,
        scratch_shapes=[pltpu.VMEM((TILES, N), jnp.float32)],
        compiler_params=params(),
        name="tile_last" if last else "tile",
    )(ids, hot, tiles, got, *extra)


def final_kernel(
    got, curve0, curve1, d0, d1, d2, u0, u1, u2, n0, n1, n2, mu, root, base, ratio, step_dual,
    step_primal,
):
    curve2 = jnp.sum(jnp.sum(got[...], axis=0, keepdims=True), axis=1, keepdims=True)
    lens = []
    for curve, norms in ((curve0[1:2, :], n0), (curve1[1:2, :], n1), (curve2, n2)):
        lens.append(norms[0:1, :] / (curve + norms[1:2, :]))
    at = pl.ds(pl.multiple_of(lax.axis_index("leg") * 32, 32), 32)
    step_dual[...] = lens[0] * d0[at, :] + lens[1] * d1[at, :] + lens[2] * d2[at, :]
    applied = lens[0] * u0[...] + lens[1] * u1[...] + lens[2] * u2[...]
    step_primal[...] = root[...] * applied + (mu[0:1, :] * ratio[...] + base[...])


def run_final(*args):
    return pl.pallas_call(
        final_kernel,
        out_shape=(f32(32, N), f32(GROUPS, N)),
        in_specs=[vspec()] * len(args),
        out_specs=(vspec(), vspec()),
        compiler_params=params(),
        name="final",
    )(*args)


ALL = ("leg", "x", "core", "z")
CHIPS = ("x", "z", "leg")


def exchange(rows, axes):
    return lax.all_to_all(rows, axes, split_axis=0, concat_axis=0, tiled=True)


def per_device(coeffs, block_ids, col_counts, primal, slack, cost, duals, demand):
    ids = block_ids.T
    parts = [duals]
    for k in (1, 2, 3):
        parts.append(lax.ppermute(duals, "leg", [(i, (i + k) % 4) for i in range(4)]))

    tiles, acc, other, small, root, hot, hot_place = run_gram(
        coeffs, ids, col_counts, primal, slack
    )
    swap = [(0, 1), (1, 0)]
    other, *parts = lax.optimization_barrier((other, *parts))
    got_big = lax.ppermute(other, "core", swap)
    small, small_other, base, ratio = run_rhs(
        ids, col_counts, hot_place, tiles, parts, primal, slack, cost, root, small
    )
    got_small = lax.ppermute(small_other, "core", swap)
    joined = run_join(acc, got_big, small, got_small)
    blocks = exchange(joined.reshape(HALF * ROWS // 4, 4, N), CHIPS).reshape(HALF * ROWS, N)
    inverse, residual, mu, msg = run_first(blocks, demand)

    direction = norms = None
    kept = []
    curves = []
    for turn in range(ITERS):
        got = exchange(msg, ALL)
        last = turn + 1 == ITERS
        direction, applied, norms, msg = run_tile(last, ids, hot, tiles, got, direction, norms)
        kept.append((direction, applied, norms))
        got = exchange(msg, ALL)
        if not last:
            residual, msg = run_owner(got, direction, norms, residual, inverse)
            curves.append(residual)
    (d0, u0, n0), (d1, u1, n1), (d2, u2, n2) = kept
    return run_final(
        got, curves[0], curves[1], d0, d1, d2, u0, u1, u2, n0, n1, n2, mu, root, base, ratio
    )


def solution(mesh):
    fine = Mesh(mesh.devices.reshape(4, 4, 2, 4), ("x", "z", "core", "leg"))
    every = ("x", "z", "core", "leg")
    return jax.shard_map(
        per_device,
        mesh=fine,
        in_specs=(
            P(every, None, None, None),
            P(every, None),
            P(every),
            P(every, None),
            P(every, None),
            P(every, None),
            P("leg", None),
            P("leg", None),
        ),
        out_specs=(P("leg", None), P(every, None)),
        check_vma=False,
    )
```

```python
import jax
import jax.numpy as jnp
from jax import lax
from jax.experimental import pallas as pl
from jax.experimental.pallas import tpu as pltpu
from jax.sharding import Mesh, PartitionSpec as P

ITERS = 3
SIGMA = 0.3
REGULAR = 1.0
PRECISE = lax.Precision.HIGHEST

N = 128
HALF = 64
SPAN = 4
GROUPS = 16
TILES = GROUPS * SPAN
EXTRA = 4
ROWS = HALF + EXTRA

VMEM = pltpu.MemorySpace.VMEM
SMEM = pltpu.MemorySpace.SMEM
HBM = pltpu.MemorySpace.HBM
NT = (((1,), (1,)), ((), ()))


def iota(shape, axis):
    return lax.broadcasted_iota(jnp.int32, shape, axis)


def vspec():
    return pl.BlockSpec(memory_space=VMEM)


def sspec():
    return pl.BlockSpec(memory_space=SMEM)


def f32(*shape):
    return jax.ShapeDtypeStruct(shape, jnp.float32)


def device_col():
    return (lax.axis_index("x") * 2 + lax.axis_index("core")) * 4 + lax.axis_index("z")


def params():
    return pltpu.CompilerParams(vmem_limit_bytes=24 << 20)


def split(x):
    high = x.astype(jnp.bfloat16)
    return high, (x - high.astype(jnp.float32)).astype(jnp.bfloat16)


def gram_product(high, low):
    both = jnp.concatenate([high, low], axis=0)
    full = lax.dot_general(both, both, NT, preferred_element_type=jnp.float32)
    return (full[:N, :N] + full[N:, N:]) + (full[:N, N:] + full[N:, :N])


CHUNKS = (0, 2, 6)


def gram_kernel(
    coeffs_in, ids_in, counts_in, primal_in, slack_in, tiles, acc, other, small, root_out,
    hot_ids, hot_place, coeffs, ids, counts, primal, slack, hot, hot2, sem, tile_sem,
):
    little = [
        pltpu.make_async_copy(ids_in, ids, sem.at[0]),
        pltpu.make_async_copy(counts_in, counts, sem.at[1]),
        pltpu.make_async_copy(primal_in, primal, sem.at[2]),
        pltpu.make_async_copy(slack_in, slack, sem.at[3]),
    ]
    big = {}
    for k, g in enumerate(CHUNKS):
        part = pl.ds(g, (CHUNKS + (GROUPS,))[k + 1] - g)
        big[g] = pltpu.make_async_copy(coeffs_in.at[part], coeffs.at[part], tile_sem.at[k])
    for copy in little + list(big.values()):
        copy.start()
    acc[...] = jnp.zeros_like(acc)
    small[...] = jnp.zeros_like(small)
    hot[...] = jnp.zeros_like(hot)
    hot2[...] = jnp.zeros_like(hot2)
    core = lax.axis_index("core")
    for copy in little:
        copy.wait()
    row = iota((HALF, N), 0)
    lane = iota((HALF, N), 1)
    line_lane = iota((1, N), 1)
    lower = jnp.logical_or(row >= lane, lane >= HALF)
    for g in range(GROUPS):
        scale = jnp.where(line_lane < counts[g], primal[g : g + 1, :] / slack[g : g + 1, :], 0.0)
        root_out[g : g + 1, :] = jnp.sqrt(scale)
    for g in range(GROUPS):
        if g in big:
            big[g].wait()
        root = root_out[g : g + 1, :]
        for s in range(SPAN):
            high, low = split(coeffs[g, s] * root)
            tiles[g, s * N : (s + 1) * N, :] = jnp.concatenate([high, low], axis=1)
            gram = gram_product(high, low)
            rolled = pltpu.roll(gram[HALF:], HALF, 1)
            packed = jnp.where(lower, gram[:HALF], rolled)
            line = jnp.sum(jnp.where(row == lane, rolled, 0.0), axis=0, keepdims=True)
            block = ids[s, g]
            chip = (((block >> 3) & 3) << 4) | ((block & 3) << 2) | (block >> 5)
            place = (((block >> 2) & 1) ^ core) * HALF + chip
            acc[place] += packed
            small[pl.ds(place * EXTRA, 1), :] += line
            t = g * SPAN + s
            hot[t : t + 1, :] = (line_lane == block).astype(jnp.float32)
            hot2[t : t + 1, :] = (line_lane == place).astype(jnp.float32)
    other[...] = acc[pl.ds(HALF, HALF)]
    hot_ids[...] = jnp.transpose(hot[...]).astype(jnp.bfloat16)
    hot_place[...] = jnp.transpose(hot2[...]).astype(jnp.bfloat16)


def run_gram(coeffs, ids, counts, primal, slack):
    return pl.pallas_call(
        gram_kernel,
        out_shape=(
            jax.ShapeDtypeStruct((GROUPS, SPAN * N, 2 * N), jnp.bfloat16),
            f32(N, HALF, N),
            f32(HALF, HALF, N),
            f32(N * EXTRA, N),
            f32(GROUPS, N),
            jax.ShapeDtypeStruct((N, N), jnp.bfloat16),
            jax.ShapeDtypeStruct((N, N), jnp.bfloat16),
        ),
        in_specs=[pl.BlockSpec(memory_space=HBM)] * 5,
        out_specs=(vspec(),) * 7,
        scratch_shapes=[
            pltpu.VMEM((GROUPS, SPAN, N, N), jnp.float32),
            pltpu.SMEM((SPAN, GROUPS), jnp.int32),
            pltpu.SMEM((GROUPS,), jnp.int32),
            pltpu.VMEM((GROUPS, N), jnp.float32),
            pltpu.VMEM((GROUPS, N), jnp.float32),
            pltpu.VMEM((N, N), jnp.float32),
            pltpu.VMEM((N, N), jnp.float32),
            pltpu.SemaphoreType.DMA((4,)),
            pltpu.SemaphoreType.DMA((GROUPS,)),
        ],
        compiler_params=params(),
        cost_estimate=pl.CostEstimate(
            flops=TILES * 2 * N**3 * 4, bytes_accessed=12 << 20, transcendentals=0
        ),
        name="gram",
    )(*(pltpu.with_memory_space_constraint(x, HBM) for x in (coeffs, ids, counts, primal, slack)))


def transpose_apply(ids, tiles, vector, spread, out):
    for t in range(TILES):
        spread[t : t + 1, :] = vector[pl.ds(ids[t % SPAN, t // SPAN], 1), :]
    high, low = split(spread[...])
    for g in range(GROUPS):
        parts = []
        for rows in (high, low):
            own = [rows[g * SPAN + s : g * SPAN + s + 1] for s in range(SPAN)]
            parts.append(jnp.concatenate(own, axis=1))
        both = jnp.concatenate(parts, axis=0)
        full = jnp.dot(both, tiles[g], preferred_element_type=jnp.float32)
        out[g : g + 1, :] = (full[0:1, :N] + full[1:2, N:]) + (full[0:1, N:] + full[1:2, :N])


def forward_apply(tiles, colvecs, outs):
    lines = []
    for w in colvecs:
        high, low = split(w)
        lines.append(jnp.concatenate([high, high], axis=1))
        lines.append(jnp.concatenate([low, jnp.zeros_like(low)], axis=1))
    every = len(colvecs) + 1
    for g in range(GROUPS):
        if g % every == every - 1:
            for s in range(SPAN):
                t = g * SPAN + s
                pair = tiles[g, s * N : (s + 1) * N, :].astype(jnp.float32)
                tile = pair[:, :N] + pair[:, N:]
                for w, out in zip(colvecs, outs):
                    turned = jnp.transpose(tile * w[g : g + 1])
                    out[t : t + 1, :] = jnp.sum(turned, axis=0, keepdims=True)
            continue
        both = jnp.concatenate([line[g : g + 1] for line in lines], axis=0)
        full = lax.dot_general(both, tiles[g], NT, preferred_element_type=jnp.float32)
        for k, out in enumerate(outs):
            total = full[2 * k : 2 * k + 1] + full[2 * k + 1 : 2 * k + 2]
            for s in range(SPAN):
                t = g * SPAN + s
                out[t : t + 1, :] = total[:, s * N : (s + 1) * N]


def place_rows(hot, rows):
    rows = jnp.concatenate([rows, jnp.zeros((N - TILES, N), jnp.float32)], axis=0)
    high = rows.astype(jnp.bfloat16)
    middle, low = split(rows - high.astype(jnp.float32))
    total = jnp.dot(hot, high, preferred_element_type=jnp.float32)
    total = total + jnp.dot(hot, middle, preferred_element_type=jnp.float32)
    return total + jnp.dot(hot, low, preferred_element_type=jnp.float32)


def rhs_kernel(
    ids, counts, hot_place, tiles, dual0, dual1, dual2, dual3, primal, slack, cost, root, small,
    own_out, other_out, base_out, scale_out, spread, spread2, duals, valid_s, applied,
):
    leg = lax.axis_index("leg")
    for k, part in enumerate((dual0, dual1, dual2, dual3)):
        at = pl.multiple_of(((leg - k) & 3) * 32, 32)
        duals[pl.ds(at, 32), :] = part[...]
    for g in range(GROUPS):
        valid_s[g : g + 1, :] = (iota((1, N), 1) < counts[g]).astype(jnp.float32)
    valid = valid_s[...]
    used = valid > 0.0
    transpose_apply(ids, tiles, duals, spread, applied)
    dual_res = cost[...] - applied[...] / jnp.where(used, root[...], 1.0) - slack[...]
    weighted = root[...] * dual_res
    ratio = valid / slack[...]
    base_out[...] = -(root[...] * weighted) - valid * primal[...]
    scale_out[...] = ratio
    product = primal[...] * slack[...]
    forward_apply(tiles, (weighted, valid / jnp.sqrt(product)), (spread, spread2))
    first = place_rows(hot_place[...], spread[...])
    second = place_rows(hot_place[...], spread2[...])
    comp = jnp.sum(valid * product, axis=0, keepdims=True)
    count = jnp.sum(jnp.sum(valid, axis=0, keepdims=True), axis=1, keepdims=True)
    for k, out in enumerate((own_out, other_out)):
        half = slice(k * HALF, k * HALF + HALF)
        diag = small[pl.ds(k * HALF * EXTRA, HALF, stride=EXTRA), :]
        diag = jnp.where(iota((HALF, N), 1) < HALF, diag, jnp.broadcast_to(count, (HALF, N)))
        out[pl.ds(0, HALF, stride=EXTRA), :] = diag
        out[pl.ds(1, HALF, stride=EXTRA), :] = first[half]
        out[pl.ds(2, HALF, stride=EXTRA), :] = second[half]
        out[pl.ds(3, HALF, stride=EXTRA), :] = jnp.broadcast_to(comp, (HALF, N))


def run_rhs(ids, counts, hot_place, tiles, duals, primal, slack, cost, root, small):
    return pl.pallas_call(
        rhs_kernel,
        out_shape=(f32(HALF * EXTRA, N), f32(HALF * EXTRA, N), f32(GROUPS, N), f32(GROUPS, N)),
        in_specs=[sspec(), sspec()] + [vspec()] * 11,
        out_specs=(vspec(),) * 4,
        scratch_shapes=[
            pltpu.VMEM((TILES, N), jnp.float32),
            pltpu.VMEM((TILES, N), jnp.float32),
            pltpu.VMEM((N, N), jnp.float32),
            pltpu.VMEM((GROUPS, N), jnp.float32),
            pltpu.VMEM((GROUPS, N), jnp.float32),
        ],
        compiler_params=params(),
        cost_estimate=pl.CostEstimate(flops=1 << 27, bytes_accessed=6 << 20, transcendentals=0),
        name="rhs",
    )(ids, counts, hot_place, tiles, *duals, primal, slack, cost, root, small)


def join_kernel(acc, got, small, small_got, out):
    for p in range(HALF // 2):
        at = 2 * ROWS * p
        out[at : at + HALF, :] = acc[2 * p] + got[2 * p]
        extra = slice(2 * EXTRA * p, 2 * EXTRA * (p + 1))
        out[at + HALF : at + HALF + 2 * EXTRA, :] = small[extra, :] + small_got[extra, :]
        out[at + HALF + 2 * EXTRA : at + 2 * ROWS, :] = acc[2 * p + 1] + got[2 * p + 1]


def run_join(acc, got, small, small_got):
    return pl.pallas_call(
        join_kernel,
        out_shape=f32(HALF * ROWS, N),
        in_specs=[vspec()] * 4,
        out_specs=vspec(),
        compiler_params=params(),
        name="join",
    )(acc, got, small, small_got)


def small_inverse(cols):
    cols = list(cols)
    sub = iota((8, N), 0)
    for m in range(8):
        rows = [jnp.broadcast_to(c[m : m + 1, :], (8, N)) for c in cols]
        inv = 1.0 / rows[m]
        factor = cols[m]
        here = sub == m
        for j in range(8):
            if j == m:
                cols[j] = jnp.where(here, inv, -factor * inv)
            else:
                scaled = rows[j] * inv
                cols[j] = jnp.where(here, scaled, cols[j] - factor * scaled)
    return cols


def invert(panels):
    panels = list(panels)
    lane = iota((8, N), 1)
    count = len(panels)
    for k in range(count):
        mine = jnp.logical_and(lane >= 8 * k, lane < 8 * k + 8)
        pivot = panels[k]
        cols = [jnp.broadcast_to(pivot[:, 8 * k + m : 8 * k + m + 1], (8, N)) for m in range(8)]
        cols = small_inverse(cols)
        total = None
        for m in range(8):
            term = cols[m] * jnp.broadcast_to(pivot[m : m + 1, :], (8, N))
            total = term if total is None else total + term
        for m in range(8):
            total = jnp.where(lane == 8 * k + m, cols[m], total)
        rows = [jnp.broadcast_to(total[m : m + 1, :], (8, N)) for m in range(8)]
        for step in range(1, count):
            i = (k + step) % count
            old = panels[i]
            new = jnp.where(mine, 0.0, old)
            for m in range(8):
                col = jnp.broadcast_to(old[:, 8 * k + m : 8 * k + m + 1], (8, N))
                new = new - col * rows[m]
            panels[i] = new
        panels[k] = total
    return panels


def pair_rows(first, second):
    return jnp.where((iota((8, N), 0) & 1) == 0, first, second)


def set_message(msg, line, scalar):
    pair = pair_rows(jnp.broadcast_to(line, (8, N)), jnp.broadcast_to(scalar, (8, N)))
    msg[...] = jnp.broadcast_to(pair[None], (N // 4, 8, N)).reshape(2 * N, N)


def first_kernel(got, demand, inverse_out, residual_out, mu_out, msg):
    def add(i, carry):
        return carry + got[pl.ds(pl.multiple_of(i * 2 * ROWS, 8), 2 * ROWS), :]

    total = lax.fori_loop(1, HALF // 2, add, got[0 : 2 * ROWS, :], unroll=True)
    total = total[:ROWS] + total[ROWS:]
    odd = (lax.axis_index("leg") & 1) == 1
    packed = jnp.where(odd, total[EXTRA:], total[:HALF])
    tail = jnp.where(odd, total[:EXTRA], total[HALF:])
    line = tail[0:1]
    comp = jnp.sum(tail[3:4], axis=1, keepdims=True)
    used = line[:, HALF : HALF + 1]
    mu = SIGMA * (comp / used)
    mu_out[...] = jnp.broadcast_to(mu, (8, N))
    residual = demand[pl.ds(device_col(), 1), :] + tail[1:2] - mu * tail[2:3]
    residual_out[...] = jnp.broadcast_to(residual, (8, N))

    row = iota((HALF, N), 0)
    lane = iota((HALF, N), 1)
    flipped = jnp.transpose(jnp.concatenate([packed, jnp.zeros((HALF, N), jnp.float32)], axis=0))
    flip_top, flip_bottom = flipped[:HALF], flipped[HALF:]
    top = jnp.where(jnp.logical_or(row >= lane, lane >= HALF), packed, flip_top)
    corner = jnp.where(row < lane, packed, flip_top)
    corner = jnp.where(row == lane, jnp.broadcast_to(line, (HALF, N)), corner)
    bottom = jnp.where(lane < HALF, flip_bottom, pltpu.roll(corner, HALF, 1))
    top = top + jnp.where(row == lane, REGULAR, 0.0)
    bottom = bottom + jnp.where(row + HALF == lane, REGULAR, 0.0)
    panels = [top[8 * i : 8 * i + 8] for i in range(8)]
    panels += [bottom[8 * i : 8 * i + 8] for i in range(8)]
    inverse = jnp.concatenate(invert(panels), axis=0)
    inverse_out[...] = inverse
    smoothed = jnp.dot(
        jnp.broadcast_to(residual, (8, N)),
        inverse,
        precision=PRECISE,
        preferred_element_type=jnp.float32,
    )[0:1]
    norm = jnp.sum(residual * smoothed, axis=1, keepdims=True)
    set_message(msg, smoothed, norm)


def run_first(got, demand):
    return pl.pallas_call(
        first_kernel,
        out_shape=(f32(N, N), f32(8, N), f32(8, N), f32(2 * N, N)),
        in_specs=[vspec(), vspec()],
        out_specs=(vspec(),) * 4,
        compiler_params=params(),
        name="first",
    )(got, demand)


def sum_pairs(got):
    total = jnp.sum(got[...].reshape(N // 4, 8, N), axis=0)
    even = (total[0:1] + total[2:3]) + (total[4:5] + total[6:7])
    odd = (total[1:2] + total[3:4]) + (total[5:6] + total[7:8])
    return even, odd


def owner_kernel(got, direction, norms, residual, inverse, residual_out, msg):
    image, curve = sum_pairs(got)
    image = image + REGULAR * direction[pl.ds(lax.axis_index("leg") * 32 + device_col(), 1), :]
    curve = jnp.sum(curve, axis=1, keepdims=True)
    step_len = norms[0:1, :] / (curve + norms[1:2, :])
    new = residual[0:1, :] - step_len * image
    residual_out[...] = pair_rows(jnp.broadcast_to(new, (8, N)), jnp.broadcast_to(curve, (8, N)))
    smoothed = jnp.dot(
        jnp.broadcast_to(new, (8, N)),
        inverse[...],
        precision=PRECISE,
        preferred_element_type=jnp.float32,
    )[0:1]
    set_message(msg, smoothed, jnp.sum(new * smoothed, axis=1, keepdims=True))


def run_owner(got, direction, norms, residual, inverse):
    return pl.pallas_call(
        owner_kernel,
        out_shape=(f32(8, N), f32(2 * N, N)),
        in_specs=[vspec()] * 5,
        out_specs=(vspec(),) * 2,
        compiler_params=params(),
        name="owner",
    )(got, direction, norms, residual, inverse)


def tile_kernel(last, begin, ids, hot, tiles, got, *refs):
    if begin:
        direction_out, applied_out, norms_out, msg, spread = refs
    else:
        direction_in, norms_in, direction_out, applied_out, norms_out, msg, spread = refs
    smoothed = got[pl.ds(0, N, stride=2), :]
    norm = jnp.sum(got[pl.ds(1, N, stride=2), :], axis=0, keepdims=True)
    if begin:
        direction = smoothed
    else:
        direction = smoothed + (norm / norms_in[0:1, :]) * direction_in[...]
    direction_out[...] = direction
    transpose_apply(ids, tiles, direction_out, spread, applied_out)
    square = jnp.sum(jnp.sum(direction * direction, axis=0, keepdims=True), axis=1, keepdims=True)
    norms_out[0:1, :] = norm
    norms_out[1:2, :] = jnp.broadcast_to(REGULAR * square, (1, N))
    applied = applied_out[...]
    curve = jnp.sum(applied * applied, axis=0, keepdims=True)
    if last:
        msg[...] = jnp.broadcast_to(curve, (N, N))
    else:
        forward_apply(tiles, (applied,), (spread,))
        msg[pl.ds(0, N, stride=2), :] = place_rows(hot[...], spread[...])
        msg[pl.ds(1, N, stride=2), :] = jnp.broadcast_to(curve, (N, N))


def run_tile(last, ids, hot, tiles, got, direction=None, norms=None):
    begin = direction is None
    extra = () if begin else (direction, norms)

    def kernel(*refs):
        tile_kernel(last, begin, *refs)

    return pl.pallas_call(
        kernel,
        out_shape=(f32(N, N), f32(GROUPS, N), f32(8, N), f32(N if last else 2 * N, N)),
        in_specs=[sspec()] + [vspec()] * (3 + len(extra)),
        out_specs=(vspec(),) * 4,
        scratch_shapes=[pltpu.VMEM((TILES, N), jnp.float32)],
        compiler_params=params(),
        name="tile_last" if last else "tile",
    )(ids, hot, tiles, got, *extra)


def final_kernel(
    got, curve0, curve1, d0, d1, d2, u0, u1, u2, n0, n1, n2, mu, root, base, ratio, step_dual,
    step_primal,
):
    curve2 = jnp.sum(jnp.sum(got[...], axis=0, keepdims=True), axis=1, keepdims=True)
    lens = []
    for curve, norms in ((curve0[1:2, :], n0), (curve1[1:2, :], n1), (curve2, n2)):
        lens.append(norms[0:1, :] / (curve + norms[1:2, :]))
    at = pl.ds(pl.multiple_of(lax.axis_index("leg") * 32, 32), 32)
    step_dual[...] = lens[0] * d0[at, :] + lens[1] * d1[at, :] + lens[2] * d2[at, :]
    applied = lens[0] * u0[...] + lens[1] * u1[...] + lens[2] * u2[...]
    step_primal[...] = root[...] * applied + (mu[0:1, :] * ratio[...] + base[...])


def run_final(*args):
    return pl.pallas_call(
        final_kernel,
        out_shape=(f32(32, N), f32(GROUPS, N)),
        in_specs=[vspec()] * len(args),
        out_specs=(vspec(), vspec()),
        compiler_params=params(),
        name="final",
    )(*args)


ALL = ("leg", "x", "core", "z")
CHIPS = ("x", "z", "leg")


def exchange(rows, axes):
    return lax.all_to_all(rows, axes, split_axis=0, concat_axis=0, tiled=True)


def per_device(coeffs, block_ids, col_counts, primal, slack, cost, duals, demand):
    ids = block_ids.T
    parts = [duals]
    for k in (1, 2, 3):
        parts.append(lax.ppermute(duals, "leg", [(i, (i + k) % 4) for i in range(4)]))

    tiles, acc, other, small, root, hot, hot_place = run_gram(
        coeffs, ids, col_counts, primal, slack
    )
    swap = [(0, 1), (1, 0)]
    other, *parts = lax.optimization_barrier((other, *parts))
    got_big = lax.ppermute(other, "core", swap)
    small, small_other, base, ratio = run_rhs(
        ids, col_counts, hot_place, tiles, parts, primal, slack, cost, root, small
    )
    got_small = lax.ppermute(small_other, "core", swap)
    joined = run_join(acc, got_big, small, got_small)
    blocks = exchange(joined.reshape(HALF * ROWS // 4, 4, N), CHIPS).reshape(HALF * ROWS, N)
    inverse, residual, mu, msg = run_first(blocks, demand)

    direction = norms = None
    kept = []
    curves = []
    for turn in range(ITERS):
        got = exchange(msg, ALL)
        last = turn + 1 == ITERS
        direction, applied, norms, msg = run_tile(last, ids, hot, tiles, got, direction, norms)
        kept.append((direction, applied, norms))
        got = exchange(msg, ALL)
        if not last:
            residual, msg = run_owner(got, direction, norms, residual, inverse)
            curves.append(residual)
    (d0, u0, n0), (d1, u1, n1), (d2, u2, n2) = kept
    return run_final(
        got, curves[0], curves[1], d0, d1, d2, u0, u1, u2, n0, n1, n2, mu, root, base, ratio
    )


def solution(mesh):
    fine = Mesh(mesh.devices.reshape(4, 4, 2, 4), ("x", "z", "core", "leg"))
    every = ("x", "z", "core", "leg")
    return jax.shard_map(
        per_device,
        mesh=fine,
        in_specs=(
            P(every, None, None, None),
            P(every, None),
            P(every),
            P(every, None),
            P(every, None),
            P(every, None),
            P("leg", None),
            P("leg", None),
        ),
        out_specs=(P("leg", None), P(every, None)),
        check_vma=False,
    )
```

```python
import jax
import jax.numpy as jnp
from jax import lax
from jax.experimental import pallas as pl
from jax.experimental.pallas import tpu as pltpu
from jax.sharding import Mesh, PartitionSpec as P

SIGMA = 0.3
REGULAR = 1.0
PRECISE = lax.Precision.HIGHEST

N = 128
HALF = 64
SPAN = 4
GROUPS = 16
TILES = GROUPS * SPAN
EXTRA = 4
ROWS = HALF + EXTRA

VMEM = pltpu.MemorySpace.VMEM
SMEM = pltpu.MemorySpace.SMEM
HBM = pltpu.MemorySpace.HBM
NT = (((1,), (1,)), ((), ()))


def iota(shape, axis):
    return lax.broadcasted_iota(jnp.int32, shape, axis)


def vspec():
    return pl.BlockSpec(memory_space=VMEM)


def sspec():
    return pl.BlockSpec(memory_space=SMEM)


def f32(*shape):
    return jax.ShapeDtypeStruct(shape, jnp.float32)


def device_col():
    return (lax.axis_index("x") * 2 + lax.axis_index("core")) * 4 + lax.axis_index("z")


def params():
    return pltpu.CompilerParams(vmem_limit_bytes=24 << 20)


def split(x):
    high = x.astype(jnp.bfloat16)
    return high, (x - high.astype(jnp.float32)).astype(jnp.bfloat16)


def gram_product(high, low):
    both = jnp.concatenate([high, low], axis=0)
    full = lax.dot_general(both, both, NT, preferred_element_type=jnp.float32)
    return (full[:N, :N] + full[N:, N:]) + (full[:N, N:] + full[N:, :N])


CHUNKS = (0, 2, 6)


def gram_kernel(
    coeffs_in, ids_in, counts_in, primal_in, slack_in, tiles, acc, other, small, root_out,
    hot_ids, hot_place, coeffs, ids, counts, primal, slack, hot, hot2, sem, tile_sem,
):
    little = [
        pltpu.make_async_copy(ids_in, ids, sem.at[0]),
        pltpu.make_async_copy(counts_in, counts, sem.at[1]),
        pltpu.make_async_copy(primal_in, primal, sem.at[2]),
        pltpu.make_async_copy(slack_in, slack, sem.at[3]),
    ]
    big = {}
    for k, g in enumerate(CHUNKS):
        part = pl.ds(g, (CHUNKS + (GROUPS,))[k + 1] - g)
        big[g] = pltpu.make_async_copy(coeffs_in.at[part], coeffs.at[part], tile_sem.at[k])
    for copy in little + list(big.values()):
        copy.start()
    acc[...] = jnp.zeros_like(acc)
    small[...] = jnp.zeros_like(small)
    hot[...] = jnp.zeros_like(hot)
    hot2[...] = jnp.zeros_like(hot2)
    core = lax.axis_index("core")
    for copy in little:
        copy.wait()
    row = iota((HALF, N), 0)
    lane = iota((HALF, N), 1)
    line_lane = iota((1, N), 1)
    lower = jnp.logical_or(row >= lane, lane >= HALF)
    for g in range(GROUPS):
        scale = jnp.where(line_lane < counts[g], primal[g : g + 1, :] / slack[g : g + 1, :], 0.0)
        root_out[g : g + 1, :] = jnp.sqrt(scale)
    for g in range(GROUPS):
        if g in big:
            big[g].wait()
        root = root_out[g : g + 1, :]
        for s in range(SPAN):
            high, low = split(coeffs[g, s] * root)
            tiles[g, s * N : (s + 1) * N, :] = jnp.concatenate([high, low], axis=1)
            gram = gram_product(high, low)
            rolled = pltpu.roll(gram[HALF:], HALF, 1)
            packed = jnp.where(lower, gram[:HALF], rolled)
            line = jnp.sum(jnp.where(row == lane, rolled, 0.0), axis=0, keepdims=True)
            block = ids[s, g]
            chip = (((block >> 3) & 3) << 4) | ((block & 3) << 2) | (block >> 5)
            place = (((block >> 2) & 1) ^ core) * HALF + chip
            acc[place] += packed
            small[pl.ds(place * EXTRA, 1), :] += line
            t = g * SPAN + s
            hot[t : t + 1, :] = (line_lane == block).astype(jnp.float32)
            hot2[t : t + 1, :] = (line_lane == place).astype(jnp.float32)
    other[...] = acc[pl.ds(HALF, HALF)]
    hot_ids[...] = jnp.transpose(hot[...]).astype(jnp.bfloat16)
    hot_place[...] = jnp.transpose(hot2[...]).astype(jnp.bfloat16)


def run_gram(coeffs, ids, counts, primal, slack):
    return pl.pallas_call(
        gram_kernel,
        out_shape=(
            jax.ShapeDtypeStruct((GROUPS, SPAN * N, 2 * N), jnp.bfloat16),
            f32(N, HALF, N),
            f32(HALF, HALF, N),
            f32(N * EXTRA, N),
            f32(GROUPS, N),
            jax.ShapeDtypeStruct((N, N), jnp.bfloat16),
            jax.ShapeDtypeStruct((N, N), jnp.bfloat16),
        ),
        in_specs=[pl.BlockSpec(memory_space=HBM)] * 5,
        out_specs=(vspec(),) * 7,
        scratch_shapes=[
            pltpu.VMEM((GROUPS, SPAN, N, N), jnp.float32),
            pltpu.SMEM((SPAN, GROUPS), jnp.int32),
            pltpu.SMEM((GROUPS,), jnp.int32),
            pltpu.VMEM((GROUPS, N), jnp.float32),
            pltpu.VMEM((GROUPS, N), jnp.float32),
            pltpu.VMEM((N, N), jnp.float32),
            pltpu.VMEM((N, N), jnp.float32),
            pltpu.SemaphoreType.DMA((4,)),
            pltpu.SemaphoreType.DMA((GROUPS,)),
        ],
        compiler_params=params(),
        cost_estimate=pl.CostEstimate(
            flops=TILES * 2 * N**3 * 4, bytes_accessed=12 << 20, transcendentals=0
        ),
        name="gram",
    )(*(pltpu.with_memory_space_constraint(x, HBM) for x in (coeffs, ids, counts, primal, slack)))


def transpose_apply(ids, tiles, vector, spread, out):
    for t in range(TILES):
        spread[t : t + 1, :] = vector[pl.ds(ids[t % SPAN, t // SPAN], 1), :]
    high, low = split(spread[...])
    for g in range(GROUPS):
        parts = []
        for rows in (high, low):
            own = [rows[g * SPAN + s : g * SPAN + s + 1] for s in range(SPAN)]
            parts.append(jnp.concatenate(own, axis=1))
        both = jnp.concatenate(parts, axis=0)
        full = jnp.dot(both, tiles[g], preferred_element_type=jnp.float32)
        out[g : g + 1, :] = (full[0:1, :N] + full[1:2, N:]) + (full[0:1, N:] + full[1:2, :N])


def forward_apply(tiles, colvecs, outs):
    lines = []
    for w in colvecs:
        high, low = split(w)
        lines.append(jnp.concatenate([high, high], axis=1))
        lines.append(jnp.concatenate([low, jnp.zeros_like(low)], axis=1))
    every = len(colvecs) + 1
    for g in range(GROUPS):
        if g % every == every - 1:
            for s in range(SPAN):
                t = g * SPAN + s
                pair = tiles[g, s * N : (s + 1) * N, :].astype(jnp.float32)
                tile = pair[:, :N] + pair[:, N:]
                for w, out in zip(colvecs, outs):
                    turned = jnp.transpose(tile * w[g : g + 1])
                    out[t : t + 1, :] = jnp.sum(turned, axis=0, keepdims=True)
            continue
        both = jnp.concatenate([line[g : g + 1] for line in lines], axis=0)
        full = lax.dot_general(both, tiles[g], NT, preferred_element_type=jnp.float32)
        for k, out in enumerate(outs):
            total = full[2 * k : 2 * k + 1] + full[2 * k + 1 : 2 * k + 2]
            for s in range(SPAN):
                t = g * SPAN + s
                out[t : t + 1, :] = total[:, s * N : (s + 1) * N]


def place_rows(hot, rows):
    rows = jnp.concatenate([rows, jnp.zeros((N - TILES, N), jnp.float32)], axis=0)
    high = rows.astype(jnp.bfloat16)
    middle, low = split(rows - high.astype(jnp.float32))
    total = jnp.dot(hot, high, preferred_element_type=jnp.float32)
    total = total + jnp.dot(hot, middle, preferred_element_type=jnp.float32)
    return total + jnp.dot(hot, low, preferred_element_type=jnp.float32)


def rhs_kernel(
    ids, counts, hot_place, tiles, dual0, dual1, dual2, dual3, primal, slack, cost, root, small,
    own_out, other_out, base_out, scale_out, spread, spread2, duals, valid_s, applied,
):
    leg = lax.axis_index("leg")
    for k, part in enumerate((dual0, dual1, dual2, dual3)):
        at = pl.multiple_of(((leg - k) & 3) * 32, 32)
        duals[pl.ds(at, 32), :] = part[...]
    for g in range(GROUPS):
        valid_s[g : g + 1, :] = (iota((1, N), 1) < counts[g]).astype(jnp.float32)
    valid = valid_s[...]
    used = valid > 0.0
    transpose_apply(ids, tiles, duals, spread, applied)
    dual_res = cost[...] - applied[...] / jnp.where(used, root[...], 1.0) - slack[...]
    weighted = root[...] * dual_res
    ratio = valid / slack[...]
    base_out[...] = -(root[...] * weighted) - valid * primal[...]
    scale_out[...] = ratio
    product = primal[...] * slack[...]
    forward_apply(tiles, (weighted, valid / jnp.sqrt(product)), (spread, spread2))
    first = place_rows(hot_place[...], spread[...])
    second = place_rows(hot_place[...], spread2[...])
    comp = jnp.sum(valid * product, axis=0, keepdims=True)
    count = jnp.sum(jnp.sum(valid, axis=0, keepdims=True), axis=1, keepdims=True)
    for k, out in enumerate((own_out, other_out)):
        half = slice(k * HALF, k * HALF + HALF)
        diag = small[pl.ds(k * HALF * EXTRA, HALF, stride=EXTRA), :]
        diag = jnp.where(iota((HALF, N), 1) < HALF, diag, jnp.broadcast_to(count, (HALF, N)))
        out[pl.ds(0, HALF, stride=EXTRA), :] = diag
        out[pl.ds(1, HALF, stride=EXTRA), :] = first[half]
        out[pl.ds(2, HALF, stride=EXTRA), :] = second[half]
        out[pl.ds(3, HALF, stride=EXTRA), :] = jnp.broadcast_to(comp, (HALF, N))


def run_rhs(ids, counts, hot_place, tiles, duals, primal, slack, cost, root, small):
    return pl.pallas_call(
        rhs_kernel,
        out_shape=(f32(HALF * EXTRA, N), f32(HALF * EXTRA, N), f32(GROUPS, N), f32(GROUPS, N)),
        in_specs=[sspec(), sspec()] + [vspec()] * 11,
        out_specs=(vspec(),) * 4,
        scratch_shapes=[
            pltpu.VMEM((TILES, N), jnp.float32),
            pltpu.VMEM((TILES, N), jnp.float32),
            pltpu.VMEM((N, N), jnp.float32),
            pltpu.VMEM((GROUPS, N), jnp.float32),
            pltpu.VMEM((GROUPS, N), jnp.float32),
        ],
        compiler_params=params(),
        cost_estimate=pl.CostEstimate(flops=1 << 27, bytes_accessed=6 << 20, transcendentals=0),
        name="rhs",
    )(ids, counts, hot_place, tiles, *duals, primal, slack, cost, root, small)


def join_kernel(acc, got, small, small_got, out):
    for p in range(HALF // 2):
        at = 2 * ROWS * p
        out[at : at + HALF, :] = acc[2 * p] + got[2 * p]
        extra = slice(2 * EXTRA * p, 2 * EXTRA * (p + 1))
        out[at + HALF : at + HALF + 2 * EXTRA, :] = small[extra, :] + small_got[extra, :]
        out[at + HALF + 2 * EXTRA : at + 2 * ROWS, :] = acc[2 * p + 1] + got[2 * p + 1]


def run_join(acc, got, small, small_got):
    return pl.pallas_call(
        join_kernel,
        out_shape=f32(HALF * ROWS, N),
        in_specs=[vspec()] * 4,
        out_specs=vspec(),
        compiler_params=params(),
        name="join",
    )(acc, got, small, small_got)


def small_inverse(cols):
    cols = list(cols)
    sub = iota((8, N), 0)
    for m in range(8):
        rows = [jnp.broadcast_to(c[m : m + 1, :], (8, N)) for c in cols]
        inv = 1.0 / rows[m]
        factor = cols[m]
        here = sub == m
        for j in range(8):
            if j == m:
                cols[j] = jnp.where(here, inv, -factor * inv)
            else:
                scaled = rows[j] * inv
                cols[j] = jnp.where(here, scaled, cols[j] - factor * scaled)
    return cols


def invert(panels):
    panels = list(panels)
    lane = iota((8, N), 1)
    count = len(panels)
    for k in range(count):
        mine = jnp.logical_and(lane >= 8 * k, lane < 8 * k + 8)
        pivot = panels[k]
        cols = [jnp.broadcast_to(pivot[:, 8 * k + m : 8 * k + m + 1], (8, N)) for m in range(8)]
        cols = small_inverse(cols)
        total = None
        for m in range(8):
            term = cols[m] * jnp.broadcast_to(pivot[m : m + 1, :], (8, N))
            total = term if total is None else total + term
        for m in range(8):
            total = jnp.where(lane == 8 * k + m, cols[m], total)
        rows = [jnp.broadcast_to(total[m : m + 1, :], (8, N)) for m in range(8)]
        for step in range(1, count):
            i = (k + step) % count
            old = panels[i]
            new = jnp.where(mine, 0.0, old)
            for m in range(8):
                col = jnp.broadcast_to(old[:, 8 * k + m : 8 * k + m + 1], (8, N))
                new = new - col * rows[m]
            panels[i] = new
        panels[k] = total
    return panels


RESIDUAL, SMOOTHED, DIRECTION, IMAGE, PART, NORM, CURVE, STEP, BETA = range(9)
KEPT = 16


def total_of(line):
    return jnp.sum(line, axis=1, keepdims=True)


def smooth(residual, inverse):
    return jnp.dot(
        jnp.broadcast_to(residual, (8, N)),
        inverse,
        precision=PRECISE,
        preferred_element_type=jnp.float32,
    )[0:1]


def first_kernel(got, demand, inverse_out, kept, mu_out, msg):
    def add(i, carry):
        return carry + got[pl.ds(pl.multiple_of(i * 2 * ROWS, 8), 2 * ROWS), :]

    total = lax.fori_loop(1, HALF // 2, add, got[0 : 2 * ROWS, :], unroll=True)
    total = total[:ROWS] + total[ROWS:]
    odd = (lax.axis_index("leg") & 1) == 1
    packed = jnp.where(odd, total[EXTRA:], total[:HALF])
    tail = jnp.where(odd, total[:EXTRA], total[HALF:])
    line = tail[0:1]
    comp = jnp.sum(tail[3:4], axis=1, keepdims=True)
    used = line[:, HALF : HALF + 1]
    mu = SIGMA * (comp / used)
    mu_out[...] = jnp.broadcast_to(mu, (8, N))
    residual = demand[pl.ds(device_col(), 1), :] + tail[1:2] - mu * tail[2:3]

    row = iota((HALF, N), 0)
    lane = iota((HALF, N), 1)
    flipped = jnp.transpose(jnp.concatenate([packed, jnp.zeros((HALF, N), jnp.float32)], axis=0))
    flip_top, flip_bottom = flipped[:HALF], flipped[HALF:]
    top = jnp.where(jnp.logical_or(row >= lane, lane >= HALF), packed, flip_top)
    corner = jnp.where(row < lane, packed, flip_top)
    corner = jnp.where(row == lane, jnp.broadcast_to(line, (HALF, N)), corner)
    bottom = jnp.where(lane < HALF, flip_bottom, pltpu.roll(corner, HALF, 1))
    top = top + jnp.where(row == lane, REGULAR, 0.0)
    bottom = bottom + jnp.where(row + HALF == lane, REGULAR, 0.0)
    panels = [top[8 * i : 8 * i + 8] for i in range(8)]
    panels += [bottom[8 * i : 8 * i + 8] for i in range(8)]
    inverse = jnp.concatenate(invert(panels), axis=0)
    inverse_out[...] = inverse
    smoothed = smooth(residual, inverse)
    part = total_of(residual * smoothed)
    zero = jnp.zeros((1, N), jnp.float32)
    kept[RESIDUAL : RESIDUAL + 1, :] = residual
    kept[SMOOTHED : SMOOTHED + 1, :] = smoothed
    kept[PART : PART + 1, :] = jnp.broadcast_to(part, (1, N))
    for at in (DIRECTION, IMAGE):
        kept[at : at + 1, :] = zero
    msg[...] = jnp.broadcast_to(smoothed, (N, N))


def run_first(got, demand):
    return pl.pallas_call(
        first_kernel,
        out_shape=(f32(N, N), f32(KEPT, N), f32(8, N), f32(N, N)),
        in_specs=[vspec(), vspec()],
        out_specs=(vspec(),) * 4,
        compiler_params=params(),
        name="first",
    )(got, demand)


def sum_pairs(got):
    total = jnp.sum(got[...].reshape(N // 4, 8, N), axis=0)
    even = (total[0:1] + total[2:3]) + (total[4:5] + total[6:7])
    odd = (total[1:2] + total[3:4]) + (total[5:6] + total[7:8])
    return even, odd


def combine(line, before, begin):
    curve, cross, norm = line[:, 0:1], line[:, 1:2], line[:, 2:3]
    if begin:
        return norm, jnp.zeros_like(norm), curve
    beta = norm / before[NORM : NORM + 1, 0:1]
    old = before[CURVE : CURVE + 1, 0:1]
    return norm, beta, curve + beta * (2.0 * cross + beta * old)


def owner_kernel(begin, got, before, inverse, kept, msg):
    image, line = sum_pairs(got)
    smoothed = before[SMOOTHED : SMOOTHED + 1, :]
    image = image + REGULAR * smoothed
    norm, beta, curve = combine(line, before, begin)
    direction = smoothed
    if not begin:
        image = image + beta * before[IMAGE : IMAGE + 1, :]
        direction = smoothed + beta * before[DIRECTION : DIRECTION + 1, :]
    step_len = norm / curve
    residual = before[RESIDUAL : RESIDUAL + 1, :] - step_len * image
    smoothed = smooth(residual, inverse[...])
    rows = (
        (RESIDUAL, residual),
        (SMOOTHED, smoothed),
        (DIRECTION, direction),
        (IMAGE, image),
        (PART, total_of(residual * smoothed)),
        (NORM, norm),
        (CURVE, curve),
        (STEP, step_len),
        (BETA, beta),
    )
    for at, row in rows:
        kept[at : at + 1, :] = jnp.broadcast_to(row, (1, N))
    msg[...] = jnp.broadcast_to(smoothed, (N, N))


def run_owner(begin, got, before, inverse):
    def kernel(*refs):
        owner_kernel(begin, *refs)

    return pl.pallas_call(
        kernel,
        out_shape=(f32(KEPT, N), f32(N, N)),
        in_specs=[vspec()] * 3,
        out_specs=(vspec(),) * 2,
        compiler_params=params(),
        name="owner",
    )(got, before, inverse)


def sum_pairs(got):
    total = jnp.sum(got[...].reshape(N // 4, 8, N), axis=0)
    even = (total[0:1] + total[2:3]) + (total[4:5] + total[6:7])
    odd = (total[1:2] + total[3:4]) + (total[5:6] + total[7:8])
    return even, odd


def tile_kernel(turn, ids, hot, tiles, got, kept, *refs):
    spread = refs[-1]
    msg, applied_out = refs[-2], refs[-3]
    transpose_apply(ids, tiles, got, spread, applied_out)
    applied = applied_out[...]
    smoothed = kept[SMOOTHED : SMOOTHED + 1, :]
    curve = jnp.sum(applied * applied, axis=0, keepdims=True) + REGULAR * smoothed * smoothed
    if turn == 0:
        cross = jnp.zeros((1, 1), jnp.float32)
    else:
        before = refs[0][...]
        if turn == 2:
            before = before + kept[BETA : BETA + 1, :] * refs[1][...]
        cross = jnp.sum(applied * before, axis=0, keepdims=True)
        cross = total_of(cross + REGULAR * smoothed * kept[DIRECTION : DIRECTION + 1, :])
    lane = iota((1, N), 1)
    line = jnp.where(lane == 0, total_of(curve), jnp.where(lane == 1, cross, 0.0))
    line = jnp.where(lane == 2, kept[PART : PART + 1, :], line)
    if turn == 2:
        msg[...] = jnp.broadcast_to(line, (N, N))
    else:
        msg[pl.ds(1, N, stride=2), :] = jnp.broadcast_to(line, (N, N))
        forward_apply(tiles, (applied,), (spread,))
        msg[pl.ds(0, N, stride=2), :] = place_rows(hot[...], spread[...])


def run_tile(turn, ids, hot, tiles, got, kept, *before):
    def kernel(*refs):
        tile_kernel(turn, *refs)

    return pl.pallas_call(
        kernel,
        out_shape=(f32(GROUPS, N), f32(N if turn == 2 else 2 * N, N)),
        in_specs=[sspec()] + [vspec()] * (4 + len(before)),
        out_specs=(vspec(),) * 2,
        scratch_shapes=[pltpu.VMEM((TILES, N), jnp.float32)],
        compiler_params=params(),
        name="tile_last" if turn == 2 else "tile",
    )(ids, hot, tiles, got, kept, *before)


def final_kernel(
    got, kept1, kept2, z0, z1, z2, a0, a1, a2, mu, root, base, ratio, step_dual, step_primal
):
    line = jnp.sum(got[...], axis=0, keepdims=True)
    norm, beta2, curve = combine(line, kept2, False)
    len2 = norm / curve
    len0, len1 = kept1[STEP : STEP + 1, :], kept2[STEP : STEP + 1, :]
    beta1 = kept2[BETA : BETA + 1, :]
    at = pl.ds(pl.multiple_of(lax.axis_index("leg") * 32, 32), 32)

    def step(v0, v1, v2):
        second = v1 + beta1 * v0
        return len0 * v0 + len1 * second + len2 * (v2 + beta2 * second)

    step_dual[...] = step(z0[at, :], z1[at, :], z2[at, :])
    applied = step(a0[...], a1[...], a2[...])
    step_primal[...] = root[...] * applied + (mu[0:1, :] * ratio[...] + base[...])


def run_final(*args):
    return pl.pallas_call(
        final_kernel,
        out_shape=(f32(32, N), f32(GROUPS, N)),
        in_specs=[vspec()] * len(args),
        out_specs=(vspec(), vspec()),
        compiler_params=params(),
        name="final",
    )(*args)


ALL = ("leg", "x", "core", "z")
CHIPS = ("x", "z", "leg")


def exchange(rows, axes):
    return lax.all_to_all(rows, axes, split_axis=0, concat_axis=0, tiled=True)


def per_device(coeffs, block_ids, col_counts, primal, slack, cost, duals, demand):
    ids = block_ids.T
    parts = [duals]
    for k in (1, 2, 3):
        parts.append(lax.ppermute(duals, "leg", [(i, (i + k) % 4) for i in range(4)]))

    tiles, acc, other, small, root, hot, hot_place = run_gram(
        coeffs, ids, col_counts, primal, slack
    )
    swap = [(0, 1), (1, 0)]
    other, *parts = lax.optimization_barrier((other, *parts))
    got_big = lax.ppermute(other, "core", swap)
    small, small_other, base, ratio = run_rhs(
        ids, col_counts, hot_place, tiles, parts, primal, slack, cost, root, small
    )
    got_small = lax.ppermute(small_other, "core", swap)
    joined = run_join(acc, got_big, small, got_small)
    blocks = exchange(joined.reshape(HALF * ROWS // 4, 4, N), CHIPS).reshape(HALF * ROWS, N)
    inverse, kept0, mu, msg = run_first(blocks, demand)

    z0 = exchange(msg, ALL)
    a0, msg = run_tile(0, ids, hot, tiles, z0, kept0)
    kept1, msg = run_owner(True, exchange(msg, ALL), kept0, inverse)
    z1 = exchange(msg, ALL)
    a1, msg = run_tile(1, ids, hot, tiles, z1, kept1, a0)
    kept2, msg = run_owner(False, exchange(msg, ALL), kept1, inverse)
    z2 = exchange(msg, ALL)
    a2, msg = run_tile(2, ids, hot, tiles, z2, kept2, a1, a0)
    got = exchange(msg, ALL)
    return run_final(got, kept1, kept2, z0, z1, z2, a0, a1, a2, mu, root, base, ratio)


def solution(mesh):
    fine = Mesh(mesh.devices.reshape(4, 4, 2, 4), ("x", "z", "core", "leg"))
    every = ("x", "z", "core", "leg")
    return jax.shard_map(
        per_device,
        mesh=fine,
        in_specs=(
            P(every, None, None, None),
            P(every, None),
            P(every),
            P(every, None),
            P(every, None),
            P(every, None),
            P("leg", None),
            P("leg", None),
        ),
        out_specs=(P("leg", None), P(every, None)),
        check_vma=False,
    )
```

```python
import jax
import jax.numpy as jnp
from jax import lax
from jax.experimental import pallas as pl
from jax.experimental.pallas import tpu as pltpu
from jax.sharding import Mesh, PartitionSpec as P

SIGMA = 0.3
REGULAR = 1.0
PRECISE = lax.Precision.HIGHEST

N = 128
HALF = 64
SPAN = 4
GROUPS = 16
TILES = GROUPS * SPAN
EXTRA = 4
ROWS = HALF + EXTRA

VMEM = pltpu.MemorySpace.VMEM
SMEM = pltpu.MemorySpace.SMEM
HBM = pltpu.MemorySpace.HBM
NT = (((1,), (1,)), ((), ()))


def iota(shape, axis):
    return lax.broadcasted_iota(jnp.int32, shape, axis)


def vspec():
    return pl.BlockSpec(memory_space=VMEM)


def sspec():
    return pl.BlockSpec(memory_space=SMEM)


def f32(*shape):
    return jax.ShapeDtypeStruct(shape, jnp.float32)


def device_col():
    return (lax.axis_index("x") * 2 + lax.axis_index("core")) * 4 + lax.axis_index("z")


def params():
    return pltpu.CompilerParams(vmem_limit_bytes=24 << 20)


def split(x):
    high = x.astype(jnp.bfloat16)
    return high, (x - high.astype(jnp.float32)).astype(jnp.bfloat16)


def gram_product(high, low):
    both = jnp.concatenate([high, low], axis=0)
    full = lax.dot_general(both, both, NT, preferred_element_type=jnp.float32)
    return (full[:N, :N] + full[N:, N:]) + (full[:N, N:] + full[N:, :N])


CHUNKS = (0, 2, 6)


def gram_kernel(
    coeffs_in, ids_in, counts_in, primal_in, slack_in, tiles, acc, other, small, root_out,
    hot_rows, hot_ids, hot_place, coeffs, ids, counts, primal, slack, hot, hot2, sem, tile_sem,
):
    little = [
        pltpu.make_async_copy(ids_in, ids, sem.at[0]),
        pltpu.make_async_copy(counts_in, counts, sem.at[1]),
        pltpu.make_async_copy(primal_in, primal, sem.at[2]),
        pltpu.make_async_copy(slack_in, slack, sem.at[3]),
    ]
    big = {}
    for k, g in enumerate(CHUNKS):
        part = pl.ds(g, (CHUNKS + (GROUPS,))[k + 1] - g)
        big[g] = pltpu.make_async_copy(coeffs_in.at[part], coeffs.at[part], tile_sem.at[k])
    for copy in little + list(big.values()):
        copy.start()
    acc[...] = jnp.zeros_like(acc)
    small[...] = jnp.zeros_like(small)
    hot[...] = jnp.zeros_like(hot)
    hot2[...] = jnp.zeros_like(hot2)
    core = lax.axis_index("core")
    for copy in little:
        copy.wait()
    row = iota((HALF, N), 0)
    lane = iota((HALF, N), 1)
    line_lane = iota((1, N), 1)
    lower = jnp.logical_or(row >= lane, lane >= HALF)
    for g in range(GROUPS):
        scale = jnp.where(line_lane < counts[g], primal[g : g + 1, :] / slack[g : g + 1, :], 0.0)
        root_out[g : g + 1, :] = jnp.sqrt(scale)
    for g in range(GROUPS):
        if g in big:
            big[g].wait()
        root = root_out[g : g + 1, :]
        for s in range(SPAN):
            high, low = split(coeffs[g, s] * root)
            tiles[g, s * N : (s + 1) * N, :] = jnp.concatenate([high, low], axis=1)
            gram = gram_product(high, low)
            rolled = pltpu.roll(gram[HALF:], HALF, 1)
            packed = jnp.where(lower, gram[:HALF], rolled)
            line = jnp.sum(jnp.where(row == lane, rolled, 0.0), axis=0, keepdims=True)
            block = ids[s, g]
            chip = (((block >> 3) & 3) << 4) | ((block & 3) << 2) | (block >> 5)
            place = (((block >> 2) & 1) ^ core) * HALF + chip
            acc[place] += packed
            small[pl.ds(place * EXTRA, 1), :] += line
            t = g * SPAN + s
            hot[t : t + 1, :] = (line_lane == block).astype(jnp.float32)
            hot2[t : t + 1, :] = (line_lane == place).astype(jnp.float32)
    other[...] = acc[pl.ds(HALF, HALF)]
    hot_rows[...] = hot[:TILES, :].astype(jnp.bfloat16)
    hot_ids[...] = jnp.transpose(hot[...]).astype(jnp.bfloat16)
    hot_place[...] = jnp.transpose(hot2[...]).astype(jnp.bfloat16)


def run_gram(coeffs, ids, counts, primal, slack):
    return pl.pallas_call(
        gram_kernel,
        out_shape=(
            jax.ShapeDtypeStruct((GROUPS, SPAN * N, 2 * N), jnp.bfloat16),
            f32(N, HALF, N),
            f32(HALF, HALF, N),
            f32(N * EXTRA, N),
            f32(GROUPS, N),
            jax.ShapeDtypeStruct((TILES, N), jnp.bfloat16),
            jax.ShapeDtypeStruct((N, N), jnp.bfloat16),
            jax.ShapeDtypeStruct((N, N), jnp.bfloat16),
        ),
        in_specs=[pl.BlockSpec(memory_space=HBM)] * 5,
        out_specs=(vspec(),) * 8,
        scratch_shapes=[
            pltpu.VMEM((GROUPS, SPAN, N, N), jnp.float32),
            pltpu.SMEM((SPAN, GROUPS), jnp.int32),
            pltpu.SMEM((GROUPS,), jnp.int32),
            pltpu.VMEM((GROUPS, N), jnp.float32),
            pltpu.VMEM((GROUPS, N), jnp.float32),
            pltpu.VMEM((N, N), jnp.float32),
            pltpu.VMEM((N, N), jnp.float32),
            pltpu.SemaphoreType.DMA((4,)),
            pltpu.SemaphoreType.DMA((GROUPS,)),
        ],
        compiler_params=params(),
        cost_estimate=pl.CostEstimate(
            flops=TILES * 2 * N**3 * 4, bytes_accessed=12 << 20, transcendentals=0
        ),
        name="gram",
    )(*(pltpu.with_memory_space_constraint(x, HBM) for x in (coeffs, ids, counts, primal, slack)))


def transpose_apply(hot, tiles, vector, out):
    high, low = split(vector[...])
    high = jnp.dot(hot, high, preferred_element_type=jnp.float32)
    low = jnp.dot(hot, low, preferred_element_type=jnp.float32)
    whole = high + low
    high, low = high.astype(jnp.bfloat16), low.astype(jnp.bfloat16)
    turned = jnp.transpose(whole)
    for g in range(GROUPS):
        if g % 5 == 4:
            total = None
            for s in range(SPAN):
                t = g * SPAN + s
                pair = tiles[g, s * N : (s + 1) * N, :].astype(jnp.float32)
                tile = pair[:, :N] + pair[:, N:]
                part = tile * jnp.broadcast_to(turned[:, t : t + 1], (N, N))
                part = jnp.sum(part.reshape(N // 8, 8, N), axis=0)
                total = part if total is None else total + part
            out[g : g + 1, :] = jnp.sum(total, axis=0, keepdims=True)
            continue
        parts = []
        for rows in (high, low):
            own = [rows[g * SPAN + s : g * SPAN + s + 1] for s in range(SPAN)]
            parts.append(jnp.concatenate(own, axis=1))
        both = jnp.concatenate(parts, axis=0)
        full = jnp.dot(both, tiles[g], preferred_element_type=jnp.float32)
        out[g : g + 1, :] = (full[0:1, :N] + full[1:2, N:]) + (full[0:1, N:] + full[1:2, :N])


def forward_apply(tiles, colvecs, outs):
    lines = []
    for w in colvecs:
        high, low = split(w)
        lines.append(jnp.concatenate([high, high], axis=1))
        lines.append(jnp.concatenate([low, jnp.zeros_like(low)], axis=1))
    every = len(colvecs) + 1
    for g in range(GROUPS):
        if g % every == every - 1:
            for s in range(SPAN):
                t = g * SPAN + s
                pair = tiles[g, s * N : (s + 1) * N, :].astype(jnp.float32)
                tile = pair[:, :N] + pair[:, N:]
                for w, out in zip(colvecs, outs):
                    turned = jnp.transpose(tile * w[g : g + 1])
                    out[t : t + 1, :] = jnp.sum(turned, axis=0, keepdims=True)
            continue
        both = jnp.concatenate([line[g : g + 1] for line in lines], axis=0)
        full = lax.dot_general(both, tiles[g], NT, preferred_element_type=jnp.float32)
        for k, out in enumerate(outs):
            total = full[2 * k : 2 * k + 1] + full[2 * k + 1 : 2 * k + 2]
            for s in range(SPAN):
                t = g * SPAN + s
                out[t : t + 1, :] = total[:, s * N : (s + 1) * N]


def place_rows(hot, rows):
    rows = jnp.concatenate([rows, jnp.zeros((N - TILES, N), jnp.float32)], axis=0)
    high = rows.astype(jnp.bfloat16)
    middle, low = split(rows - high.astype(jnp.float32))
    total = jnp.dot(hot, high, preferred_element_type=jnp.float32)
    total = total + jnp.dot(hot, middle, preferred_element_type=jnp.float32)
    return total + jnp.dot(hot, low, preferred_element_type=jnp.float32)


def rhs_kernel(
    hot_rows, hot_place, tiles, dual0, dual1, dual2, dual3, primal, slack, cost, root, small,
    own_out, other_out, base_out, scale_out, spread, spread2, duals, applied,
):
    leg = lax.axis_index("leg")
    for k, part in enumerate((dual0, dual1, dual2, dual3)):
        at = pl.multiple_of(((leg - k) & 3) * 32, 32)
        duals[pl.ds(at, 32), :] = part[...]
    used = root[...] > 0.0
    valid = used.astype(jnp.float32)
    transpose_apply(hot_rows[...], tiles, duals, applied)
    dual_res = cost[...] - applied[...] / jnp.where(used, root[...], 1.0) - slack[...]
    weighted = root[...] * dual_res
    ratio = valid / slack[...]
    base_out[...] = -(root[...] * weighted) - valid * primal[...]
    scale_out[...] = ratio
    product = primal[...] * slack[...]
    forward_apply(tiles, (weighted, valid / jnp.sqrt(product)), (spread, spread2))
    first = place_rows(hot_place[...], spread[...])
    second = place_rows(hot_place[...], spread2[...])
    comp = jnp.sum(valid * product, axis=0, keepdims=True)
    count = jnp.sum(jnp.sum(valid, axis=0, keepdims=True), axis=1, keepdims=True)
    for k, out in enumerate((own_out, other_out)):
        half = slice(k * HALF, k * HALF + HALF)
        diag = small[pl.ds(k * HALF * EXTRA, HALF, stride=EXTRA), :]
        diag = jnp.where(iota((HALF, N), 1) < HALF, diag, jnp.broadcast_to(count, (HALF, N)))
        out[pl.ds(0, HALF, stride=EXTRA), :] = diag
        out[pl.ds(1, HALF, stride=EXTRA), :] = first[half]
        out[pl.ds(2, HALF, stride=EXTRA), :] = second[half]
        out[pl.ds(3, HALF, stride=EXTRA), :] = jnp.broadcast_to(comp, (HALF, N))


def run_rhs(hot_rows, hot_place, tiles, duals, primal, slack, cost, root, small):
    return pl.pallas_call(
        rhs_kernel,
        out_shape=(f32(HALF * EXTRA, N), f32(HALF * EXTRA, N), f32(GROUPS, N), f32(GROUPS, N)),
        in_specs=[vspec()] * 12,
        out_specs=(vspec(),) * 4,
        scratch_shapes=[
            pltpu.VMEM((TILES, N), jnp.float32),
            pltpu.VMEM((TILES, N), jnp.float32),
            pltpu.VMEM((N, N), jnp.float32),
            pltpu.VMEM((GROUPS, N), jnp.float32),
        ],
        compiler_params=params(),
        cost_estimate=pl.CostEstimate(flops=1 << 27, bytes_accessed=6 << 20, transcendentals=0),
        name="rhs",
    )(hot_rows, hot_place, tiles, *duals, primal, slack, cost, root, small)


def join_kernel(acc, got, small, small_got, out):
    for p in range(HALF // 2):
        at = 2 * ROWS * p
        out[at : at + HALF, :] = acc[2 * p] + got[2 * p]
        extra = slice(2 * EXTRA * p, 2 * EXTRA * (p + 1))
        out[at + HALF : at + HALF + 2 * EXTRA, :] = small[extra, :] + small_got[extra, :]
        out[at + HALF + 2 * EXTRA : at + 2 * ROWS, :] = acc[2 * p + 1] + got[2 * p + 1]


def run_join(acc, got, small, small_got):
    return pl.pallas_call(
        join_kernel,
        out_shape=f32(HALF * ROWS, N),
        in_specs=[vspec()] * 4,
        out_specs=vspec(),
        compiler_params=params(),
        name="join",
    )(acc, got, small, small_got)


def small_inverse(cols):
    cols = list(cols)
    sub = iota((8, N), 0)
    for m in range(8):
        rows = [jnp.broadcast_to(c[m : m + 1, :], (8, N)) for c in cols]
        inv = 1.0 / rows[m]
        factor = cols[m]
        here = sub == m
        for j in range(8):
            if j == m:
                cols[j] = jnp.where(here, inv, -factor * inv)
            else:
                scaled = rows[j] * inv
                cols[j] = jnp.where(here, scaled, cols[j] - factor * scaled)
    return cols


def invert(panels):
    panels = list(panels)
    lane = iota((8, N), 1)
    count = len(panels)
    for k in range(count):
        mine = jnp.logical_and(lane >= 8 * k, lane < 8 * k + 8)
        pivot = panels[k]
        cols = [jnp.broadcast_to(pivot[:, 8 * k + m : 8 * k + m + 1], (8, N)) for m in range(8)]
        cols = small_inverse(cols)
        total = None
        for m in range(8):
            term = cols[m] * jnp.broadcast_to(pivot[m : m + 1, :], (8, N))
            total = term if total is None else total + term
        for m in range(8):
            total = jnp.where(lane == 8 * k + m, cols[m], total)
        rows = [jnp.broadcast_to(total[m : m + 1, :], (8, N)) for m in range(8)]
        for step in range(1, count):
            i = (k + step) % count
            old = panels[i]
            new = jnp.where(mine, 0.0, old)
            for m in range(8):
                col = jnp.broadcast_to(old[:, 8 * k + m : 8 * k + m + 1], (8, N))
                new = new - col * rows[m]
            panels[i] = new
        panels[k] = total
    return panels


RESIDUAL, SMOOTHED, DIRECTION, IMAGE, PART, NORM, CURVE, STEP, BETA = range(9)
KEPT = 16


def total_of(line):
    return jnp.sum(line, axis=1, keepdims=True)


def smooth(residual, inverse):
    return jnp.dot(
        jnp.broadcast_to(residual, (8, N)),
        inverse,
        precision=PRECISE,
        preferred_element_type=jnp.float32,
    )[0:1]


def first_kernel(got, demand, inverse_out, kept, mu_out, msg):
    def add(i, carry):
        return carry + got[pl.ds(pl.multiple_of(i * 2 * ROWS, 8), 2 * ROWS), :]

    total = lax.fori_loop(1, HALF // 2, add, got[0 : 2 * ROWS, :], unroll=True)
    total = total[:ROWS] + total[ROWS:]
    odd = (lax.axis_index("leg") & 1) == 1
    packed = jnp.where(odd, total[EXTRA:], total[:HALF])
    tail = jnp.where(odd, total[:EXTRA], total[HALF:])
    line = tail[0:1]
    comp = jnp.sum(tail[3:4], axis=1, keepdims=True)
    used = line[:, HALF : HALF + 1]
    mu = SIGMA * (comp / used)
    mu_out[...] = jnp.broadcast_to(mu, (8, N))
    residual = demand[pl.ds(device_col(), 1), :] + tail[1:2] - mu * tail[2:3]

    row = iota((HALF, N), 0)
    lane = iota((HALF, N), 1)
    flipped = jnp.transpose(jnp.concatenate([packed, jnp.zeros((HALF, N), jnp.float32)], axis=0))
    flip_top, flip_bottom = flipped[:HALF], flipped[HALF:]
    top = jnp.where(jnp.logical_or(row >= lane, lane >= HALF), packed, flip_top)
    corner = jnp.where(row < lane, packed, flip_top)
    corner = jnp.where(row == lane, jnp.broadcast_to(line, (HALF, N)), corner)
    bottom = jnp.where(lane < HALF, flip_bottom, pltpu.roll(corner, HALF, 1))
    top = top + jnp.where(row == lane, REGULAR, 0.0)
    bottom = bottom + jnp.where(row + HALF == lane, REGULAR, 0.0)
    panels = [top[8 * i : 8 * i + 8] for i in range(8)]
    panels += [bottom[8 * i : 8 * i + 8] for i in range(8)]
    inverse = jnp.concatenate(invert(panels), axis=0)
    inverse_out[...] = inverse
    smoothed = smooth(residual, inverse)
    part = total_of(residual * smoothed)
    zero = jnp.zeros((1, N), jnp.float32)
    kept[RESIDUAL : RESIDUAL + 1, :] = residual
    kept[SMOOTHED : SMOOTHED + 1, :] = smoothed
    kept[PART : PART + 1, :] = jnp.broadcast_to(part, (1, N))
    for at in (DIRECTION, IMAGE):
        kept[at : at + 1, :] = zero
    msg[...] = jnp.broadcast_to(smoothed, (N, N))


def run_first(got, demand):
    return pl.pallas_call(
        first_kernel,
        out_shape=(f32(N, N), f32(KEPT, N), f32(8, N), f32(N, N)),
        in_specs=[vspec(), vspec()],
        out_specs=(vspec(),) * 4,
        compiler_params=params(),
        name="first",
    )(got, demand)


def sum_pairs(got):
    total = jnp.sum(got[...].reshape(N // 4, 8, N), axis=0)
    even = (total[0:1] + total[2:3]) + (total[4:5] + total[6:7])
    odd = (total[1:2] + total[3:4]) + (total[5:6] + total[7:8])
    return even, odd


def combine(line, before, begin):
    curve, cross, norm = (jnp.broadcast_to(line[:, k : k + 1], (1, N)) for k in range(3))
    if begin:
        return norm, jnp.zeros_like(norm), curve
    beta = norm / before[NORM : NORM + 1, :]
    old = before[CURVE : CURVE + 1, :]
    return norm, beta, curve + beta * (2.0 * cross + beta * old)


def owner_kernel(begin, got, before, inverse, kept, msg):
    image, line = sum_pairs(got)
    smoothed = before[SMOOTHED : SMOOTHED + 1, :]
    image = image + REGULAR * smoothed
    norm, beta, curve = combine(line, before, begin)
    direction = smoothed
    if not begin:
        image = image + beta * before[IMAGE : IMAGE + 1, :]
        direction = smoothed + beta * before[DIRECTION : DIRECTION + 1, :]
    step_len = norm / curve
    residual = before[RESIDUAL : RESIDUAL + 1, :] - step_len * image
    smoothed = smooth(residual, inverse[...])
    rows = (
        (RESIDUAL, residual),
        (SMOOTHED, smoothed),
        (DIRECTION, direction),
        (IMAGE, image),
        (PART, total_of(residual * smoothed)),
        (NORM, norm),
        (CURVE, curve),
        (STEP, step_len),
        (BETA, beta),
    )
    for at, row in rows:
        kept[at : at + 1, :] = jnp.broadcast_to(row, (1, N))
    msg[...] = jnp.broadcast_to(smoothed, (N, N))


def run_owner(begin, got, before, inverse):
    def kernel(*refs):
        owner_kernel(begin, *refs)

    return pl.pallas_call(
        kernel,
        out_shape=(f32(KEPT, N), f32(N, N)),
        in_specs=[vspec()] * 3,
        out_specs=(vspec(),) * 2,
        compiler_params=params(),
        name="owner",
    )(got, before, inverse)


def sum_pairs(got):
    total = jnp.sum(got[...].reshape(N // 4, 8, N), axis=0)
    even = (total[0:1] + total[2:3]) + (total[4:5] + total[6:7])
    odd = (total[1:2] + total[3:4]) + (total[5:6] + total[7:8])
    return even, odd


def tile_kernel(turn, hot_rows, hot, tiles, got, kept, *refs):
    spread = refs[-1]
    msg, applied_out = refs[-2], refs[-3]
    transpose_apply(hot_rows[...], tiles, got, applied_out)
    applied = applied_out[...]
    smoothed = kept[SMOOTHED : SMOOTHED + 1, :]
    curve = jnp.sum(applied * applied, axis=0, keepdims=True) + REGULAR * smoothed * smoothed
    if turn == 0:
        cross = jnp.zeros((1, 1), jnp.float32)
    else:
        before = refs[0][...]
        if turn == 2:
            before = before + kept[BETA : BETA + 1, :] * refs[1][...]
        cross = jnp.sum(applied * before, axis=0, keepdims=True)
        cross = total_of(cross + REGULAR * smoothed * kept[DIRECTION : DIRECTION + 1, :])
    lane = iota((1, N), 1)
    line = jnp.where(lane == 0, total_of(curve), jnp.where(lane == 1, cross, 0.0))
    line = jnp.where(lane == 2, kept[PART : PART + 1, :], line)
    if turn == 2:
        msg[...] = jnp.broadcast_to(line, (N, N))
    else:
        msg[pl.ds(1, N, stride=2), :] = jnp.broadcast_to(line, (N, N))
        forward_apply(tiles, (applied,), (spread,))
        msg[pl.ds(0, N, stride=2), :] = place_rows(hot[...], spread[...])


def run_tile(turn, hot_rows, hot, tiles, got, kept, *before):
    def kernel(*refs):
        tile_kernel(turn, *refs)

    return pl.pallas_call(
        kernel,
        out_shape=(f32(GROUPS, N), f32(N if turn == 2 else 2 * N, N)),
        in_specs=[vspec()] * (5 + len(before)),
        out_specs=(vspec(),) * 2,
        scratch_shapes=[pltpu.VMEM((TILES, N), jnp.float32)],
        compiler_params=params(),
        name="tile_last" if turn == 2 else "tile",
    )(hot_rows, hot, tiles, got, kept, *before)


def final_kernel(
    got, kept1, kept2, z0, z1, z2, a0, a1, a2, mu, root, base, ratio, step_dual, step_primal
):
    line = jnp.sum(got[...], axis=0, keepdims=True)
    norm, beta2, curve = combine(line, kept2, False)
    len2 = norm / curve
    len0, len1 = kept1[STEP : STEP + 1, :], kept2[STEP : STEP + 1, :]
    beta1 = kept2[BETA : BETA + 1, :]
    at = pl.ds(pl.multiple_of(lax.axis_index("leg") * 32, 32), 32)

    def step(v0, v1, v2):
        second = v1 + beta1 * v0
        return len0 * v0 + len1 * second + len2 * (v2 + beta2 * second)

    step_dual[...] = step(z0[at, :], z1[at, :], z2[at, :])
    applied = step(a0[...], a1[...], a2[...])
    step_primal[...] = root[...] * applied + (mu[0:1, :] * ratio[...] + base[...])


def run_final(*args):
    return pl.pallas_call(
        final_kernel,
        out_shape=(f32(32, N), f32(GROUPS, N)),
        in_specs=[vspec()] * len(args),
        out_specs=(vspec(), vspec()),
        compiler_params=params(),
        name="final",
    )(*args)


ALL = ("leg", "x", "core", "z")
CHIPS = ("x", "z", "leg")


def exchange(rows, axes):
    return lax.all_to_all(rows, axes, split_axis=0, concat_axis=0, tiled=True)


def per_device(coeffs, block_ids, col_counts, primal, slack, cost, duals, demand):
    ids = block_ids.T
    parts = [duals]
    for k in (1, 2, 3):
        parts.append(lax.ppermute(duals, "leg", [(i, (i + k) % 4) for i in range(4)]))

    tiles, acc, other, small, root, hot_rows, hot, hot_place = run_gram(
        coeffs, ids, col_counts, primal, slack
    )
    swap = [(0, 1), (1, 0)]
    other, *parts = lax.optimization_barrier((other, *parts))
    got_big = lax.ppermute(other, "core", swap)
    small, small_other, base, ratio = run_rhs(
        hot_rows, hot_place, tiles, parts, primal, slack, cost, root, small
    )
    got_small = lax.ppermute(small_other, "core", swap)
    joined = run_join(acc, got_big, small, got_small)
    blocks = exchange(joined.reshape(HALF * ROWS // 4, 4, N), CHIPS).reshape(HALF * ROWS, N)
    inverse, kept0, mu, msg = run_first(blocks, demand)

    z0 = exchange(msg, ALL)
    a0, msg = run_tile(0, hot_rows, hot, tiles, z0, kept0)
    kept1, msg = run_owner(True, exchange(msg, ALL), kept0, inverse)
    z1 = exchange(msg, ALL)
    a1, msg = run_tile(1, hot_rows, hot, tiles, z1, kept1, a0)
    kept2, msg = run_owner(False, exchange(msg, ALL), kept1, inverse)
    z2 = exchange(msg, ALL)
    a2, msg = run_tile(2, hot_rows, hot, tiles, z2, kept2, a1, a0)
    got = exchange(msg, ALL)
    return run_final(got, kept1, kept2, z0, z1, z2, a0, a1, a2, mu, root, base, ratio)


def solution(mesh):
    fine = Mesh(mesh.devices.reshape(4, 4, 2, 4), ("x", "z", "core", "leg"))
    every = ("x", "z", "core", "leg")
    return jax.shard_map(
        per_device,
        mesh=fine,
        in_specs=(
            P(every, None, None, None),
            P(every, None),
            P(every),
            P(every, None),
            P(every, None),
            P(every, None),
            P("leg", None),
            P("leg", None),
        ),
        out_specs=(P("leg", None), P(every, None)),
        check_vma=False,
    )
```

```python
import jax
import jax.numpy as jnp
from jax import lax
from jax.experimental import pallas as pl
from jax.experimental.pallas import tpu as pltpu
from jax.sharding import Mesh, PartitionSpec as P

SIGMA = 0.3
REGULAR = 1.0
PRECISE = lax.Precision.HIGHEST

N = 128
HALF = 64
SPAN = 4
GROUPS = 16
TILES = GROUPS * SPAN
EXTRA = 4
ROWS = HALF + EXTRA

VMEM = pltpu.MemorySpace.VMEM
SMEM = pltpu.MemorySpace.SMEM
HBM = pltpu.MemorySpace.HBM
NT = (((1,), (1,)), ((), ()))


def iota(shape, axis):
    return lax.broadcasted_iota(jnp.int32, shape, axis)


def vspec():
    return pl.BlockSpec(memory_space=VMEM)


def sspec():
    return pl.BlockSpec(memory_space=SMEM)


def f32(*shape):
    return jax.ShapeDtypeStruct(shape, jnp.float32)


def device_col():
    return (lax.axis_index("x") * 2 + lax.axis_index("core")) * 4 + lax.axis_index("z")


def params():
    return pltpu.CompilerParams(vmem_limit_bytes=24 << 20)


def split(x):
    high = x.astype(jnp.bfloat16)
    return high, (x - high.astype(jnp.float32)).astype(jnp.bfloat16)


def gram_product(high, low):
    both = jnp.concatenate([high, low], axis=0)
    full = lax.dot_general(both, both, NT, preferred_element_type=jnp.float32)
    return (full[:N, :N] + full[N:, N:]) + (full[:N, N:] + full[N:, :N])


CHUNKS = (0, 5)


def gram_kernel(
    coeffs_in, ids_in, counts_in, primal_in, slack_in, tiles, acc, other, small, root_out,
    hot_rows, hot_ids, hot_place, coeffs, ids, counts, primal, slack, hot, hot2, sem, tile_sem,
):
    little = [
        pltpu.make_async_copy(ids_in, ids, sem.at[0]),
        pltpu.make_async_copy(counts_in, counts, sem.at[1]),
        pltpu.make_async_copy(primal_in, primal, sem.at[2]),
        pltpu.make_async_copy(slack_in, slack, sem.at[3]),
    ]
    big = {}
    for k, g in enumerate(CHUNKS):
        part = pl.ds(g, (CHUNKS + (GROUPS,))[k + 1] - g)
        big[g] = pltpu.make_async_copy(coeffs_in.at[part], coeffs.at[part], tile_sem.at[k])
    for copy in little + list(big.values()):
        copy.start()
    acc[...] = jnp.zeros_like(acc)
    small[...] = jnp.zeros_like(small)
    hot[...] = jnp.zeros_like(hot)
    hot2[...] = jnp.zeros_like(hot2)
    core = lax.axis_index("core")
    for copy in little:
        copy.wait()
    row = iota((HALF, N), 0)
    lane = iota((HALF, N), 1)
    line_lane = iota((1, N), 1)
    lower = jnp.logical_or(row >= lane, lane >= HALF)
    for g in range(GROUPS):
        scale = jnp.where(line_lane < counts[g], primal[g : g + 1, :] / slack[g : g + 1, :], 0.0)
        root_out[g : g + 1, :] = jnp.sqrt(scale)
    for g in range(GROUPS):
        if g in big:
            big[g].wait()
        root = root_out[g : g + 1, :]
        for s in range(SPAN):
            high, low = split(coeffs[g, s] * root)
            tiles[g, s * N : (s + 1) * N, :] = jnp.concatenate([high, low], axis=1)
            gram = gram_product(high, low)
            rolled = pltpu.roll(gram[HALF:], HALF, 1)
            packed = jnp.where(lower, gram[:HALF], rolled)
            line = jnp.sum(jnp.where(row == lane, rolled, 0.0), axis=0, keepdims=True)
            block = ids[s, g]
            chip = (((block >> 3) & 3) << 4) | ((block & 3) << 2) | (block >> 5)
            place = (((block >> 2) & 1) ^ core) * HALF + chip
            acc[place] += packed
            small[pl.ds(place * EXTRA, 1), :] += line
            t = g * SPAN + s
            hot[t : t + 1, :] = (line_lane == block).astype(jnp.float32)
            hot2[t : t + 1, :] = (line_lane == place).astype(jnp.float32)
    other[...] = acc[pl.ds(HALF, HALF)]
    hot_rows[...] = hot[:TILES, :].astype(jnp.bfloat16)
    hot_ids[...] = jnp.transpose(hot[...]).astype(jnp.bfloat16)
    hot_place[...] = jnp.transpose(hot2[...]).astype(jnp.bfloat16)


def run_gram(coeffs, ids, counts, primal, slack):
    return pl.pallas_call(
        gram_kernel,
        out_shape=(
            jax.ShapeDtypeStruct((GROUPS, SPAN * N, 2 * N), jnp.bfloat16),
            f32(N, HALF, N),
            f32(HALF, HALF, N),
            f32(N * EXTRA, N),
            f32(GROUPS, N),
            jax.ShapeDtypeStruct((TILES, N), jnp.bfloat16),
            jax.ShapeDtypeStruct((N, N), jnp.bfloat16),
            jax.ShapeDtypeStruct((N, N), jnp.bfloat16),
        ),
        in_specs=[pl.BlockSpec(memory_space=HBM)] * 5,
        out_specs=(vspec(),) * 8,
        scratch_shapes=[
            pltpu.VMEM((GROUPS, SPAN, N, N), jnp.float32),
            pltpu.SMEM((SPAN, GROUPS), jnp.int32),
            pltpu.SMEM((GROUPS,), jnp.int32),
            pltpu.VMEM((GROUPS, N), jnp.float32),
            pltpu.VMEM((GROUPS, N), jnp.float32),
            pltpu.VMEM((N, N), jnp.float32),
            pltpu.VMEM((N, N), jnp.float32),
            pltpu.SemaphoreType.DMA((4,)),
            pltpu.SemaphoreType.DMA((GROUPS,)),
        ],
        compiler_params=params(),
        cost_estimate=pl.CostEstimate(
            flops=TILES * 2 * N**3 * 4, bytes_accessed=12 << 20, transcendentals=0
        ),
        name="gram",
    )(*(pltpu.with_memory_space_constraint(x, HBM) for x in (coeffs, ids, counts, primal, slack)))


def transpose_apply(hot, tiles, vector, out):
    high, low = split(vector[...])
    high = jnp.dot(hot, high, preferred_element_type=jnp.float32)
    low = jnp.dot(hot, low, preferred_element_type=jnp.float32)
    whole = high + low
    high, low = high.astype(jnp.bfloat16), low.astype(jnp.bfloat16)
    turned = jnp.transpose(whole)
    for g in range(GROUPS):
        if g % 5 == 4:
            total = None
            for s in range(SPAN):
                t = g * SPAN + s
                pair = tiles[g, s * N : (s + 1) * N, :].astype(jnp.float32)
                tile = pair[:, :N] + pair[:, N:]
                part = tile * jnp.broadcast_to(turned[:, t : t + 1], (N, N))
                part = jnp.sum(part.reshape(N // 8, 8, N), axis=0)
                total = part if total is None else total + part
            out[g : g + 1, :] = jnp.sum(total, axis=0, keepdims=True)
            continue
        parts = []
        for rows in (high, low):
            own = [rows[g * SPAN + s : g * SPAN + s + 1] for s in range(SPAN)]
            parts.append(jnp.concatenate(own, axis=1))
        both = jnp.concatenate(parts, axis=0)
        full = jnp.dot(both, tiles[g], preferred_element_type=jnp.float32)
        out[g : g + 1, :] = (full[0:1, :N] + full[1:2, N:]) + (full[0:1, N:] + full[1:2, :N])


def forward_apply(tiles, colvecs, outs):
    lines = []
    for w in colvecs:
        high, low = split(w)
        lines.append(jnp.concatenate([high, high], axis=1))
        lines.append(jnp.concatenate([low, jnp.zeros_like(low)], axis=1))
    every = len(colvecs) + 1
    for g in range(GROUPS):
        if g % every == every - 1:
            for s in range(SPAN):
                t = g * SPAN + s
                pair = tiles[g, s * N : (s + 1) * N, :].astype(jnp.float32)
                tile = pair[:, :N] + pair[:, N:]
                for w, out in zip(colvecs, outs):
                    turned = jnp.transpose(tile * w[g : g + 1])
                    out[t : t + 1, :] = jnp.sum(turned, axis=0, keepdims=True)
            continue
        both = jnp.concatenate([line[g : g + 1] for line in lines], axis=0)
        full = lax.dot_general(both, tiles[g], NT, preferred_element_type=jnp.float32)
        for k, out in enumerate(outs):
            total = full[2 * k : 2 * k + 1] + full[2 * k + 1 : 2 * k + 2]
            for s in range(SPAN):
                t = g * SPAN + s
                out[t : t + 1, :] = total[:, s * N : (s + 1) * N]


def place_rows(hot, rows):
    rows = jnp.concatenate([rows, jnp.zeros((N - TILES, N), jnp.float32)], axis=0)
    high = rows.astype(jnp.bfloat16)
    middle, low = split(rows - high.astype(jnp.float32))
    total = jnp.dot(hot, high, preferred_element_type=jnp.float32)
    total = total + jnp.dot(hot, middle, preferred_element_type=jnp.float32)
    return total + jnp.dot(hot, low, preferred_element_type=jnp.float32)


def rhs_kernel(
    hot_rows, hot_place, tiles, dual0, dual1, dual2, dual3, primal, slack, cost, root, small,
    own_out, other_out, base_out, scale_out, spread, spread2, duals, applied,
):
    leg = lax.axis_index("leg")
    for k, part in enumerate((dual0, dual1, dual2, dual3)):
        at = pl.multiple_of(((leg - k) & 3) * 32, 32)
        duals[pl.ds(at, 32), :] = part[...]
    used = root[...] > 0.0
    valid = used.astype(jnp.float32)
    transpose_apply(hot_rows[...], tiles, duals, applied)
    dual_res = cost[...] - applied[...] / jnp.where(used, root[...], 1.0) - slack[...]
    weighted = root[...] * dual_res
    ratio = valid / slack[...]
    base_out[...] = -(root[...] * weighted) - valid * primal[...]
    scale_out[...] = ratio
    product = primal[...] * slack[...]
    forward_apply(tiles, (weighted, valid / jnp.sqrt(product)), (spread, spread2))
    first = place_rows(hot_place[...], spread[...])
    second = place_rows(hot_place[...], spread2[...])
    comp = jnp.sum(valid * product, axis=0, keepdims=True)
    count = jnp.sum(jnp.sum(valid, axis=0, keepdims=True), axis=1, keepdims=True)
    for k, out in enumerate((own_out, other_out)):
        half = slice(k * HALF, k * HALF + HALF)
        diag = small[pl.ds(k * HALF * EXTRA, HALF, stride=EXTRA), :]
        diag = jnp.where(iota((HALF, N), 1) < HALF, diag, jnp.broadcast_to(count, (HALF, N)))
        out[pl.ds(0, HALF, stride=EXTRA), :] = diag
        out[pl.ds(1, HALF, stride=EXTRA), :] = first[half]
        out[pl.ds(2, HALF, stride=EXTRA), :] = second[half]
        out[pl.ds(3, HALF, stride=EXTRA), :] = jnp.broadcast_to(comp, (HALF, N))


def run_rhs(hot_rows, hot_place, tiles, duals, primal, slack, cost, root, small):
    return pl.pallas_call(
        rhs_kernel,
        out_shape=(f32(HALF * EXTRA, N), f32(HALF * EXTRA, N), f32(GROUPS, N), f32(GROUPS, N)),
        in_specs=[vspec()] * 12,
        out_specs=(vspec(),) * 4,
        scratch_shapes=[
            pltpu.VMEM((TILES, N), jnp.float32),
            pltpu.VMEM((TILES, N), jnp.float32),
            pltpu.VMEM((N, N), jnp.float32),
            pltpu.VMEM((GROUPS, N), jnp.float32),
        ],
        compiler_params=params(),
        cost_estimate=pl.CostEstimate(flops=1 << 27, bytes_accessed=6 << 20, transcendentals=0),
        name="rhs",
    )(hot_rows, hot_place, tiles, *duals, primal, slack, cost, root, small)


def join_kernel(acc, got, small, small_got, out):
    for p in range(HALF // 2):
        at = 2 * ROWS * p
        out[at : at + HALF, :] = acc[2 * p] + got[2 * p]
        extra = slice(2 * EXTRA * p, 2 * EXTRA * (p + 1))
        out[at + HALF : at + HALF + 2 * EXTRA, :] = small[extra, :] + small_got[extra, :]
        out[at + HALF + 2 * EXTRA : at + 2 * ROWS, :] = acc[2 * p + 1] + got[2 * p + 1]


def run_join(acc, got, small, small_got):
    return pl.pallas_call(
        join_kernel,
        out_shape=f32(HALF * ROWS, N),
        in_specs=[vspec()] * 4,
        out_specs=vspec(),
        compiler_params=params(),
        name="join",
    )(acc, got, small, small_got)


def small_inverse(cols):
    cols = list(cols)
    sub = iota((8, N), 0)
    for m in range(8):
        rows = [jnp.broadcast_to(c[m : m + 1, :], (8, N)) for c in cols]
        inv = 1.0 / rows[m]
        factor = cols[m]
        here = sub == m
        for j in range(8):
            if j == m:
                cols[j] = jnp.where(here, inv, -factor * inv)
            else:
                scaled = rows[j] * inv
                cols[j] = jnp.where(here, scaled, cols[j] - factor * scaled)
    return cols


def invert(panels):
    panels = list(panels)
    lane = iota((8, N), 1)
    count = len(panels)
    for k in range(count):
        mine = jnp.logical_and(lane >= 8 * k, lane < 8 * k + 8)
        pivot = panels[k]
        cols = [jnp.broadcast_to(pivot[:, 8 * k + m : 8 * k + m + 1], (8, N)) for m in range(8)]
        cols = small_inverse(cols)
        total = None
        for m in range(8):
            term = cols[m] * jnp.broadcast_to(pivot[m : m + 1, :], (8, N))
            total = term if total is None else total + term
        for m in range(8):
            total = jnp.where(lane == 8 * k + m, cols[m], total)
        rows = [jnp.broadcast_to(total[m : m + 1, :], (8, N)) for m in range(8)]
        for step in range(1, count):
            i = (k + step) % count
            old = panels[i]
            terms = []
            for m in range(8):
                col = jnp.broadcast_to(old[:, 8 * k + m : 8 * k + m + 1], (8, N))
                terms.append(col * rows[m])
            while len(terms) > 1:
                terms = [terms[j] + terms[j + 1] for j in range(0, len(terms), 2)]
            panels[i] = jnp.where(mine, 0.0, old) - terms[0]
        panels[k] = total
    return panels


RESIDUAL, SMOOTHED, DIRECTION, IMAGE, PART, NORM, CURVE, STEP, BETA = range(9)
KEPT = 16


def total_of(line):
    return jnp.sum(line, axis=1, keepdims=True)


def smooth(residual, inverse):
    return jnp.dot(
        jnp.broadcast_to(residual, (8, N)),
        inverse,
        precision=PRECISE,
        preferred_element_type=jnp.float32,
    )[0:1]


def first_kernel(got, demand, inverse_out, kept, mu_out, msg):
    def add(i, carry):
        return carry + got[pl.ds(pl.multiple_of(i * 2 * ROWS, 8), 2 * ROWS), :]

    total = lax.fori_loop(1, HALF // 2, add, got[0 : 2 * ROWS, :], unroll=True)
    total = total[:ROWS] + total[ROWS:]
    odd = (lax.axis_index("leg") & 1) == 1
    packed = jnp.where(odd, total[EXTRA:], total[:HALF])
    tail = jnp.where(odd, total[:EXTRA], total[HALF:])
    line = tail[0:1]
    comp = jnp.sum(tail[3:4], axis=1, keepdims=True)
    used = line[:, HALF : HALF + 1]
    mu = SIGMA * (comp / used)
    mu_out[...] = jnp.broadcast_to(mu, (8, N))
    residual = demand[pl.ds(device_col(), 1), :] + tail[1:2] - mu * tail[2:3]

    row = iota((HALF, N), 0)
    lane = iota((HALF, N), 1)
    flipped = jnp.transpose(jnp.concatenate([packed, jnp.zeros((HALF, N), jnp.float32)], axis=0))
    flip_top, flip_bottom = flipped[:HALF], flipped[HALF:]
    top = jnp.where(jnp.logical_or(row >= lane, lane >= HALF), packed, flip_top)
    corner = jnp.where(row < lane, packed, flip_top)
    corner = jnp.where(row == lane, jnp.broadcast_to(line, (HALF, N)), corner)
    bottom = jnp.where(lane < HALF, flip_bottom, pltpu.roll(corner, HALF, 1))
    top = top + jnp.where(row == lane, REGULAR, 0.0)
    bottom = bottom + jnp.where(row + HALF == lane, REGULAR, 0.0)
    panels = [top[8 * i : 8 * i + 8] for i in range(8)]
    panels += [bottom[8 * i : 8 * i + 8] for i in range(8)]
    inverse = jnp.concatenate(invert(panels), axis=0)
    inverse_out[...] = inverse
    smoothed = smooth(residual, inverse)
    part = total_of(residual * smoothed)
    zero = jnp.zeros((1, N), jnp.float32)
    kept[RESIDUAL : RESIDUAL + 1, :] = residual
    kept[SMOOTHED : SMOOTHED + 1, :] = smoothed
    kept[PART : PART + 1, :] = jnp.broadcast_to(part, (1, N))
    for at in (DIRECTION, IMAGE):
        kept[at : at + 1, :] = zero
    msg[...] = jnp.broadcast_to(smoothed, (N, N))


def run_first(got, demand):
    return pl.pallas_call(
        first_kernel,
        out_shape=(f32(N, N), f32(KEPT, N), f32(8, N), f32(N, N)),
        in_specs=[vspec(), vspec()],
        out_specs=(vspec(),) * 4,
        compiler_params=params(),
        name="first",
    )(got, demand)


def sum_pairs(got):
    total = jnp.sum(got[...].reshape(N // 4, 8, N), axis=0)
    even = (total[0:1] + total[2:3]) + (total[4:5] + total[6:7])
    odd = (total[1:2] + total[3:4]) + (total[5:6] + total[7:8])
    return even, odd


def combine(line, before, begin):
    curve, cross, norm = (jnp.broadcast_to(line[:, k : k + 1], (1, N)) for k in range(3))
    if begin:
        return norm, jnp.zeros_like(norm), curve
    beta = norm / before[NORM : NORM + 1, :]
    old = before[CURVE : CURVE + 1, :]
    return norm, beta, curve + beta * (2.0 * cross + beta * old)


def owner_kernel(begin, got, before, inverse, kept, msg):
    image, line = sum_pairs(got)
    smoothed = before[SMOOTHED : SMOOTHED + 1, :]
    image = image + REGULAR * smoothed
    norm, beta, curve = combine(line, before, begin)
    direction = smoothed
    if not begin:
        image = image + beta * before[IMAGE : IMAGE + 1, :]
        direction = smoothed + beta * before[DIRECTION : DIRECTION + 1, :]
    step_len = norm / curve
    residual = before[RESIDUAL : RESIDUAL + 1, :] - step_len * image
    smoothed = smooth(residual, inverse[...])
    rows = (
        (RESIDUAL, residual),
        (SMOOTHED, smoothed),
        (DIRECTION, direction),
        (IMAGE, image),
        (PART, total_of(residual * smoothed)),
        (NORM, norm),
        (CURVE, curve),
        (STEP, step_len),
        (BETA, beta),
    )
    for at, row in rows:
        kept[at : at + 1, :] = jnp.broadcast_to(row, (1, N))
    msg[...] = jnp.broadcast_to(smoothed, (N, N))


def run_owner(begin, got, before, inverse):
    def kernel(*refs):
        owner_kernel(begin, *refs)

    return pl.pallas_call(
        kernel,
        out_shape=(f32(KEPT, N), f32(N, N)),
        in_specs=[vspec()] * 3,
        out_specs=(vspec(),) * 2,
        compiler_params=params(),
        name="owner",
    )(got, before, inverse)


def sum_pairs(got):
    total = jnp.sum(got[...].reshape(N // 4, 8, N), axis=0)
    even = (total[0:1] + total[2:3]) + (total[4:5] + total[6:7])
    odd = (total[1:2] + total[3:4]) + (total[5:6] + total[7:8])
    return even, odd


def tile_kernel(turn, hot_rows, hot, tiles, got, kept, *refs):
    spread = refs[-1]
    msg, applied_out = refs[-2], refs[-3]
    transpose_apply(hot_rows[...], tiles, got, applied_out)
    applied = applied_out[...]
    smoothed = kept[SMOOTHED : SMOOTHED + 1, :]
    curve = jnp.sum(applied * applied, axis=0, keepdims=True) + REGULAR * smoothed * smoothed
    if turn == 0:
        cross = jnp.zeros((1, 1), jnp.float32)
    else:
        before = refs[0][...]
        if turn == 2:
            before = before + kept[BETA : BETA + 1, :] * refs[1][...]
        cross = jnp.sum(applied * before, axis=0, keepdims=True)
        cross = total_of(cross + REGULAR * smoothed * kept[DIRECTION : DIRECTION + 1, :])
    lane = iota((1, N), 1)
    line = jnp.where(lane == 0, total_of(curve), jnp.where(lane == 1, cross, 0.0))
    line = jnp.where(lane == 2, kept[PART : PART + 1, :], line)
    if turn == 2:
        msg[...] = jnp.broadcast_to(line, (N, N))
    else:
        msg[pl.ds(1, N, stride=2), :] = jnp.broadcast_to(line, (N, N))
        forward_apply(tiles, (applied,), (spread,))
        msg[pl.ds(0, N, stride=2), :] = place_rows(hot[...], spread[...])


def run_tile(turn, hot_rows, hot, tiles, got, kept, *before):
    def kernel(*refs):
        tile_kernel(turn, *refs)

    return pl.pallas_call(
        kernel,
        out_shape=(f32(GROUPS, N), f32(N if turn == 2 else 2 * N, N)),
        in_specs=[vspec()] * (5 + len(before)),
        out_specs=(vspec(),) * 2,
        scratch_shapes=[pltpu.VMEM((TILES, N), jnp.float32)],
        compiler_params=params(),
        name="tile_last" if turn == 2 else "tile",
    )(hot_rows, hot, tiles, got, kept, *before)


def final_kernel(
    got, kept1, kept2, z0, z1, z2, a0, a1, a2, mu, root, base, ratio, step_dual, step_primal
):
    line = jnp.sum(got[...], axis=0, keepdims=True)
    norm, beta2, curve = combine(line, kept2, False)
    len2 = norm / curve
    len0, len1 = kept1[STEP : STEP + 1, :], kept2[STEP : STEP + 1, :]
    beta1 = kept2[BETA : BETA + 1, :]
    at = pl.ds(pl.multiple_of(lax.axis_index("leg") * 32, 32), 32)

    def step(v0, v1, v2):
        second = v1 + beta1 * v0
        return len0 * v0 + len1 * second + len2 * (v2 + beta2 * second)

    step_dual[...] = step(z0[at, :], z1[at, :], z2[at, :])
    applied = step(a0[...], a1[...], a2[...])
    step_primal[...] = root[...] * applied + (mu[0:1, :] * ratio[...] + base[...])


def run_final(*args):
    return pl.pallas_call(
        final_kernel,
        out_shape=(f32(32, N), f32(GROUPS, N)),
        in_specs=[vspec()] * len(args),
        out_specs=(vspec(), vspec()),
        compiler_params=params(),
        name="final",
    )(*args)


ALL = ("leg", "x", "core", "z")
CHIPS = ("x", "z", "leg")


def exchange(rows, axes):
    return lax.all_to_all(rows, axes, split_axis=0, concat_axis=0, tiled=True)


def per_device(coeffs, block_ids, col_counts, primal, slack, cost, duals, demand):
    ids = block_ids.T
    parts = [duals]
    for k in (1, 2, 3):
        parts.append(lax.ppermute(duals, "leg", [(i, (i + k) % 4) for i in range(4)]))

    tiles, acc, other, small, root, hot_rows, hot, hot_place = run_gram(
        coeffs, ids, col_counts, primal, slack
    )
    swap = [(0, 1), (1, 0)]
    other, *parts = lax.optimization_barrier((other, *parts))
    got_big = lax.ppermute(other, "core", swap)
    small, small_other, base, ratio = run_rhs(
        hot_rows, hot_place, tiles, parts, primal, slack, cost, root, small
    )
    got_small = lax.ppermute(small_other, "core", swap)
    joined = run_join(acc, got_big, small, got_small)
    blocks = exchange(joined.reshape(HALF * ROWS // 4, 4, N), CHIPS).reshape(HALF * ROWS, N)
    inverse, kept0, mu, msg = run_first(blocks, demand)

    z0 = exchange(msg, ALL)
    a0, msg = run_tile(0, hot_rows, hot, tiles, z0, kept0)
    kept1, msg = run_owner(True, exchange(msg, ALL), kept0, inverse)
    z1 = exchange(msg, ALL)
    a1, msg = run_tile(1, hot_rows, hot, tiles, z1, kept1, a0)
    kept2, msg = run_owner(False, exchange(msg, ALL), kept1, inverse)
    z2 = exchange(msg, ALL)
    a2, msg = run_tile(2, hot_rows, hot, tiles, z2, kept2, a1, a0)
    got = exchange(msg, ALL)
    return run_final(got, kept1, kept2, z0, z1, z2, a0, a1, a2, mu, root, base, ratio)


def solution(mesh):
    fine = Mesh(mesh.devices.reshape(4, 4, 2, 4), ("x", "z", "core", "leg"))
    every = ("x", "z", "core", "leg")
    return jax.shard_map(
        per_device,
        mesh=fine,
        in_specs=(
            P(every, None, None, None),
            P(every, None),
            P(every),
            P(every, None),
            P(every, None),
            P(every, None),
            P("leg", None),
            P("leg", None),
        ),
        out_specs=(P("leg", None), P(every, None)),
        check_vma=False,
    )
```

```python
import jax
import jax.numpy as jnp
from jax import lax
from jax.experimental import pallas as pl
from jax.experimental.pallas import tpu as pltpu
from jax.sharding import Mesh, PartitionSpec as P

SIGMA = 0.3
REGULAR = 1.0
PRECISE = lax.Precision.HIGHEST

N = 128
HALF = 64
SPAN = 4
GROUPS = 16
TILES = GROUPS * SPAN
EXTRA = 4
ROWS = HALF + EXTRA

VMEM = pltpu.MemorySpace.VMEM
SMEM = pltpu.MemorySpace.SMEM
HBM = pltpu.MemorySpace.HBM
NT = (((1,), (1,)), ((), ()))


def iota(shape, axis):
    return lax.broadcasted_iota(jnp.int32, shape, axis)


def vspec():
    return pl.BlockSpec(memory_space=VMEM)


def sspec():
    return pl.BlockSpec(memory_space=SMEM)


def f32(*shape):
    return jax.ShapeDtypeStruct(shape, jnp.float32)


def device_col():
    return (lax.axis_index("x") * 2 + lax.axis_index("core")) * 4 + lax.axis_index("z")


def params():
    return pltpu.CompilerParams(vmem_limit_bytes=24 << 20)


def split(x):
    high = x.astype(jnp.bfloat16)
    return high, (x - high.astype(jnp.float32)).astype(jnp.bfloat16)


def gram_product(high, low):
    both = jnp.concatenate([high, low], axis=0)
    full = lax.dot_general(both, both, NT, preferred_element_type=jnp.float32)
    return (full[:N, :N] + full[N:, N:]) + (full[:N, N:] + full[N:, :N])


CHUNKS = (0, 5)


def gram_kernel(
    coeffs_in, ids_in, counts_in, primal_in, slack_in, tiles, acc, other, small, root_out,
    hot_rows, hot_ids, hot_place, coeffs, ids, counts, primal, slack, hot, hot2, sem, tile_sem,
):
    little = [
        pltpu.make_async_copy(ids_in, ids, sem.at[0]),
        pltpu.make_async_copy(counts_in, counts, sem.at[1]),
        pltpu.make_async_copy(primal_in, primal, sem.at[2]),
        pltpu.make_async_copy(slack_in, slack, sem.at[3]),
    ]
    big = {}
    for k, g in enumerate(CHUNKS):
        part = pl.ds(g, (CHUNKS + (GROUPS,))[k + 1] - g)
        big[g] = pltpu.make_async_copy(coeffs_in.at[part], coeffs.at[part], tile_sem.at[k])
    for copy in little + list(big.values()):
        copy.start()
    acc[...] = jnp.zeros_like(acc)
    small[...] = jnp.zeros_like(small)
    hot[...] = jnp.zeros_like(hot)
    hot2[...] = jnp.zeros_like(hot2)
    core = lax.axis_index("core")
    for copy in little:
        copy.wait()
    row = iota((HALF, N), 0)
    lane = iota((HALF, N), 1)
    line_lane = iota((1, N), 1)
    lower = jnp.logical_or(row >= lane, lane >= HALF)
    for g in range(GROUPS):
        scale = jnp.where(line_lane < counts[g], primal[g : g + 1, :] / slack[g : g + 1, :], 0.0)
        root_out[g : g + 1, :] = jnp.sqrt(scale)
    for g in range(GROUPS):
        if g in big:
            big[g].wait()
        root = root_out[g : g + 1, :]
        for s in range(SPAN):
            high, low = split(coeffs[g, s] * root)
            tiles[g, s * N : (s + 1) * N, :] = jnp.concatenate([high, low], axis=1)
            gram = gram_product(high, low)
            rolled = pltpu.roll(gram[HALF:], HALF, 1)
            packed = jnp.where(lower, gram[:HALF], rolled)
            line = jnp.sum(jnp.where(row == lane, rolled, 0.0), axis=0, keepdims=True)
            block = ids[s, g]
            owner = (block & 4) << 4 | (block >> 5) << 4 | ((block >> 3) & 3) << 2 | block & 3
            chip = (((block >> 3) & 3) << 4) | ((block & 3) << 2) | (block >> 5)
            place = (((block >> 2) & 1) ^ core) * HALF + chip
            acc[place] += packed
            small[pl.ds(place * EXTRA, 1), :] += line
            t = g * SPAN + s
            hot[t : t + 1, :] = (line_lane == owner).astype(jnp.float32)
            hot2[t : t + 1, :] = (line_lane == place).astype(jnp.float32)
    other[...] = acc[pl.ds(HALF, HALF)]
    hot_rows[...] = hot[:TILES, :].astype(jnp.bfloat16)
    hot_ids[...] = jnp.transpose(hot[...]).astype(jnp.bfloat16)
    hot_place[...] = jnp.transpose(hot2[...]).astype(jnp.bfloat16)


def run_gram(coeffs, ids, counts, primal, slack):
    return pl.pallas_call(
        gram_kernel,
        out_shape=(
            jax.ShapeDtypeStruct((GROUPS, SPAN * N, 2 * N), jnp.bfloat16),
            f32(N, HALF, N),
            f32(HALF, HALF, N),
            f32(N * EXTRA, N),
            f32(GROUPS, N),
            jax.ShapeDtypeStruct((TILES, N), jnp.bfloat16),
            jax.ShapeDtypeStruct((N, N), jnp.bfloat16),
            jax.ShapeDtypeStruct((N, N), jnp.bfloat16),
        ),
        in_specs=[pl.BlockSpec(memory_space=HBM)] * 5,
        out_specs=(vspec(),) * 8,
        scratch_shapes=[
            pltpu.VMEM((GROUPS, SPAN, N, N), jnp.float32),
            pltpu.SMEM((SPAN, GROUPS), jnp.int32),
            pltpu.SMEM((GROUPS,), jnp.int32),
            pltpu.VMEM((GROUPS, N), jnp.float32),
            pltpu.VMEM((GROUPS, N), jnp.float32),
            pltpu.VMEM((N, N), jnp.float32),
            pltpu.VMEM((N, N), jnp.float32),
            pltpu.SemaphoreType.DMA((4,)),
            pltpu.SemaphoreType.DMA((GROUPS,)),
        ],
        compiler_params=params(),
        cost_estimate=pl.CostEstimate(
            flops=TILES * 2 * N**3 * 4, bytes_accessed=12 << 20, transcendentals=0
        ),
        name="gram",
    )(*(pltpu.with_memory_space_constraint(x, HBM) for x in (coeffs, ids, counts, primal, slack)))


def transpose_apply(hot, tiles, vector, out):
    high, low = split(vector[...])
    high = jnp.dot(hot, high, preferred_element_type=jnp.float32)
    low = jnp.dot(hot, low, preferred_element_type=jnp.float32)
    whole = high + low
    high, low = high.astype(jnp.bfloat16), low.astype(jnp.bfloat16)
    turned = jnp.transpose(whole)
    for g in range(GROUPS):
        if g % 5 == 4:
            total = None
            for s in range(SPAN):
                t = g * SPAN + s
                pair = tiles[g, s * N : (s + 1) * N, :].astype(jnp.float32)
                tile = pair[:, :N] + pair[:, N:]
                part = tile * jnp.broadcast_to(turned[:, t : t + 1], (N, N))
                part = jnp.sum(part.reshape(N // 8, 8, N), axis=0)
                total = part if total is None else total + part
            out[g : g + 1, :] = jnp.sum(total, axis=0, keepdims=True)
            continue
        parts = []
        for rows in (high, low):
            own = [rows[g * SPAN + s : g * SPAN + s + 1] for s in range(SPAN)]
            parts.append(jnp.concatenate(own, axis=1))
        both = jnp.concatenate(parts, axis=0)
        full = jnp.dot(both, tiles[g], preferred_element_type=jnp.float32)
        out[g : g + 1, :] = (full[0:1, :N] + full[1:2, N:]) + (full[0:1, N:] + full[1:2, :N])


def forward_apply(tiles, colvecs, outs):
    lines = []
    for w in colvecs:
        high, low = split(w)
        lines.append(jnp.concatenate([high, high], axis=1))
        lines.append(jnp.concatenate([low, jnp.zeros_like(low)], axis=1))
    every = len(colvecs) + 1
    for g in range(GROUPS):
        if g % every == every - 1:
            for s in range(SPAN):
                t = g * SPAN + s
                pair = tiles[g, s * N : (s + 1) * N, :].astype(jnp.float32)
                tile = pair[:, :N] + pair[:, N:]
                for w, out in zip(colvecs, outs):
                    turned = jnp.transpose(tile * w[g : g + 1])
                    out[t : t + 1, :] = jnp.sum(turned, axis=0, keepdims=True)
            continue
        both = jnp.concatenate([line[g : g + 1] for line in lines], axis=0)
        full = lax.dot_general(both, tiles[g], NT, preferred_element_type=jnp.float32)
        for k, out in enumerate(outs):
            total = full[2 * k : 2 * k + 1] + full[2 * k + 1 : 2 * k + 2]
            for s in range(SPAN):
                t = g * SPAN + s
                out[t : t + 1, :] = total[:, s * N : (s + 1) * N]


def place_rows(hot, rows):
    rows = jnp.concatenate([rows, jnp.zeros((N - TILES, N), jnp.float32)], axis=0)
    high = rows.astype(jnp.bfloat16)
    middle, low = split(rows - high.astype(jnp.float32))
    total = jnp.dot(hot, high, preferred_element_type=jnp.float32)
    total = total + jnp.dot(hot, middle, preferred_element_type=jnp.float32)
    return total + jnp.dot(hot, low, preferred_element_type=jnp.float32)


def rhs_kernel(
    hot_rows, hot_place, tiles, dual0, dual1, dual2, dual3, primal, slack, cost, root, small,
    own_out, other_out, base_out, scale_out, spread, spread2, duals, applied,
):
    leg = lax.axis_index("leg")
    for k, part in enumerate((dual0, dual1, dual2, dual3)):
        at = pl.multiple_of(((leg - k) & 3) * 32, 32)
        at = pl.multiple_of(at // 2, 16)
        for core in range(2):
            rows = [part[8 * x + 4 * core : 8 * x + 4 * core + 4, :] for x in range(4)]
            duals[pl.ds(HALF * core + at, 16), :] = jnp.concatenate(rows, axis=0)
    used = root[...] > 0.0
    valid = used.astype(jnp.float32)
    transpose_apply(hot_rows[...], tiles, duals, applied)
    dual_res = cost[...] - applied[...] / jnp.where(used, root[...], 1.0) - slack[...]
    weighted = root[...] * dual_res
    ratio = valid / slack[...]
    base_out[...] = -(root[...] * weighted) - valid * primal[...]
    scale_out[...] = ratio
    product = primal[...] * slack[...]
    forward_apply(tiles, (weighted, valid / jnp.sqrt(product)), (spread, spread2))
    first = place_rows(hot_place[...], spread[...])
    second = place_rows(hot_place[...], spread2[...])
    comp = jnp.sum(valid * product, axis=0, keepdims=True)
    count = jnp.sum(jnp.sum(valid, axis=0, keepdims=True), axis=1, keepdims=True)
    for k, out in enumerate((own_out, other_out)):
        half = slice(k * HALF, k * HALF + HALF)
        diag = small[pl.ds(k * HALF * EXTRA, HALF, stride=EXTRA), :]
        diag = jnp.where(iota((HALF, N), 1) < HALF, diag, jnp.broadcast_to(count, (HALF, N)))
        out[pl.ds(0, HALF, stride=EXTRA), :] = diag
        out[pl.ds(1, HALF, stride=EXTRA), :] = first[half]
        out[pl.ds(2, HALF, stride=EXTRA), :] = second[half]
        out[pl.ds(3, HALF, stride=EXTRA), :] = jnp.broadcast_to(comp, (HALF, N))


def run_rhs(hot_rows, hot_place, tiles, duals, primal, slack, cost, root, small):
    return pl.pallas_call(
        rhs_kernel,
        out_shape=(f32(HALF * EXTRA, N), f32(HALF * EXTRA, N), f32(GROUPS, N), f32(GROUPS, N)),
        in_specs=[vspec()] * 12,
        out_specs=(vspec(),) * 4,
        scratch_shapes=[
            pltpu.VMEM((TILES, N), jnp.float32),
            pltpu.VMEM((TILES, N), jnp.float32),
            pltpu.VMEM((N, N), jnp.float32),
            pltpu.VMEM((GROUPS, N), jnp.float32),
        ],
        compiler_params=params(),
        cost_estimate=pl.CostEstimate(flops=1 << 27, bytes_accessed=6 << 20, transcendentals=0),
        name="rhs",
    )(hot_rows, hot_place, tiles, *duals, primal, slack, cost, root, small)


def join_kernel(acc, got, small, small_got, out):
    for p in range(HALF // 2):
        at = 2 * ROWS * p
        out[at : at + HALF, :] = acc[2 * p] + got[2 * p]
        extra = slice(2 * EXTRA * p, 2 * EXTRA * (p + 1))
        out[at + HALF : at + HALF + 2 * EXTRA, :] = small[extra, :] + small_got[extra, :]
        out[at + HALF + 2 * EXTRA : at + 2 * ROWS, :] = acc[2 * p + 1] + got[2 * p + 1]


def run_join(acc, got, small, small_got):
    return pl.pallas_call(
        join_kernel,
        out_shape=f32(HALF * ROWS, N),
        in_specs=[vspec()] * 4,
        out_specs=vspec(),
        compiler_params=params(),
        name="join",
    )(acc, got, small, small_got)


def small_inverse(cols):
    cols = list(cols)
    sub = iota((8, N), 0)
    for m in range(8):
        rows = [jnp.broadcast_to(c[m : m + 1, :], (8, N)) for c in cols]
        inv = 1.0 / rows[m]
        factor = cols[m]
        here = sub == m
        for j in range(8):
            if j == m:
                cols[j] = jnp.where(here, inv, -factor * inv)
            else:
                scaled = rows[j] * inv
                cols[j] = jnp.where(here, scaled, cols[j] - factor * scaled)
    return cols


def invert(panels):
    panels = list(panels)
    lane = iota((8, N), 1)
    count = len(panels)
    for k in range(count):
        mine = jnp.logical_and(lane >= 8 * k, lane < 8 * k + 8)
        pivot = panels[k]
        cols = [jnp.broadcast_to(pivot[:, 8 * k + m : 8 * k + m + 1], (8, N)) for m in range(8)]
        cols = small_inverse(cols)
        total = None
        for m in range(8):
            term = cols[m] * jnp.broadcast_to(pivot[m : m + 1, :], (8, N))
            total = term if total is None else total + term
        for m in range(8):
            total = jnp.where(lane == 8 * k + m, cols[m], total)
        rows = [jnp.broadcast_to(total[m : m + 1, :], (8, N)) for m in range(8)]
        for step in range(1, count):
            i = (k + step) % count
            old = panels[i]
            terms = []
            for m in range(8):
                col = jnp.broadcast_to(old[:, 8 * k + m : 8 * k + m + 1], (8, N))
                terms.append(col * rows[m])
            while len(terms) > 1:
                terms = [terms[j] + terms[j + 1] for j in range(0, len(terms), 2)]
            panels[i] = jnp.where(mine, 0.0, old) - terms[0]
        panels[k] = total
    return panels


RESIDUAL, SMOOTHED, DIRECTION, IMAGE, PART, NORM, CURVE, STEP, BETA = range(9)
KEPT = 16


def total_of(line):
    return jnp.sum(line, axis=1, keepdims=True)


def smooth(residual, inverse):
    return jnp.dot(
        jnp.broadcast_to(residual, (8, N)),
        inverse,
        precision=PRECISE,
        preferred_element_type=jnp.float32,
    )[0:1]


def first_kernel(got, demand, inverse_out, kept, mu_out, msg):
    def add(i, carry):
        return carry + got[pl.ds(pl.multiple_of(i * 2 * ROWS, 8), 2 * ROWS), :]

    total = lax.fori_loop(1, HALF // 2, add, got[0 : 2 * ROWS, :], unroll=True)
    total = total[:ROWS] + total[ROWS:]
    odd = (lax.axis_index("leg") & 1) == 1
    packed = jnp.where(odd, total[EXTRA:], total[:HALF])
    tail = jnp.where(odd, total[:EXTRA], total[HALF:])
    line = tail[0:1]
    comp = jnp.sum(tail[3:4], axis=1, keepdims=True)
    used = line[:, HALF : HALF + 1]
    mu = SIGMA * (comp / used)
    mu_out[...] = jnp.broadcast_to(mu, (8, N))
    residual = demand[pl.ds(device_col(), 1), :] + tail[1:2] - mu * tail[2:3]

    row = iota((HALF, N), 0)
    lane = iota((HALF, N), 1)
    flipped = jnp.transpose(jnp.concatenate([packed, jnp.zeros((HALF, N), jnp.float32)], axis=0))
    flip_top, flip_bottom = flipped[:HALF], flipped[HALF:]
    top = jnp.where(jnp.logical_or(row >= lane, lane >= HALF), packed, flip_top)
    corner = jnp.where(row < lane, packed, flip_top)
    corner = jnp.where(row == lane, jnp.broadcast_to(line, (HALF, N)), corner)
    bottom = jnp.where(lane < HALF, flip_bottom, pltpu.roll(corner, HALF, 1))
    top = top + jnp.where(row == lane, REGULAR, 0.0)
    bottom = bottom + jnp.where(row + HALF == lane, REGULAR, 0.0)
    panels = [top[8 * i : 8 * i + 8] for i in range(8)]
    panels += [bottom[8 * i : 8 * i + 8] for i in range(8)]
    inverse = jnp.concatenate(invert(panels), axis=0)
    inverse_out[...] = inverse
    smoothed = smooth(residual, inverse)
    part = total_of(residual * smoothed)
    zero = jnp.zeros((1, N), jnp.float32)
    kept[RESIDUAL : RESIDUAL + 1, :] = residual
    kept[SMOOTHED : SMOOTHED + 1, :] = smoothed
    kept[PART : PART + 1, :] = jnp.broadcast_to(part, (1, N))
    for at in (DIRECTION, IMAGE):
        kept[at : at + 1, :] = zero
    msg[...] = jnp.broadcast_to(smoothed, (N, N))


def run_first(got, demand):
    return pl.pallas_call(
        first_kernel,
        out_shape=(f32(N, N), f32(KEPT, N), f32(8, N), f32(N, N)),
        in_specs=[vspec(), vspec()],
        out_specs=(vspec(),) * 4,
        compiler_params=params(),
        name="first",
    )(got, demand)


def sum_pairs(got):
    total = jnp.sum(got[...].reshape(N // 4, 8, N), axis=0)
    even = (total[0:1] + total[2:3]) + (total[4:5] + total[6:7])
    odd = (total[1:2] + total[3:4]) + (total[5:6] + total[7:8])
    return even, odd


def combine(line, before, begin):
    curve, cross, norm = (jnp.broadcast_to(line[:, k : k + 1], (1, N)) for k in range(3))
    if begin:
        return norm, jnp.zeros_like(norm), curve
    beta = norm / before[NORM : NORM + 1, :]
    old = before[CURVE : CURVE + 1, :]
    return norm, beta, curve + beta * (2.0 * cross + beta * old)


def owner_kernel(begin, got, before, inverse, kept, msg):
    image, line = sum_pairs(got)
    smoothed = before[SMOOTHED : SMOOTHED + 1, :]
    image = image + REGULAR * smoothed
    norm, beta, curve = combine(line, before, begin)
    direction = smoothed
    if not begin:
        image = image + beta * before[IMAGE : IMAGE + 1, :]
        direction = smoothed + beta * before[DIRECTION : DIRECTION + 1, :]
    step_len = norm / curve
    residual = before[RESIDUAL : RESIDUAL + 1, :] - step_len * image
    smoothed = smooth(residual, inverse[...])
    rows = (
        (RESIDUAL, residual),
        (SMOOTHED, smoothed),
        (DIRECTION, direction),
        (IMAGE, image),
        (PART, total_of(residual * smoothed)),
        (NORM, norm),
        (CURVE, curve),
        (STEP, step_len),
        (BETA, beta),
    )
    for at, row in rows:
        kept[at : at + 1, :] = jnp.broadcast_to(row, (1, N))
    msg[...] = jnp.broadcast_to(smoothed, (N, N))


def run_owner(begin, got, before, inverse):
    def kernel(*refs):
        owner_kernel(begin, *refs)

    return pl.pallas_call(
        kernel,
        out_shape=(f32(KEPT, N), f32(N, N)),
        in_specs=[vspec()] * 3,
        out_specs=(vspec(),) * 2,
        compiler_params=params(),
        name="owner",
    )(got, before, inverse)


def sum_pairs(got):
    total = jnp.sum(got[...].reshape(N // 4, 8, N), axis=0)
    even = (total[0:1] + total[2:3]) + (total[4:5] + total[6:7])
    odd = (total[1:2] + total[3:4]) + (total[5:6] + total[7:8])
    return even, odd


def tile_kernel(turn, hot_rows, hot, tiles, got, kept, *refs):
    spread = refs[-1]
    msg, applied_out = refs[-2], refs[-3]
    transpose_apply(hot_rows[...], tiles, got, applied_out)
    applied = applied_out[...]
    smoothed = kept[SMOOTHED : SMOOTHED + 1, :]
    curve = jnp.sum(applied * applied, axis=0, keepdims=True) + REGULAR * smoothed * smoothed
    if turn == 0:
        cross = jnp.zeros((1, 1), jnp.float32)
    else:
        before = refs[0][...]
        if turn == 2:
            before = before + kept[BETA : BETA + 1, :] * refs[1][...]
        cross = jnp.sum(applied * before, axis=0, keepdims=True)
        cross = total_of(cross + REGULAR * smoothed * kept[DIRECTION : DIRECTION + 1, :])
    lane = iota((1, N), 1)
    line = jnp.where(lane == 0, total_of(curve), jnp.where(lane == 1, cross, 0.0))
    line = jnp.where(lane == 2, kept[PART : PART + 1, :], line)
    if turn == 2:
        msg[...] = jnp.broadcast_to(line, (N, N))
    else:
        msg[pl.ds(1, N, stride=2), :] = jnp.broadcast_to(line, (N, N))
        forward_apply(tiles, (applied,), (spread,))
        msg[pl.ds(0, N, stride=2), :] = place_rows(hot[...], spread[...])


def run_tile(turn, hot_rows, hot, tiles, got, kept, *before):
    def kernel(*refs):
        tile_kernel(turn, *refs)

    return pl.pallas_call(
        kernel,
        out_shape=(f32(GROUPS, N), f32(N if turn == 2 else 2 * N, N)),
        in_specs=[vspec()] * (5 + len(before)),
        out_specs=(vspec(),) * 2,
        scratch_shapes=[pltpu.VMEM((TILES, N), jnp.float32)],
        compiler_params=params(),
        name="tile_last" if turn == 2 else "tile",
    )(hot_rows, hot, tiles, got, kept, *before)


def final_kernel(
    got, kept1, kept2, z0, z1, z2, a0, a1, a2, mu, root, base, ratio, step_dual, step_primal
):
    line = jnp.sum(got[...], axis=0, keepdims=True)
    norm, beta2, curve = combine(line, kept2, False)
    len2 = norm / curve
    len0, len1 = kept1[STEP : STEP + 1, :], kept2[STEP : STEP + 1, :]
    beta1 = kept2[BETA : BETA + 1, :]
    at = pl.multiple_of(lax.axis_index("leg") * 16, 16)

    def step(v0, v1, v2):
        second = v1 + beta1 * v0
        return len0 * v0 + len1 * second + len2 * (v2 + beta2 * second)

    for core in range(2):
        mine = pl.ds(HALF * core + at, 16)
        part = step(z0[mine, :], z1[mine, :], z2[mine, :])
        for x in range(4):
            row = 8 * x + 4 * core
            step_dual[row : row + 4, :] = part[4 * x : 4 * x + 4]
    applied = step(a0[...], a1[...], a2[...])
    step_primal[...] = root[...] * applied + (mu[0:1, :] * ratio[...] + base[...])


def run_final(*args):
    return pl.pallas_call(
        final_kernel,
        out_shape=(f32(32, N), f32(GROUPS, N)),
        in_specs=[vspec()] * len(args),
        out_specs=(vspec(), vspec()),
        compiler_params=params(),
        name="final",
    )(*args)


ALL = ("core", "leg", "x", "z")
CHIPS = ("x", "z", "leg")


def exchange(rows, axes):
    return lax.all_to_all(rows, axes, split_axis=0, concat_axis=0, tiled=True)


def per_device(coeffs, block_ids, col_counts, primal, slack, cost, duals, demand):
    ids = block_ids.T
    parts = [duals]
    for k in (1, 2, 3):
        parts.append(lax.ppermute(duals, "leg", [(i, (i + k) % 4) for i in range(4)]))

    tiles, acc, other, small, root, hot_rows, hot, hot_place = run_gram(
        coeffs, ids, col_counts, primal, slack
    )
    swap = [(0, 1), (1, 0)]
    other, *parts = lax.optimization_barrier((other, *parts))
    got_big = lax.ppermute(other, "core", swap)
    small, small_other, base, ratio = run_rhs(
        hot_rows, hot_place, tiles, parts, primal, slack, cost, root, small
    )
    got_small = lax.ppermute(small_other, "core", swap)
    joined = run_join(acc, got_big, small, got_small)
    blocks = exchange(joined.reshape(HALF * ROWS // 4, 4, N), CHIPS).reshape(HALF * ROWS, N)
    inverse, kept0, mu, msg = run_first(blocks, demand)

    z0 = exchange(msg, ALL)
    a0, msg = run_tile(0, hot_rows, hot, tiles, z0, kept0)
    kept1, msg = run_owner(True, exchange(msg, ALL), kept0, inverse)
    z1 = exchange(msg, ALL)
    a1, msg = run_tile(1, hot_rows, hot, tiles, z1, kept1, a0)
    kept2, msg = run_owner(False, exchange(msg, ALL), kept1, inverse)
    z2 = exchange(msg, ALL)
    a2, msg = run_tile(2, hot_rows, hot, tiles, z2, kept2, a1, a0)
    got = exchange(msg, ALL)
    return run_final(got, kept1, kept2, z0, z1, z2, a0, a1, a2, mu, root, base, ratio)


def solution(mesh):
    fine = Mesh(mesh.devices.reshape(4, 4, 2, 4), ("x", "z", "core", "leg"))
    every = ("x", "z", "core", "leg")
    return jax.shard_map(
        per_device,
        mesh=fine,
        in_specs=(
            P(every, None, None, None),
            P(every, None),
            P(every),
            P(every, None),
            P(every, None),
            P(every, None),
            P("leg", None),
            P("leg", None),
        ),
        out_specs=(P("leg", None), P(every, None)),
        check_vma=False,
    )
```

```python
import jax
import jax.numpy as jnp
from jax import lax
from jax.experimental import pallas as pl
from jax.experimental.pallas import tpu as pltpu
from jax.sharding import Mesh, PartitionSpec as P

SIGMA = 0.3
REGULAR = 1.0
PRECISE = lax.Precision.HIGHEST

N = 128
HALF = 64
SPAN = 4
GROUPS = 16
TILES = GROUPS * SPAN
EXTRA = 4
ROWS = HALF + EXTRA

VMEM = pltpu.MemorySpace.VMEM
SMEM = pltpu.MemorySpace.SMEM
HBM = pltpu.MemorySpace.HBM
NT = (((1,), (1,)), ((), ()))


def iota(shape, axis):
    return lax.broadcasted_iota(jnp.int32, shape, axis)


def vspec():
    return pl.BlockSpec(memory_space=VMEM)


def sspec():
    return pl.BlockSpec(memory_space=SMEM)


def f32(*shape):
    return jax.ShapeDtypeStruct(shape, jnp.float32)


def device_col():
    return (lax.axis_index("x") * 2 + lax.axis_index("core")) * 4 + lax.axis_index("z")


def params():
    return pltpu.CompilerParams(vmem_limit_bytes=24 << 20)


def split(x):
    high = x.astype(jnp.bfloat16)
    return high, (x - high.astype(jnp.float32)).astype(jnp.bfloat16)


def gram_product(high, low):
    both = jnp.concatenate([high, low], axis=0)
    full = lax.dot_general(both, both, NT, preferred_element_type=jnp.float32)
    return (full[:N, :N] + full[N:, N:]) + (full[:N, N:] + full[N:, :N])


CHUNKS = (0, 5)


def gram_kernel(
    coeffs_in, ids_in, counts_in, primal_in, slack_in, tiles, acc, other, small, root_out,
    hot_rows, hot_ids, hot_place, coeffs, ids, counts, primal, slack, hot, hot2, sem, tile_sem,
):
    little = [
        pltpu.make_async_copy(ids_in, ids, sem.at[0]),
        pltpu.make_async_copy(counts_in, counts, sem.at[1]),
        pltpu.make_async_copy(primal_in, primal, sem.at[2]),
        pltpu.make_async_copy(slack_in, slack, sem.at[3]),
    ]
    big = {}
    for k, g in enumerate(CHUNKS):
        part = pl.ds(g, (CHUNKS + (GROUPS,))[k + 1] - g)
        big[g] = pltpu.make_async_copy(coeffs_in.at[part], coeffs.at[part], tile_sem.at[k])
    for copy in little + list(big.values()):
        copy.start()
    acc[...] = jnp.zeros_like(acc)
    small[...] = jnp.zeros_like(small)
    hot[...] = jnp.zeros_like(hot)
    hot2[...] = jnp.zeros_like(hot2)
    core = lax.axis_index("core")
    for copy in little:
        copy.wait()
    row = iota((HALF, N), 0)
    lane = iota((HALF, N), 1)
    line_lane = iota((1, N), 1)
    lower = jnp.logical_or(row >= lane, lane >= HALF)
    for g in range(GROUPS):
        scale = jnp.where(line_lane < counts[g], primal[g : g + 1, :] / slack[g : g + 1, :], 0.0)
        root_out[g : g + 1, :] = jnp.sqrt(scale)
    for g in range(GROUPS):
        if g in big:
            big[g].wait()
        root = root_out[g : g + 1, :]
        for s in range(SPAN):
            high, low = split(coeffs[g, s] * root)
            tiles[g, s * N : (s + 1) * N, :] = jnp.concatenate([high, low], axis=1)
            gram = gram_product(high, low)
            rolled = pltpu.roll(gram[HALF:], HALF, 1)
            packed = jnp.where(lower, gram[:HALF], rolled)
            line = jnp.sum(jnp.where(row == lane, rolled, 0.0), axis=0, keepdims=True)
            block = ids[s, g]
            owner = (block & 4) << 4 | (block >> 5) << 4 | ((block >> 3) & 3) << 2 | block & 3
            chip = (((block >> 3) & 3) << 4) | ((block & 3) << 2) | (block >> 5)
            place = (((block >> 2) & 1) ^ core) * HALF + chip
            acc[place] += packed
            small[pl.ds(place * EXTRA, 1), :] += line
            t = g * SPAN + s
            hot[t : t + 1, :] = (line_lane == owner).astype(jnp.float32)
            hot2[t : t + 1, :] = (line_lane == place).astype(jnp.float32)
    other[...] = acc[pl.ds(HALF, HALF)]
    hot_rows[...] = hot[:TILES, :].astype(jnp.bfloat16)
    hot_ids[...] = jnp.transpose(hot[...]).astype(jnp.bfloat16)
    hot_place[...] = jnp.transpose(hot2[...]).astype(jnp.bfloat16)


def run_gram(coeffs, ids, counts, primal, slack):
    return pl.pallas_call(
        gram_kernel,
        out_shape=(
            jax.ShapeDtypeStruct((GROUPS, SPAN * N, 2 * N), jnp.bfloat16),
            f32(N, HALF, N),
            f32(HALF, HALF, N),
            f32(N * EXTRA, N),
            f32(GROUPS, N),
            jax.ShapeDtypeStruct((TILES, N), jnp.bfloat16),
            jax.ShapeDtypeStruct((N, N), jnp.bfloat16),
            jax.ShapeDtypeStruct((N, N), jnp.bfloat16),
        ),
        in_specs=[pl.BlockSpec(memory_space=HBM)] * 5,
        out_specs=(vspec(),) * 8,
        scratch_shapes=[
            pltpu.VMEM((GROUPS, SPAN, N, N), jnp.float32),
            pltpu.SMEM((SPAN, GROUPS), jnp.int32),
            pltpu.SMEM((GROUPS,), jnp.int32),
            pltpu.VMEM((GROUPS, N), jnp.float32),
            pltpu.VMEM((GROUPS, N), jnp.float32),
            pltpu.VMEM((N, N), jnp.float32),
            pltpu.VMEM((N, N), jnp.float32),
            pltpu.SemaphoreType.DMA((4,)),
            pltpu.SemaphoreType.DMA((GROUPS,)),
        ],
        compiler_params=params(),
        cost_estimate=pl.CostEstimate(
            flops=TILES * 2 * N**3 * 4, bytes_accessed=12 << 20, transcendentals=0
        ),
        name="gram",
    )(*(pltpu.with_memory_space_constraint(x, HBM) for x in (coeffs, ids, counts, primal, slack)))


def transpose_apply(hot, tiles, vector, out):
    high, low = split(vector[...])
    high = jnp.dot(hot, high, preferred_element_type=jnp.float32)
    low = jnp.dot(hot, low, preferred_element_type=jnp.float32)
    whole = high + low
    high, low = high.astype(jnp.bfloat16), low.astype(jnp.bfloat16)
    turned = jnp.transpose(whole)
    for g in range(GROUPS):
        if g % 5 == 4:
            total = None
            for s in range(SPAN):
                t = g * SPAN + s
                pair = tiles[g, s * N : (s + 1) * N, :].astype(jnp.float32)
                tile = pair[:, :N] + pair[:, N:]
                part = tile * jnp.broadcast_to(turned[:, t : t + 1], (N, N))
                part = jnp.sum(part.reshape(N // 8, 8, N), axis=0)
                total = part if total is None else total + part
            out[g : g + 1, :] = jnp.sum(total, axis=0, keepdims=True)
            continue
        parts = []
        for rows in (high, low):
            own = [rows[g * SPAN + s : g * SPAN + s + 1] for s in range(SPAN)]
            parts.append(jnp.concatenate(own, axis=1))
        both = jnp.concatenate(parts, axis=0)
        full = jnp.dot(both, tiles[g], preferred_element_type=jnp.float32)
        out[g : g + 1, :] = (full[0:1, :N] + full[1:2, N:]) + (full[0:1, N:] + full[1:2, :N])


def forward_apply(tiles, colvecs, outs):
    lines = []
    for w in colvecs:
        high, low = split(w)
        lines.append(jnp.concatenate([high, high], axis=1))
        lines.append(jnp.concatenate([low, jnp.zeros_like(low)], axis=1))
    every = len(colvecs) + 1
    for g in range(GROUPS):
        if g % every == every - 1:
            for s in range(SPAN):
                t = g * SPAN + s
                pair = tiles[g, s * N : (s + 1) * N, :].astype(jnp.float32)
                tile = pair[:, :N] + pair[:, N:]
                for w, out in zip(colvecs, outs):
                    turned = jnp.transpose(tile * w[g : g + 1])
                    out[t : t + 1, :] = jnp.sum(turned, axis=0, keepdims=True)
            continue
        both = jnp.concatenate([line[g : g + 1] for line in lines], axis=0)
        full = lax.dot_general(both, tiles[g], NT, preferred_element_type=jnp.float32)
        for k, out in enumerate(outs):
            total = full[2 * k : 2 * k + 1] + full[2 * k + 1 : 2 * k + 2]
            for s in range(SPAN):
                t = g * SPAN + s
                out[t : t + 1, :] = total[:, s * N : (s + 1) * N]


def place_rows(hot, rows):
    rows = jnp.concatenate([rows, jnp.zeros((N - TILES, N), jnp.float32)], axis=0)
    high = rows.astype(jnp.bfloat16)
    middle, low = split(rows - high.astype(jnp.float32))
    total = jnp.dot(hot, high, preferred_element_type=jnp.float32)
    total = total + jnp.dot(hot, middle, preferred_element_type=jnp.float32)
    return total + jnp.dot(hot, low, preferred_element_type=jnp.float32)


def rhs_kernel(
    hot_rows, hot_place, tiles, dual0, dual1, dual2, dual3, primal, slack, cost, root, small,
    own_out, other_out, base_out, scale_out, spread, spread2, duals, applied,
):
    leg = lax.axis_index("leg")
    for k, part in ((0, dual0), (2, dual1), (1, dual2), (3, dual3)):
        at = pl.multiple_of(((leg - k) & 3) * 32, 32)
        at = pl.multiple_of(at // 2, 16)
        for core in range(2):
            rows = [part[8 * x + 4 * core : 8 * x + 4 * core + 4, :] for x in range(4)]
            duals[pl.ds(HALF * core + at, 16), :] = jnp.concatenate(rows, axis=0)
    used = root[...] > 0.0
    valid = used.astype(jnp.float32)
    transpose_apply(hot_rows[...], tiles, duals, applied)
    dual_res = cost[...] - applied[...] / jnp.where(used, root[...], 1.0) - slack[...]
    weighted = root[...] * dual_res
    ratio = valid / slack[...]
    base_out[...] = -(root[...] * weighted) - valid * primal[...]
    scale_out[...] = ratio
    product = primal[...] * slack[...]
    forward_apply(tiles, (weighted, valid / jnp.sqrt(product)), (spread, spread2))
    first = place_rows(hot_place[...], spread[...])
    second = place_rows(hot_place[...], spread2[...])
    comp = jnp.sum(valid * product, axis=0, keepdims=True)
    count = jnp.sum(jnp.sum(valid, axis=0, keepdims=True), axis=1, keepdims=True)
    for k, out in enumerate((own_out, other_out)):
        half = slice(k * HALF, k * HALF + HALF)
        diag = small[pl.ds(k * HALF * EXTRA, HALF, stride=EXTRA), :]
        diag = jnp.where(iota((HALF, N), 1) < HALF, diag, jnp.broadcast_to(count, (HALF, N)))
        out[pl.ds(0, HALF, stride=EXTRA), :] = diag
        out[pl.ds(1, HALF, stride=EXTRA), :] = first[half]
        out[pl.ds(2, HALF, stride=EXTRA), :] = second[half]
        out[pl.ds(3, HALF, stride=EXTRA), :] = jnp.broadcast_to(comp, (HALF, N))


def run_rhs(hot_rows, hot_place, tiles, duals, primal, slack, cost, root, small):
    return pl.pallas_call(
        rhs_kernel,
        out_shape=(f32(HALF * EXTRA, N), f32(HALF * EXTRA, N), f32(GROUPS, N), f32(GROUPS, N)),
        in_specs=[vspec()] * 12,
        out_specs=(vspec(),) * 4,
        scratch_shapes=[
            pltpu.VMEM((TILES, N), jnp.float32),
            pltpu.VMEM((TILES, N), jnp.float32),
            pltpu.VMEM((N, N), jnp.float32),
            pltpu.VMEM((GROUPS, N), jnp.float32),
        ],
        compiler_params=params(),
        cost_estimate=pl.CostEstimate(flops=1 << 27, bytes_accessed=6 << 20, transcendentals=0),
        name="rhs",
    )(hot_rows, hot_place, tiles, *duals, primal, slack, cost, root, small)


def join_kernel(acc, got, small, small_got, out):
    for p in range(HALF // 2):
        at = 2 * ROWS * p
        out[at : at + HALF, :] = acc[2 * p] + got[2 * p]
        extra = slice(2 * EXTRA * p, 2 * EXTRA * (p + 1))
        out[at + HALF : at + HALF + 2 * EXTRA, :] = small[extra, :] + small_got[extra, :]
        out[at + HALF + 2 * EXTRA : at + 2 * ROWS, :] = acc[2 * p + 1] + got[2 * p + 1]


def run_join(acc, got, small, small_got):
    return pl.pallas_call(
        join_kernel,
        out_shape=f32(HALF * ROWS, N),
        in_specs=[vspec()] * 4,
        out_specs=vspec(),
        compiler_params=params(),
        name="join",
    )(acc, got, small, small_got)


def small_inverse(cols):
    cols = list(cols)
    sub = iota((8, N), 0)
    for m in range(8):
        rows = [jnp.broadcast_to(c[m : m + 1, :], (8, N)) for c in cols]
        inv = 1.0 / rows[m]
        factor = cols[m]
        here = sub == m
        for j in range(8):
            if j == m:
                cols[j] = jnp.where(here, inv, -factor * inv)
            else:
                scaled = rows[j] * inv
                cols[j] = jnp.where(here, scaled, cols[j] - factor * scaled)
    return cols


def invert(panels):
    panels = list(panels)
    lane = iota((8, N), 1)
    count = len(panels)
    for k in range(count):
        mine = jnp.logical_and(lane >= 8 * k, lane < 8 * k + 8)
        pivot = panels[k]
        cols = [jnp.broadcast_to(pivot[:, 8 * k + m : 8 * k + m + 1], (8, N)) for m in range(8)]
        cols = small_inverse(cols)
        total = None
        for m in range(8):
            term = cols[m] * jnp.broadcast_to(pivot[m : m + 1, :], (8, N))
            total = term if total is None else total + term
        for m in range(8):
            total = jnp.where(lane == 8 * k + m, cols[m], total)
        rows = [jnp.broadcast_to(total[m : m + 1, :], (8, N)) for m in range(8)]
        for step in range(1, count):
            i = (k + step) % count
            old = panels[i]
            terms = []
            for m in range(8):
                col = jnp.broadcast_to(old[:, 8 * k + m : 8 * k + m + 1], (8, N))
                terms.append(col * rows[m])
            while len(terms) > 1:
                terms = [terms[j] + terms[j + 1] for j in range(0, len(terms), 2)]
            panels[i] = jnp.where(mine, 0.0, old) - terms[0]
        panels[k] = total
    return panels


RESIDUAL, SMOOTHED, DIRECTION, IMAGE, PART, NORM, CURVE, STEP, BETA = range(9)
KEPT = 16


def total_of(line):
    return jnp.sum(line, axis=1, keepdims=True)


def smooth(residual, inverse):
    return jnp.dot(
        jnp.broadcast_to(residual, (8, N)),
        inverse,
        precision=PRECISE,
        preferred_element_type=jnp.float32,
    )[0:1]


def first_kernel(got, demand, inverse_out, kept, mu_out, msg):
    def add(i, carry):
        return carry + got[pl.ds(pl.multiple_of(i * 2 * ROWS, 8), 2 * ROWS), :]

    total = lax.fori_loop(1, HALF // 2, add, got[0 : 2 * ROWS, :], unroll=True)
    total = total[:ROWS] + total[ROWS:]
    odd = (lax.axis_index("leg") & 1) == 1
    packed = jnp.where(odd, total[EXTRA:], total[:HALF])
    tail = jnp.where(odd, total[:EXTRA], total[HALF:])
    line = tail[0:1]
    comp = jnp.sum(tail[3:4], axis=1, keepdims=True)
    used = line[:, HALF : HALF + 1]
    mu = SIGMA * (comp / used)
    mu_out[...] = jnp.broadcast_to(mu, (8, N))
    residual = demand[pl.ds(device_col(), 1), :] + tail[1:2] - mu * tail[2:3]

    row = iota((HALF, N), 0)
    lane = iota((HALF, N), 1)
    flipped = jnp.transpose(jnp.concatenate([packed, jnp.zeros((HALF, N), jnp.float32)], axis=0))
    flip_top, flip_bottom = flipped[:HALF], flipped[HALF:]
    top = jnp.where(jnp.logical_or(row >= lane, lane >= HALF), packed, flip_top)
    corner = jnp.where(row < lane, packed, flip_top)
    corner = jnp.where(row == lane, jnp.broadcast_to(line, (HALF, N)), corner)
    bottom = jnp.where(lane < HALF, flip_bottom, pltpu.roll(corner, HALF, 1))
    top = top + jnp.where(row == lane, REGULAR, 0.0)
    bottom = bottom + jnp.where(row + HALF == lane, REGULAR, 0.0)
    panels = [top[8 * i : 8 * i + 8] for i in range(8)]
    panels += [bottom[8 * i : 8 * i + 8] for i in range(8)]
    inverse = jnp.concatenate(invert(panels), axis=0)
    inverse_out[...] = inverse
    smoothed = smooth(residual, inverse)
    part = total_of(residual * smoothed)
    zero = jnp.zeros((1, N), jnp.float32)
    kept[RESIDUAL : RESIDUAL + 1, :] = residual
    kept[SMOOTHED : SMOOTHED + 1, :] = smoothed
    kept[PART : PART + 1, :] = jnp.broadcast_to(part, (1, N))
    for at in (DIRECTION, IMAGE):
        kept[at : at + 1, :] = zero
    msg[...] = jnp.broadcast_to(smoothed, (N, N))


def run_first(got, demand):
    return pl.pallas_call(
        first_kernel,
        out_shape=(f32(N, N), f32(KEPT, N), f32(8, N), f32(N, N)),
        in_specs=[vspec(), vspec()],
        out_specs=(vspec(),) * 4,
        compiler_params=params(),
        name="first",
    )(got, demand)


def sum_pairs(got):
    total = jnp.sum(got[...].reshape(N // 4, 8, N), axis=0)
    even = (total[0:1] + total[2:3]) + (total[4:5] + total[6:7])
    odd = (total[1:2] + total[3:4]) + (total[5:6] + total[7:8])
    return even, odd


def combine(line, before, begin):
    curve, cross, norm = (jnp.broadcast_to(line[:, k : k + 1], (1, N)) for k in range(3))
    if begin:
        return norm, jnp.zeros_like(norm), curve
    beta = norm / before[NORM : NORM + 1, :]
    old = before[CURVE : CURVE + 1, :]
    return norm, beta, curve + beta * (2.0 * cross + beta * old)


def owner_kernel(begin, got, before, inverse, kept, msg):
    image, line = sum_pairs(got)
    smoothed = before[SMOOTHED : SMOOTHED + 1, :]
    image = image + REGULAR * smoothed
    norm, beta, curve = combine(line, before, begin)
    direction = smoothed
    if not begin:
        image = image + beta * before[IMAGE : IMAGE + 1, :]
        direction = smoothed + beta * before[DIRECTION : DIRECTION + 1, :]
    step_len = norm / curve
    residual = before[RESIDUAL : RESIDUAL + 1, :] - step_len * image
    smoothed = smooth(residual, inverse[...])
    rows = (
        (RESIDUAL, residual),
        (SMOOTHED, smoothed),
        (DIRECTION, direction),
        (IMAGE, image),
        (PART, total_of(residual * smoothed)),
        (NORM, norm),
        (CURVE, curve),
        (STEP, step_len),
        (BETA, beta),
    )
    for at, row in rows:
        kept[at : at + 1, :] = jnp.broadcast_to(row, (1, N))
    msg[...] = jnp.broadcast_to(smoothed, (N, N))


def run_owner(begin, got, before, inverse):
    def kernel(*refs):
        owner_kernel(begin, *refs)

    return pl.pallas_call(
        kernel,
        out_shape=(f32(KEPT, N), f32(N, N)),
        in_specs=[vspec()] * 3,
        out_specs=(vspec(),) * 2,
        compiler_params=params(),
        name="owner",
    )(got, before, inverse)


def sum_pairs(got):
    total = jnp.sum(got[...].reshape(N // 4, 8, N), axis=0)
    even = (total[0:1] + total[2:3]) + (total[4:5] + total[6:7])
    odd = (total[1:2] + total[3:4]) + (total[5:6] + total[7:8])
    return even, odd


def tile_kernel(turn, hot_rows, hot, tiles, got, kept, *refs):
    spread = refs[-1]
    msg, applied_out = refs[-2], refs[-3]
    transpose_apply(hot_rows[...], tiles, got, applied_out)
    applied = applied_out[...]
    smoothed = kept[SMOOTHED : SMOOTHED + 1, :]
    curve = jnp.sum(applied * applied, axis=0, keepdims=True) + REGULAR * smoothed * smoothed
    if turn == 0:
        cross = jnp.zeros((1, 1), jnp.float32)
    else:
        before = refs[0][...]
        if turn == 2:
            before = before + kept[BETA : BETA + 1, :] * refs[1][...]
        cross = jnp.sum(applied * before, axis=0, keepdims=True)
        cross = total_of(cross + REGULAR * smoothed * kept[DIRECTION : DIRECTION + 1, :])
    lane = iota((1, N), 1)
    line = jnp.where(lane == 0, total_of(curve), jnp.where(lane == 1, cross, 0.0))
    line = jnp.where(lane == 2, kept[PART : PART + 1, :], line)
    if turn == 2:
        msg[...] = jnp.broadcast_to(line, (N, N))
    else:
        msg[pl.ds(1, N, stride=2), :] = jnp.broadcast_to(line, (N, N))
        forward_apply(tiles, (applied,), (spread,))
        msg[pl.ds(0, N, stride=2), :] = place_rows(hot[...], spread[...])


def run_tile(turn, hot_rows, hot, tiles, got, kept, *before):
    def kernel(*refs):
        tile_kernel(turn, *refs)

    return pl.pallas_call(
        kernel,
        out_shape=(f32(GROUPS, N), f32(N if turn == 2 else 2 * N, N)),
        in_specs=[vspec()] * (5 + len(before)),
        out_specs=(vspec(),) * 2,
        scratch_shapes=[pltpu.VMEM((TILES, N), jnp.float32)],
        compiler_params=params(),
        name="tile_last" if turn == 2 else "tile",
    )(hot_rows, hot, tiles, got, kept, *before)


def final_kernel(
    got, kept1, kept2, z0, z1, z2, a0, a1, a2, mu, root, base, ratio, step_dual, step_primal
):
    line = jnp.sum(got[...], axis=0, keepdims=True)
    norm, beta2, curve = combine(line, kept2, False)
    len2 = norm / curve
    len0, len1 = kept1[STEP : STEP + 1, :], kept2[STEP : STEP + 1, :]
    beta1 = kept2[BETA : BETA + 1, :]
    at = pl.multiple_of(lax.axis_index("leg") * 16, 16)

    def step(v0, v1, v2):
        second = v1 + beta1 * v0
        return len0 * v0 + len1 * second + len2 * (v2 + beta2 * second)

    for core in range(2):
        mine = pl.ds(HALF * core + at, 16)
        part = step(z0[mine, :], z1[mine, :], z2[mine, :])
        for x in range(4):
            row = 8 * x + 4 * core
            step_dual[row : row + 4, :] = part[4 * x : 4 * x + 4]
    applied = step(a0[...], a1[...], a2[...])
    step_primal[...] = root[...] * applied + (mu[0:1, :] * ratio[...] + base[...])


def run_final(*args):
    return pl.pallas_call(
        final_kernel,
        out_shape=(f32(32, N), f32(GROUPS, N)),
        in_specs=[vspec()] * len(args),
        out_specs=(vspec(), vspec()),
        compiler_params=params(),
        name="final",
    )(*args)


ALL = ("core", "leg", "x", "z")
CHIPS = ("x", "z", "leg")


def exchange(rows, axes):
    return lax.all_to_all(rows, axes, split_axis=0, concat_axis=0, tiled=True)


def per_device(coeffs, block_ids, col_counts, primal, slack, cost, duals, demand):
    ids = block_ids.T
    parts = [duals]
    for k in (2, 1, 3):
        parts.append(lax.ppermute(duals, "leg", [(i, (i + k) % 4) for i in range(4)]))

    tiles, acc, other, small, root, hot_rows, hot, hot_place = run_gram(
        coeffs, ids, col_counts, primal, slack
    )
    swap = [(0, 1), (1, 0)]
    other, *parts = lax.optimization_barrier((other, *parts))
    got_big = lax.ppermute(other, "core", swap)
    small, small_other, base, ratio = run_rhs(
        hot_rows, hot_place, tiles, parts, primal, slack, cost, root, small
    )
    got_small = lax.ppermute(small_other, "core", swap)
    joined = run_join(acc, got_big, small, got_small)
    blocks = exchange(joined.reshape(HALF * ROWS // 4, 4, N), CHIPS).reshape(HALF * ROWS, N)
    inverse, kept0, mu, msg = run_first(blocks, demand)

    z0 = exchange(msg, ALL)
    a0, msg = run_tile(0, hot_rows, hot, tiles, z0, kept0)
    kept1, msg = run_owner(True, exchange(msg, ALL), kept0, inverse)
    z1 = exchange(msg, ALL)
    a1, msg = run_tile(1, hot_rows, hot, tiles, z1, kept1, a0)
    kept2, msg = run_owner(False, exchange(msg, ALL), kept1, inverse)
    z2 = exchange(msg, ALL)
    a2, msg = run_tile(2, hot_rows, hot, tiles, z2, kept2, a1, a0)
    got = exchange(msg, ALL)
    return run_final(got, kept1, kept2, z0, z1, z2, a0, a1, a2, mu, root, base, ratio)


def solution(mesh):
    fine = Mesh(mesh.devices.reshape(4, 4, 2, 4), ("x", "z", "core", "leg"))
    every = ("x", "z", "core", "leg")
    return jax.shard_map(
        per_device,
        mesh=fine,
        in_specs=(
            P(every, None, None, None),
            P(every, None),
            P(every),
            P(every, None),
            P(every, None),
            P(every, None),
            P("leg", None),
            P("leg", None),
        ),
        out_specs=(P("leg", None), P(every, None)),
        check_vma=False,
    )
```
